32 devices in a mesh: section: 2 (over core), dp: 4 (over z), heads: 4 (over y, x).
Axes of the slice: x: 2, y: 2, z: 4, core: 2. Of those that a mesh axis runs over, the one named last changes fastest.
Arguments:
- query_embed: bfloat16 [256, 16, 768], P('heads', 'dp'), may hold values from -6 to 6
- key_embed: bfloat16 [256, 16, 768], P('heads', 'dp'), may hold values from -6 to 6
- crop_counts: int32 [16, 2], P('dp'), may hold values from 1 to 256, as said below
- pair_mask: int32 [16], P('dp'), may hold values from 0 to 1, as said below
- negative_queue: bfloat16 [4096, 768], P('dp'), may hold values from -6 to 6
- online_inproj: bfloat16 [2, 768, 3, 768], P('section', None, None, 'heads'), may hold values from -0.21875 to 0.21875
- online_inbias: bfloat16 [2, 2, 12, 64], P('section', None, 'heads'), may hold values from -3 to 3
- online_outproj: bfloat16 [2, 768, 768], P('section', 'heads'), may hold values from -0.625 to 0.625
- online_gains: bfloat16 [2, 2, 768], P('section'), may hold values from 0.5 to 1.5
- online_shifts: bfloat16 [2, 4, 768], P('section'), may hold values from -1.1953125 to 1.1953125
- online_expand: bfloat16 [2, 768, 3072], P('section', None, 'heads'), may hold values from -0.21875 to 0.21875
- online_expbias: bfloat16 [2, 12, 256], P('section', 'heads'), may hold values from -3 to 3
- online_contract: bfloat16 [2, 3072, 768], P('section', 'heads'), may hold values from -0.109375 to 0.109375
- momentum_inproj: bfloat16 [2, 768, 3, 768], P('section', None, None, 'heads'), may hold values from -0.21875 to 0.21875
- momentum_inbias: bfloat16 [2, 2, 12, 64], P('section', None, 'heads'), may hold values from -3 to 3
- momentum_outproj: bfloat16 [2, 768, 768], P('section', 'heads'), may hold values from -0.625 to 0.625
- momentum_gains: bfloat16 [2, 2, 768], P('section'), may hold values from 0.5 to 1.5
- momentum_shifts: bfloat16 [2, 4, 768], P('section'), may hold values from -1.1953125 to 1.1953125
- momentum_expand: bfloat16 [2, 768, 3072], P('section', None, 'heads'), may hold values from -0.21875 to 0.21875
- momentum_expbias: bfloat16 [2, 12, 256], P('section', 'heads'), may hold values from -3 to 3
- momentum_contract: bfloat16 [2, 3072, 768], P('section', 'heads'), may hold values from -0.109375 to 0.109375
Outputs:
- loss_value: float32 [], replicated
- input_grad: bfloat16 [256, 16, 768], P('heads', 'dp', 'section')
- grad_inproj: float32 [2, 768, 3, 768], P('section', 'dp', None, 'heads')
- grad_inbias: float32 [2, 2, 12, 64], P('section', None, 'heads', 'dp')
- grad_outproj: float32 [2, 768, 768], P('section', 'heads', 'dp')
- grad_gains: float32 [2, 2, 768], P('section', None, ('dp', 'heads'))
- grad_shifts: float32 [2, 4, 768], P('section', None, ('dp', 'heads'))
- grad_expand: float32 [2, 768, 3072], P('section', 'dp', 'heads')
- grad_expbias: float32 [2, 12, 256], P('section', 'heads', 'dp')
- grad_contract: float32 [2, 3072, 768], P('section', 'heads', 'dp')
- rms_values: float32 [2, 3], replicated
The draws below stay inside these ranges and needn't reach their ends.
Inputs may be any that keep to these rules, and one draw needn't show every extreme that they name: `crop_counts`: every crop has at least one valid token; some pair has both crops full. `pair_mask`: at least one pair is live.
All inputs are finite; a program needn't handle non-finite values.
Results may differ from the reference program's by a relative error of at most 0.028.
Values may be sent and summed in bfloat16 or wider, within the bound.
No kernel may reach another device: no remote copies, remote signals or barrier semaphores. Data moves between devices by JAX's collectives and lax.ppermute only.
A program may use at most 128 MiB of HBM per device.

```python
import math
import jax
import jax.numpy as jnp
from jax import lax

D = 768
HEADS = 12
HEAD = 64
FF = 3072
LEN = 256
QUEUE = 4096
PAIRS_DEV = 4
PAIRS = 16
LAYERS = 2


def crop_plan(key):
    streams = jax.random.split(jax.random.fold_in(key, 11), 5)
    scale_bits = jax.random.randint(streams[0], (PAIRS, 2), 2, 9)
    limits = jnp.left_shift(jnp.ones((PAIRS, 2), jnp.int32), scale_bits)
    counts = 1 + jax.random.randint(streams[1], (PAIRS, 2), 0, limits)
    counts = jnp.minimum(counts, LEN)
    full_pair = jax.random.randint(streams[2], (), 0, PAIRS)
    pair_rows = jnp.arange(PAIRS)
    counts = jnp.where((pair_rows == full_pair)[:, None], LEN, counts)
    levels = jax.random.randint(streams[3], (PAIRS // PAIRS_DEV, 1), 1, 5)
    levels = jnp.broadcast_to(levels, (PAIRS // PAIRS_DEV, PAIRS_DEV)).reshape(PAIRS)
    live = (jax.random.randint(streams[4], (PAIRS,), 0, 4) < levels).astype(jnp.int32)
    live = jnp.where(pair_rows == full_pair, 1, live)
    return (counts.astype(jnp.int32), live.astype(jnp.int32))


def draw_crop_counts(key, part):
    return crop_plan(key)[0]


def draw_pair_mask(key, part):
    return crop_plan(key)[1]


def steps_of(rng, dims, cuts, low, high):
    def one(dim, blocks):
        heights = jax.random.uniform(jax.random.fold_in(jax.random.fold_in(rng, 6), dim), (blocks,), jnp.float32, low / len(cuts), high / len(cuts))
        return jnp.repeat(jnp.exp(heights), dims[dim] // blocks).reshape((-1,) + (1,) * (len(dims) - dim - 1))

    factor_of = one(*cuts[0])
    for cut in cuts[1:]:
        factor_of = factor_of * one(*cut)
    return factor_of


def noise(rng, dims, deviation, reach, cuts=(), held_as=jnp.bfloat16):
    values = jax.random.normal(rng, dims, jnp.float32) * deviation
    if len(cuts) > 0:
        values = steps_of(rng, dims, cuts, -0.22, 0.18) * values
    return jnp.clip(values, min=-reach, max=reach).astype(held_as)


def setup_inputs(seed: int = 0) -> dict:
    arg_keys = jax.random.split(jax.random.key(seed), 22)
    query_embed = noise(arg_keys[0], (LEN, PAIRS, D), 1.0, 6.0, ((0, 4), (1, 4)))
    key_embed = noise(arg_keys[1], (LEN, PAIRS, D), 1.0, 6.0, ((0, 4), (1, 4)))
    crop_counts = draw_crop_counts(jax.random.fold_in(arg_keys[21], 71), 0)
    pair_mask = draw_pair_mask(jax.random.fold_in(arg_keys[21], 71), 0)
    negative_queue = noise(arg_keys[4], (QUEUE, D), 1.0, 6.0, ((0, 4),))
    online_inproj = noise(arg_keys[5], (LAYERS, D, 3, D), D ** -0.5, 0.21875, ((0, 2), (3, 4)))
    online_inbias = noise(arg_keys[6], (LAYERS, 2, HEADS, HEAD), 0.5, 3.0, ((0, 2), (2, 4)))
    online_outproj = noise(arg_keys[7], (LAYERS, D, D), (D // 8) ** -0.5, 0.625, ((0, 2), (1, 4)))
    online_gains = jnp.clip(1.0 + 0.1 * jax.random.normal(arg_keys[8], (LAYERS, 2, D), jnp.float32), 0.5, 1.5).astype(jnp.bfloat16)
    online_shifts = noise(arg_keys[9], (LAYERS, 4, D), 0.2, 1.1953125, ((0, 2),))
    online_expand = noise(arg_keys[10], (LAYERS, D, FF), D ** -0.5, 0.21875, ((0, 2), (2, 4)))
    online_expbias = noise(arg_keys[11], (LAYERS, HEADS, FF // HEADS), 0.5, 3.0, ((0, 2), (1, 4)))
    online_contract = noise(arg_keys[12], (LAYERS, FF, D), FF ** -0.5, 0.109375, ((0, 2), (1, 4)))
    momentum_inproj = noise(arg_keys[13], (LAYERS, D, 3, D), D ** -0.5, 0.21875, ((0, 2), (3, 4)))
    momentum_inbias = noise(arg_keys[14], (LAYERS, 2, HEADS, HEAD), 0.5, 3.0, ((0, 2), (2, 4)))
    momentum_outproj = noise(arg_keys[15], (LAYERS, D, D), (D // 8) ** -0.5, 0.625, ((0, 2), (1, 4)))
    momentum_gains = jnp.clip(1.0 + 0.1 * jax.random.normal(arg_keys[16], (LAYERS, 2, D), jnp.float32), 0.5, 1.5).astype(jnp.bfloat16)
    momentum_shifts = noise(arg_keys[17], (LAYERS, 4, D), 0.2, 1.1953125, ((0, 2),))
    momentum_expand = noise(arg_keys[18], (LAYERS, D, FF), D ** -0.5, 0.21875, ((0, 2), (2, 4)))
    momentum_expbias = noise(arg_keys[19], (LAYERS, HEADS, FF // HEADS), 0.5, 3.0, ((0, 2), (1, 4)))
    momentum_contract = noise(arg_keys[20], (LAYERS, FF, D), FF ** -0.5, 0.109375, ((0, 2), (1, 4)))
    return {"query_embed": query_embed, "key_embed": key_embed, "crop_counts": crop_counts, "pair_mask": pair_mask, "negative_queue": negative_queue, "online_inproj": online_inproj, "online_inbias": online_inbias, "online_outproj": online_outproj, "online_gains": online_gains, "online_shifts": online_shifts, "online_expand": online_expand, "online_expbias": online_expbias, "online_contract": online_contract, "momentum_inproj": momentum_inproj, "momentum_inbias": momentum_inbias, "momentum_outproj": momentum_outproj, "momentum_gains": momentum_gains, "momentum_shifts": momentum_shifts, "momentum_expand": momentum_expand, "momentum_expbias": momentum_expbias, "momentum_contract": momentum_contract}


TEMPER = 0.05
NORM_EPS = 1e-06
NEG_FILL = -1000000000.0
HIGH = lax.Precision.HIGHEST

@jax.custom_vjp
def low(v):
    return lax.optimization_barrier(v.astype(jnp.bfloat16)).astype(jnp.float32)

@jax.custom_vjp
def low_back(v):
    return v

def low_keep(v):
    return (low(v), None)

def low_pass(kept, grad):
    return (grad,)

def back_keep(v):
    return (v, None)

def back_low(kept, grad):
    return (low(grad),)
low.defvjp(low_keep, low_pass)
low_back.defvjp(back_keep, back_low)

def layer_norm(values, gain_row, shift_row):
    center = values - lax.optimization_barrier(jnp.mean(values, axis=-1, keepdims=True))
    spread = lax.optimization_barrier(jnp.mean(center * center, axis=-1, keepdims=True))
    return center * lax.rsqrt(spread + NORM_EPS) * gain_row + shift_row

def normalize(values):
    return values * lax.rsqrt(lax.optimization_barrier(jnp.sum(values * values, axis=-1, keepdims=True)) + NORM_EPS)

def attend_block(members):
    queries, keys_here, values, keep = members
    scale = HEAD ** (-0.5)
    scores = low_back(jnp.einsum('qbhd,kbhd->bhqk', queries, keys_here, precision=HIGH) * scale)
    scores = jnp.where(jnp.transpose(keep)[:, None, None, :], scores, NEG_FILL)
    shares = low(jax.nn.softmax(scores, axis=-1))
    return low(low_back(jnp.einsum('bhqk,kbhd->qbhd', shares, values, precision=HIGH)))

def attention(queries, keys_here, values, keep):
    length, pair_count, width = queries.shape
    block_pairs = math.gcd(pair_count, 16)
    blocks = pair_count // block_pairs

    def split_heads(member):
        shaped = member.reshape((length, blocks, block_pairs) + member.shape[2:])
        return jnp.moveaxis(shaped, 1, 0)
    heads_form = [split_heads(member.reshape(length, pair_count, HEADS, HEAD)) for member in (queries, keys_here, values)]
    result = lax.map(jax.checkpoint(attend_block), (heads_form[0], heads_form[1], heads_form[2], split_heads(keep)))
    return jnp.moveaxis(result, 0, 1).reshape(length, pair_count, width)

def run_layer(inputs, weights, keep):
    inproj, inbias, outproj, gains, shifts, expand, expbias, contract = weights
    width = inputs.shape[2]
    project = low_back(jnp.einsum('lpd,dcn->lpcn', inputs, inproj, precision=HIGH))
    bias = inbias.reshape(2, width)
    queries = low(project[:, :, 0] + bias[0])
    keys_here = low(project[:, :, 1])
    values = low(project[:, :, 2] + bias[1])
    context = attention(queries, keys_here, values, keep)
    attn_out = low_back(jnp.einsum('lpn,nd->lpd', context, outproj, precision=HIGH)) + shifts[0]
    hidden = layer_norm(inputs + attn_out, gains[0], shifts[1])
    inner = low_back(jnp.einsum('lpd,df->lpf', low(hidden), expand, precision=HIGH)) + expbias.reshape(-1)
    active = low(jax.nn.gelu(inner, approximate=False))
    feed_out = low_back(jnp.einsum('lpf,fd->lpd', active, contract, precision=HIGH)) + shifts[2]
    layer_out = layer_norm(hidden + feed_out, gains[1], shifts[3])
    return (layer_out, attn_out, feed_out)

def pool(values, keep, counts):
    return lax.optimization_barrier(jnp.sum(jnp.where(keep[..., None], values, 0.0), axis=0)) / counts.astype(jnp.float32)[:, None]

def masked_square(values, keep):
    return jnp.sum(jnp.where(keep[..., None], values * values, 0.0))

def reference(query_embed, key_embed, crop_counts, pair_mask, negative_queue, online_inproj, online_inbias, online_outproj, online_gains, online_shifts, online_expand, online_expbias, online_contract, momentum_inproj, momentum_inbias, momentum_outproj, momentum_gains, momentum_shifts, momentum_expand, momentum_expbias, momentum_contract):
    online = tuple((member.astype(jnp.float32) for member in (online_inproj, online_inbias, online_outproj, online_gains, online_shifts, online_expand, online_expbias, online_contract)))
    momentum = tuple((member.astype(jnp.float32) for member in (momentum_inproj, momentum_inbias, momentum_outproj, momentum_gains, momentum_shifts, momentum_expand, momentum_expbias, momentum_contract)))
    positions = jnp.arange(LEN)
    query_keep = positions[:, None] < crop_counts[None, :, 0]
    key_keep = positions[:, None] < crop_counts[None, :, 1]
    key_state = key_embed.astype(jnp.float32)
    for layer_index in range(LAYERS):
        if layer_index > 0:
            key_state = low(key_state)
        key_state = run_layer(key_state, [member[layer_index] for member in momentum], key_keep)[0]
    key_unit = low(normalize(pool(key_state, key_keep, crop_counts[:, 1])))
    queue_unit = low(normalize(negative_queue.astype(jnp.float32)))
    live = pair_mask.astype(jnp.float32)
    live_total = jnp.sum(live)
    token_total = jnp.sum(query_keep.astype(jnp.float32))
    own_pair = jnp.arange(PAIRS)[:, None] == jnp.arange(PAIRS)[None, :]

    def forward(embed, weights):
        state = low_back(embed)
        squares = []
        for layer_index in range(LAYERS):
            if layer_index > 0:
                state = low_back(low(state))
            state, attn_out, feed_out = run_layer(state, [member[layer_index] for member in weights], query_keep)
            squares.append(jnp.stack([masked_square(attn_out, query_keep), masked_square(feed_out, query_keep), masked_square(state, query_keep)]))
        query_unit = low(normalize(pool(state, query_keep, crop_counts[:, 0])))
        positive = low_back(jnp.dot(query_unit, key_unit.T, precision=HIGH)) / TEMPER
        positive = jnp.where(live[None, :] > 0, positive, NEG_FILL)
        negative = low_back(jnp.dot(query_unit, queue_unit.T, precision=HIGH)) / TEMPER
        totals = jax.nn.logsumexp(jnp.concatenate([positive, negative], axis=1), axis=1)
        target = lax.optimization_barrier(jnp.sum(jnp.where(own_pair, positive, 0.0), axis=1))
        loss = jnp.sum(live * (totals - target)) / live_total
        rms = jnp.sqrt(jnp.stack(squares) / (token_total * D))
        return (loss, rms)
    embed = query_embed.astype(jnp.float32)
    loss, pull, rms = jax.vjp(forward, embed, online, has_aux=True)
    d_embed, d_weights = pull(jnp.ones_like(loss))
    return (loss, d_embed.astype(jnp.bfloat16), d_weights[0], d_weights[1], d_weights[2], d_weights[3], d_weights[4], d_weights[5], d_weights[6], d_weights[7], rms)
```

```python
import functools

import jax
import jax.numpy as jnp
from jax import lax
from jax.experimental import pallas as pl
from jax.experimental.pallas import tpu as pltpu
from jax.sharding import PartitionSpec as P

TEMPER = 0.05
NORM_EPS = 1e-06
NEG_FILL = -1000000000.0
F32 = jnp.float32
LOW = jnp.bfloat16
VMEM_LIMIT = 40 * 1024 * 1024

ROW_GAIN = 0
ROW_SHIFT = 2
ROW_EXP = 6
ROW_IN = 7


def dot_nn(a, b):
    return lax.dot_general(a, b, (((1,), (0,)), ((), ())), preferred_element_type=F32)


def dot_nt(a, b):
    return lax.dot_general(a, b, (((1,), (1,)), ((), ())), preferred_element_type=F32)


def dot_tn(a, b):
    return lax.dot_general(a, b, (((0,), (0,)), ((), ())), preferred_element_type=F32)


def kernel_call(body, outs, scalars, arrays, flops, name):
    in_specs = [pl.BlockSpec(memory_space=pltpu.SMEM)] + [
        pl.BlockSpec(memory_space=pltpu.VMEM) for _ in arrays
    ]
    moved = sum(a.size * a.dtype.itemsize for a in arrays) + sum(
        functools.reduce(lambda x, y: x * y, s, 1) * jnp.dtype(d).itemsize for s, d in outs
    )
    return pl.pallas_call(
        body,
        out_shape=[jax.ShapeDtypeStruct(s, d) for s, d in outs],
        in_specs=in_specs,
        out_specs=[pl.BlockSpec(memory_space=pltpu.VMEM) for _ in outs],
        compiler_params=pltpu.CompilerParams(vmem_limit_bytes=VMEM_LIMIT),
        cost_estimate=pl.CostEstimate(flops=flops, bytes_accessed=moved, transcendentals=0),
        name=name,
    )(scalars, *arrays)


def swap(value, axis, distance):
    count = lax.axis_size(axis)
    return lax.ppermute(value, axis, [(i, i ^ distance) for i in range(count)])


def over_x(value):
    return swap(value, "heads", 1)


def over_y(value):
    return swap(value, "heads", 2)


def over_core(value):
    return swap(value, "section", 1)


def bf(value):
    return value.astype(LOW)


def norm_parts(values):
    mean = jnp.mean(values, axis=-1, keepdims=True)
    center = values - mean
    spread = jnp.mean(center * center, axis=-1, keepdims=True)
    rstd = lax.rsqrt(spread + NORM_EPS)
    return center * rstd, rstd


def row_keep(scal, pair, rows):
    position = scal[0] * rows + lax.broadcasted_iota(jnp.int32, (rows, 1), 0)
    return position < scal[3 + pair]


def key_keep(scal, pair, rows, order):
    lane = lax.broadcasted_iota(jnp.int32, (1, 4 * rows), 1)
    slot = lane // rows
    inner = lane - slot * rows
    if order == (0, 2, 1, 3):
        slot = (slot & 1) * 2 + slot // 2
    block = jnp.bitwise_xor(slot, scal[0])
    return block * rows + inner < scal[3 + pair]


def attn_forward(scal, own, first, second, wqkv, wout, small, order, save):
    pairs, rows, width = own.shape
    local = wout.shape[0]
    heads = local // 64
    full = 4 * rows

    def body(s, own_r, g1_r, g2_r, wq_r, wo_r, sm_r, p0_r, p1_r, p2_r, *kept):
        def one(pair, _):
            rows_in = jnp.concatenate([own_r[pair], g1_r[pair], g2_r[0, pair], g2_r[1, pair]], axis=0)
            project = dot_nt(rows_in, wq_r[...])
            q = bf(project[:, :local] + sm_r[ROW_IN : ROW_IN + 1, :local])
            k = bf(project[:, local : 2 * local])
            v = bf(project[:, 2 * local :] + sm_r[ROW_IN : ROW_IN + 1, local : 2 * local])
            if save:
                kept[0][pair, :, :local] = q
                kept[0][pair, :, local : 2 * local] = k
                kept[0][pair, :, 2 * local :] = v
            keep = key_keep(s, pair, rows, order)
            pieces = []
            for h in range(heads):
                cut = slice(64 * h, 64 * h + 64)
                scores = jnp.where(keep, dot_nt(q[:, cut] * 0.125, k[:, cut]), NEG_FILL)
                raised = jnp.exp(scores - jnp.max(scores, axis=-1, keepdims=True))
                shares = bf(raised / jnp.sum(raised, axis=-1, keepdims=True))
                if save:
                    kept[1][pair, h] = shares
                pieces.append(bf(dot_nn(shares, v[:, cut])))
            context = jnp.concatenate(pieces, axis=1)
            if save:
                kept[2][pair] = context
            out = dot_nn(context, wo_r[...])
            p0_r[pair] = out[:rows]
            p1_r[pair] = bf(out[rows : 2 * rows])
            p2_r[0, pair] = bf(out[2 * rows : 3 * rows])
            p2_r[1, pair] = bf(out[3 * rows :])
            return 0

        lax.fori_loop(0, pairs, one, 0)

    outs = [
        ((pairs, rows, width), F32),
        ((pairs, rows, width), LOW),
        ((2, pairs, rows, width), LOW),
    ]
    if save:
        outs += [
            ((pairs, full, 3 * local), LOW),
            ((pairs, heads, full, full), LOW),
            ((pairs, full, local), LOW),
        ]
    flops = 2 * pairs * full * (4 * local * width + 2 * local * full)
    return kernel_call(body, outs, scal, [own, first, second, wqkv, wout, small], flops, "attn_forward")


def feed_forward(scal, own, first, second, wexp, wcon, small, order, save):
    pairs, rows, width = own.shape
    hidden_units = wexp.shape[1]
    full = 4 * rows

    def body(s, own_r, g1_r, g2_r, we_r, wc_r, sm_r, p0_r, p1_r, p2_r, *kept):
        def one(pair, _):
            rows_in = jnp.concatenate([own_r[pair], g1_r[pair], g2_r[0, pair], g2_r[1, pair]], axis=0)
            inner = dot_nn(rows_in, we_r[...]) + sm_r[ROW_EXP : ROW_EXP + 1, :]
            phi = 0.5 * (1.0 + lax.erf(inner * (0.5**0.5)))
            active = bf(inner * phi)
            if save:
                density = jnp.exp(-0.5 * inner * inner) * 0.3989422804014327
                kept[0][pair] = active
                kept[1][pair] = bf(phi + inner * density)
            out = dot_nn(active, wc_r[...])
            p0_r[pair] = out[:rows]
            p1_r[pair] = bf(out[rows : 2 * rows])
            p2_r[0, pair] = bf(out[2 * rows : 3 * rows])
            p2_r[1, pair] = bf(out[3 * rows :])
            return 0

        lax.fori_loop(0, pairs, one, 0)

    outs = [
        ((pairs, rows, width), F32),
        ((pairs, rows, width), LOW),
        ((2, pairs, rows, width), LOW),
    ]
    if save:
        outs += [((pairs, full, hidden_units), LOW), ((pairs, full, hidden_units), LOW)]
    flops = 4 * pairs * full * width * hidden_units
    return kernel_call(body, outs, scal, [own, first, second, wexp, wcon, small], flops, "feed_forward")


def norm_middle(scal, part, second, first, layer_in, small, save):
    pairs, rows, width = part.shape

    def body(s, p_r, g_r, f_r, x_r, sm_r, hid_r, low_r, *kept):
        total = jnp.zeros((1, width), F32)
        for pair in range(pairs):
            attn = p_r[pair] + g_r[0, pair].astype(F32) + f_r[pair].astype(F32)
            attn = attn + sm_r[ROW_SHIFT : ROW_SHIFT + 1, :]
            mixed = x_r[pair].astype(F32) + attn
            xhat, _ = norm_parts(mixed)
            hidden = xhat * sm_r[ROW_GAIN : ROW_GAIN + 1, :] + sm_r[ROW_SHIFT + 1 : ROW_SHIFT + 2, :]
            hid_r[pair] = hidden
            low_r[pair] = bf(hidden)
            if save:
                kept[0][pair] = mixed
                square = jnp.where(row_keep(s, pair, rows), attn * attn, 0.0)
                total = total + jnp.sum(square, axis=0, keepdims=True)
        if save:
            kept[1][...] = total

    outs = [((pairs, rows, width), F32), ((pairs, rows, width), LOW)]
    if save:
        outs += [((pairs, rows, width), F32), ((1, width), F32)]
    return kernel_call(
        body, outs, scal, [part, second, first, layer_in, small], 20 * part.size, "norm_middle"
    )


def norm_last(scal, part, second, first, hidden, small, save, pool):
    pairs, rows, width = part.shape

    def body(s, p_r, g_r, f_r, h_r, sm_r, out_r, *kept):
        feed_total = jnp.zeros((1, width), F32)
        out_total = jnp.zeros((1, width), F32)
        for pair in range(pairs):
            feed = p_r[pair] + g_r[0, pair].astype(F32) + f_r[pair].astype(F32)
            feed = feed + sm_r[ROW_SHIFT + 2 : ROW_SHIFT + 3, :]
            summed = h_r[pair] + feed
            xhat, _ = norm_parts(summed)
            out = xhat * sm_r[ROW_GAIN + 1 : ROW_GAIN + 2, :] + sm_r[ROW_SHIFT + 3 : ROW_SHIFT + 4, :]
            keep = row_keep(s, pair, rows)
            if pool:
                out_r[pair : pair + 1, :] = jnp.sum(jnp.where(keep, out, 0.0), axis=0, keepdims=True)
            else:
                out_r[pair] = bf(out)
            if save:
                kept[0][pair] = summed
                feed_total += jnp.sum(jnp.where(keep, feed * feed, 0.0), axis=0, keepdims=True)
                out_total += jnp.sum(jnp.where(keep, out * out, 0.0), axis=0, keepdims=True)
        if save:
            kept[1][0:1, :] = feed_total
            kept[1][1:2, :] = out_total

    outs = [((pairs, width), F32) if pool else ((pairs, rows, width), LOW)]
    if save:
        outs += [((pairs, rows, width), F32), ((2, width), F32)]
    return kernel_call(
        body, outs, scal, [part, second, first, hidden, small], 20 * part.size, "norm_last"
    )


def scatter_mid(first, received):
    return bf(first.astype(F32) + received[1].astype(F32))


def gather_stream(own, hop_one, hop_two):
    first = hop_one(own)
    second = hop_two(jnp.stack([own, first]))
    return first, second


def scatter_stream(p1, p2, hop_one, hop_two):
    second = hop_two(p2)
    first = hop_one(scatter_mid(p1, second))
    return second, first


def joined(low_half, high_half, pair, half):
    return low_half[pair] if pair < half else high_half[pair - half]


def whole_rows(half, pair, own_a, own_b, g1a, g1b, g2a, g2b):
    if pair < half:
        return jnp.concatenate([own_a[pair], g1a[pair], g2a[0, pair], g2a[1, pair]], axis=0)
    at = pair - half
    return jnp.concatenate([own_b[at], g2b[0, at], g1b[at], g2b[1, at]], axis=0)


def store_parts(half, pair, rows, out, p0, pfa, pfb, pga, pgb):
    p0[pair] = out[:rows]
    if pair < half:
        pfa[pair] = bf(out[rows : 2 * rows])
        pga[0, pair] = bf(out[2 * rows : 3 * rows])
        pga[1, pair] = bf(out[3 * rows :])
    else:
        at = pair - half
        pfb[at] = bf(out[2 * rows : 3 * rows])
        pgb[0, at] = bf(out[rows : 2 * rows])
        pgb[1, at] = bf(out[3 * rows :])


def parts_shapes(pairs, rows, width):
    half = pairs // 2
    rest = pairs - half
    return [
        ((pairs, rows, width), F32),
        ((half, rows, width), LOW),
        ((rest, rows, width), LOW),
        ((2, half, rows, width), LOW),
        ((2, rest, rows, width), LOW),
    ]


def gather_halves(own_a, own_b):
    g1a, g1b = over_x(own_a), over_y(own_b)
    g2a, g2b = over_y(jnp.stack([own_a, g1a])), over_x(jnp.stack([own_b, g1b]))
    return [own_a, own_b, g1a, g1b, g2a, g2b]


def scatter_halves(pfa, pfb, pga, pgb):
    rga, rgb = over_y(pga), over_x(pgb)
    rfa, rfb = over_x(scatter_mid(pfa, rga)), over_y(scatter_mid(pfb, rgb))
    return [rga, rgb, rfa, rfb]


def scattered(half, pair, p0, rga, rgb, rfa, rfb):
    if pair < half:
        return p0[pair] + rga[0, pair].astype(F32) + rfa[pair].astype(F32)
    at = pair - half
    return p0[pair] + rgb[0, at].astype(F32) + rfb[at].astype(F32)


def norm_backward(values, grad, gain_row):
    xhat, rstd = norm_parts(values)
    scaled = grad * gain_row
    d_values = rstd * (
        scaled
        - jnp.mean(scaled, axis=-1, keepdims=True)
        - xhat * jnp.mean(scaled * xhat, axis=-1, keepdims=True)
    )
    return d_values, jnp.sum(grad * xhat, axis=0, keepdims=True)


def column_sum(values):
    return jnp.sum(values, axis=0, keepdims=True)


def last_backward(scal, summed, small, pooled=None, residual=None, pieces=None):
    pairs, rows, width = summed.shape
    half = pairs // 2

    def body(s, y_r, sm_r, *rest):
        if pooled is not None:
            source, outs = rest[:1], rest[1:]
        else:
            source, outs = rest[:6], rest[6:]
        d_r, la_r, lb_r, rows_r = outs
        totals = [jnp.zeros((1, width), F32) for _ in range(3)]
        for pair in range(pairs):
            if pooled is not None:
                grad = jnp.where(row_keep(s, pair, rows), source[0][pair : pair + 1, :], 0.0)
            else:
                grad = source[0][pair] + scattered(half, pair, *source[1:])
                grad = bf(grad).astype(F32)
            d_summed, d_gain = norm_backward(y_r[pair], grad, sm_r[ROW_GAIN + 1 : ROW_GAIN + 2, :])
            d_r[pair] = d_summed
            if pair < half:
                la_r[pair] = bf(d_summed)
            else:
                lb_r[pair - half] = bf(d_summed)
            for i, v in enumerate((d_gain, column_sum(grad), column_sum(d_summed))):
                totals[i] = totals[i] + v
        for i in range(3):
            rows_r[i : i + 1, :] = totals[i]

    source = [pooled] if pooled is not None else [residual] + pieces
    outs = [
        ((pairs, rows, width), F32),
        ((half, rows, width), LOW),
        ((pairs - half, rows, width), LOW),
        ((3, width), F32),
    ]
    return kernel_call(body, outs, scal, [summed, small] + source, 30 * summed.size, "last_backward")


def middle_backward(scal, mixed, small, residual, pieces):
    pairs, rows, width = mixed.shape
    half = pairs // 2

    def body(s, y_r, sm_r, *rest):
        source, outs = rest[:6], rest[6:]
        d_r, la_r, lb_r, rows_r = outs
        totals = [jnp.zeros((1, width), F32) for _ in range(3)]
        for pair in range(pairs):
            grad = source[0][pair] + scattered(half, pair, *source[1:])
            d_mixed, d_gain = norm_backward(y_r[pair], grad, sm_r[ROW_GAIN : ROW_GAIN + 1, :])
            d_r[pair] = d_mixed
            if pair < half:
                la_r[pair] = bf(d_mixed)
            else:
                lb_r[pair - half] = bf(d_mixed)
            for i, v in enumerate((d_gain, column_sum(grad), column_sum(d_mixed))):
                totals[i] = totals[i] + v
        for i in range(3):
            rows_r[i : i + 1, :] = totals[i]

    outs = [
        ((pairs, rows, width), F32),
        ((half, rows, width), LOW),
        ((pairs - half, rows, width), LOW),
        ((3, width), F32),
    ]
    return kernel_call(
        body, outs, scal, [mixed, small, residual] + pieces, 30 * mixed.size, "middle_backward"
    )


def feed_backward(scal, grads, slope, wexp, wcon):
    pairs, full, units = slope.shape
    rows, width = full // 4, wexp.shape[0]
    half = pairs // 2

    def body(s, *refs):
        grad_r, (sl_r, we_r, wc_r), outs = refs[:6], refs[6:9], refs[9:]
        dinner_r, bias_r = outs[5:]
        total = jnp.zeros((1, units), F32)
        for pair in range(pairs):
            d_feed = whole_rows(half, pair, *grad_r)
            d_inner = dot_nt(d_feed, wc_r[...]) * sl_r[pair].astype(F32)
            total = total + column_sum(d_inner)
            low = bf(d_inner)
            dinner_r[pair] = low
            store_parts(half, pair, rows, dot_nt(low, we_r[...]), *outs[:5])
        bias_r[...] = total

    outs = parts_shapes(pairs, rows, width) + [((pairs, full, units), LOW), ((1, units), F32)]
    flops = 4 * pairs * full * width * units
    return kernel_call(body, outs, scal, grads + [slope, wexp, wcon], flops, "feed_backward")


def attn_backward(scal, grads, qkv, shares, context, wqkv, wout):
    pairs, full, triple = qkv.shape
    local = triple // 3
    heads = local // 64
    rows, width = full // 4, wout.shape[1]
    half = pairs // 2

    def body(s, *refs):
        grad_r, (qkv_r, sh_r, cx_r, wq_r, wo_r), outs = refs[:6], refs[6:11], refs[11:]
        dproj_r, bias_r = outs[5:]
        q_total = jnp.zeros((1, local), F32)
        v_total = jnp.zeros((1, local), F32)
        for pair in range(pairs):
            d_attn = whole_rows(half, pair, *grad_r)
            d_context = bf(dot_nt(d_attn, wo_r[...]))
            q = qkv_r[pair, :, :local]
            k = qkv_r[pair, :, local : 2 * local]
            v = qkv_r[pair, :, 2 * local :]
            weighted = d_context.astype(F32) * cx_r[pair].astype(F32)
            dqs, dks, dvs = [], [], []
            for h in range(heads):
                cut = slice(64 * h, 64 * h + 64)
                share = sh_r[pair, h]
                dc = d_context[:, cut]
                dvs.append(dot_tn(share, dc))
                drop = jnp.sum(weighted[:, cut], axis=-1, keepdims=True)
                d_scores = bf(share.astype(F32) * (dot_nt(dc, v[:, cut]) - drop))
                dqs.append(dot_nn(d_scores, k[:, cut]) * 0.125)
                dks.append(dot_tn(d_scores, q[:, cut]) * 0.125)
            dq = jnp.concatenate(dqs, axis=1)
            dk = jnp.concatenate(dks, axis=1)
            dv = jnp.concatenate(dvs, axis=1)
            q_total = q_total + column_sum(dq)
            v_total = v_total + column_sum(dv)
            d_project = bf(jnp.concatenate([dq, dk, dv], axis=1))
            dproj_r[pair] = d_project
            store_parts(half, pair, rows, dot_nn(d_project, wq_r[...]), *outs[:5])
        bias_r[...] = jnp.zeros((1, width), F32)
        bias_r[:, :local] = q_total
        bias_r[:, local : 2 * local] = v_total

    outs = parts_shapes(pairs, rows, width) + [((pairs, full, triple), LOW), ((1, width), F32)]
    flops = 2 * pairs * full * (4 * local * width + 4 * local * full)
    return kernel_call(
        body, outs, scal, grads + [qkv, shares, context, wqkv, wout], flops, "attn_backward"
    )


def put_blocks(s, out_ref, at, value, blocks):
    span = value.shape[0] // blocks
    half = span // 2
    for block in range(blocks):
        for side in range(2):
            piece = value[block * span + side * half : block * span + (side + 1) * half]
            core = jnp.bitwise_xor(s[1], side)
            place = jnp.bitwise_xor(s[2], block)
            if at is None:
                out_ref[core, place] = piece
            else:
                out_ref[core, place, at] = piece


def feed_weights(scal, grads, hidden, active, d_inner, blocks):
    pairs, full, units = active.shape
    own, first, second = hidden
    rows, width = full // 4, own.shape[2]
    half = pairs // 2
    split = blocks > 1

    def body(s, *refs):
        grad_r, (o_r, f_r, g_r, a_r, d_r, out_r) = refs[:6], refs[6:]
        contract = jnp.zeros((width, units), F32)
        expand = jnp.zeros((width, units), F32)
        for pair in range(pairs):
            d_feed = whole_rows(half, pair, *grad_r)
            contract = contract + dot_tn(d_feed, a_r[pair])
            rows_in = jnp.concatenate([o_r[pair], f_r[pair], g_r[0, pair], g_r[1, pair]], axis=0)
            expand = expand + dot_tn(rows_in, d_r[pair])
        if split:
            put_blocks(s, out_r, 0, bf(contract), blocks)
            put_blocks(s, out_r, 1, bf(expand), blocks)
        else:
            out_r[0] = bf(contract)
            out_r[1] = bf(expand)

    shape = (2, blocks, 2, width // blocks // 2, units) if split else (2, width, units)
    flops = 4 * pairs * full * width * units
    return kernel_call(
        body, [(shape, LOW)], scal, grads + [own, first, second, active, d_inner], flops, "feed_weights"
    )[0]


def attn_weights(scal, grads, layer_in, context, d_project, blocks):
    pairs, full, local = context.shape
    own, first, second = layer_in
    width = own.shape[2]
    half = pairs // 2
    split = blocks > 1

    def body(s, *refs):
        grad_r, (o_r, f_r, g_r, c_r, d_r, out_r) = refs[:6], refs[6:]
        outproj = jnp.zeros((width, local), F32)
        inproj = jnp.zeros((width, 3 * local), F32)
        for pair in range(pairs):
            d_attn = whole_rows(half, pair, *grad_r)
            outproj = outproj + dot_tn(d_attn, c_r[pair])
            rows_in = jnp.concatenate([o_r[pair], f_r[pair], g_r[0, pair], g_r[1, pair]], axis=0)
            inproj = inproj + dot_tn(rows_in, d_r[pair])
        both = bf(jnp.concatenate([inproj, outproj], axis=1))
        if split:
            put_blocks(s, out_r, None, both, blocks)
        else:
            out_r[...] = both

    shape = (2, blocks, width // blocks // 2, 4 * local) if split else (width, 4 * local)
    flops = 8 * pairs * full * width * local
    return kernel_call(
        body, [(shape, LOW)], scal, grads + [own, first, second, context, d_project], flops, "attn_weights"
    )[0]


def reduce_blocks(grads):
    count = lax.axis_size("dp")
    mine = grads[0].astype(F32) + over_core(grads[1]).astype(F32)
    low = bf(mine)
    total = mine[0]
    for distance in range(1, count):
        total = total + swap(low[distance], "dp", distance).astype(F32)
    return total


def both_halves(section, layer_zero, layer_one):
    first = section == 0
    kept = jnp.where(first, layer_zero, layer_one)
    arrived = over_core(bf(jnp.where(first, layer_one, layer_zero))).astype(F32)
    return jnp.where(first, kept, arrived), jnp.where(first, arrived, kept)


def summed_over(value, axis):
    count = lax.axis_size(axis)
    distance = 1
    while distance < count:
        value = value + swap(value, axis, distance)
        distance *= 2
    return value


def by_distance(entries, axis):
    count = entries.shape[0]
    order = jnp.bitwise_xor(jnp.arange(count), lax.axis_index(axis))
    chosen = (order[:, None] == jnp.arange(count)[None, :]).astype(entries.dtype)
    flat = jnp.dot(chosen, entries.reshape(count, -1), precision=lax.Precision.HIGHEST)
    return flat.astype(entries.dtype).reshape(entries.shape)


def loss_section(pooled, counts, live, queue_unit, section):
    pairs = pooled.shape[1]
    count = lax.axis_size("dp")
    with jax.named_scope("pool"):
        pooled = summed_over(pooled, "heads")
    vectors = pooled / counts.T[:, :, None]
    inverse = lax.rsqrt(jnp.sum(vectors * vectors, axis=-1, keepdims=True) + NORM_EPS)
    units = vectors * inverse
    low = bf(units)
    width = low.shape[-1]
    flags = jnp.zeros((1, width), LOW).at[0, :pairs].set(bf(live))
    packet = jnp.concatenate([low[0], low[1], flags], axis=0)
    with jax.named_scope("keys"):
        if count <= 8:
            lanes = jnp.stack([packet] + [swap(packet, "dp", r) for r in range(1, count)])
        else:
            lanes = lax.all_gather(packet, "dp", axis=0)
            lanes = by_distance(lanes, "dp")
        every = jnp.stack([lanes, over_core(lanes)])
    keys = every[:, :, pairs : 2 * pairs].reshape(2 * count * pairs, width)
    alive = every[:, :, 2 * pairs, :pairs].reshape(2 * count * pairs).astype(F32)
    queries = lanes[:, :pairs].reshape(count * pairs, width)
    negative = dot_nt(queries, queue_unit) / TEMPER
    raised = jnp.exp(negative)
    mass = jnp.sum(raised, axis=1)
    pull = dot_nn(bf(raised), queue_unit)
    spread = jnp.concatenate([pull, jnp.broadcast_to(mass[:, None], (count * pairs, 128))], axis=1)
    spread = spread.reshape(count, pairs, width + 128)
    with jax.named_scope("pulls"):
        if count <= 8:
            total = spread[0]
            for r in range(1, count):
                total = total + swap(spread[r], "dp", r)
        else:
            placed = by_distance(spread, "dp")
            total = lax.psum_scatter(placed, "dp", scatter_dimension=0, tiled=True)[0]
    positive = dot_nt(low[0], keys) / TEMPER
    positive = jnp.where(alive[None, :] > 0, positive, NEG_FILL)
    pos_raised = jnp.exp(positive)
    mass = total[:, width] + jnp.sum(pos_raised, axis=1)
    own_pair = (jnp.arange(keys.shape[0])[None, :] == jnp.arange(pairs)[:, None]).astype(F32)
    weight = live / jnp.sum(alive)
    loss_part = jnp.sum(weight * (jnp.log(mass) - jnp.sum(own_pair * positive, axis=1)))
    d_positive = bf(weight[:, None] * (pos_raised / mass[:, None] - own_pair) / TEMPER)
    d_unit = dot_nn(d_positive, keys) + (weight / mass / TEMPER)[:, None] * total[:, :width]
    d_vector = inverse[0] * (d_unit - units[0] * jnp.sum(units[0] * d_unit, axis=-1, keepdims=True))
    return loss_part, d_vector / counts[:, 0:1]


def small_rows(gains, shifts, expbias, inbias):
    width = gains.shape[-1]
    inrow = inbias.reshape(1, -1)
    inrow = jnp.concatenate([inrow, jnp.zeros((1, width - inrow.shape[1]), LOW)], axis=1)
    return jnp.concatenate([gains[0], shifts[0], expbias.reshape(1, width), inrow], axis=0)


def per_device(
    query_embed,
    key_embed,
    crop_counts,
    pair_mask,
    negative_queue,
    online_inproj,
    online_inbias,
    online_outproj,
    online_gains,
    online_shifts,
    online_expand,
    online_expbias,
    online_contract,
    momentum_inproj,
    momentum_inbias,
    momentum_outproj,
    momentum_gains,
    momentum_shifts,
    momentum_expand,
    momentum_expbias,
    momentum_contract,
):
    section = lax.axis_index("section")
    head = lax.axis_index("heads")
    data = lax.axis_index("dp")
    dp_count = lax.axis_size("dp")
    rows, pairs_dev, width = query_embed.shape
    pairs = pairs_dev // lax.axis_size("section")
    local = online_outproj.shape[1]
    blocks = dp_count if width % (dp_count * 32) == 0 and dp_count <= 8 else 1

    def own_pairs(table, axis):
        return lax.dynamic_slice_in_dim(table, section * pairs, pairs, axis)

    own_counts = own_pairs(crop_counts, 0)
    scal_q = jnp.concatenate([jnp.stack([head, section, data]), own_counts[:, 0]]).astype(jnp.int32)
    scal_k = jnp.concatenate([jnp.stack([head, section, data]), own_counts[:, 1]]).astype(jnp.int32)

    def weight_set(inproj, inbias, outproj, gains, shifts, expand, expbias, contract):
        return [
            jnp.transpose(inproj[0], (1, 2, 0)).reshape(3 * local, width),
            outproj[0],
            small_rows(gains, shifts, expbias, inbias),
            expand[0],
            contract[0],
        ]

    held_q = weight_set(
        online_inproj,
        online_inbias,
        online_outproj,
        online_gains,
        online_shifts,
        online_expand,
        online_expbias,
        online_contract,
    )
    held_k = weight_set(
        momentum_inproj,
        momentum_inbias,
        momentum_outproj,
        momentum_gains,
        momentum_shifts,
        momentum_expand,
        momentum_expbias,
        momentum_contract,
    )

    def two_layers(held):
        arrived = [over_core(w) for w in held]
        zero = [jnp.where(section == 0, a, b) for a, b in zip(held, arrived)]
        one = [jnp.where(section == 0, b, a) for a, b in zip(held, arrived)]
        for layer in (zero, one):
            layer[2] = layer[2].astype(F32)
        return zero, one

    with jax.named_scope("weights"):
        weights_q = two_layers(held_q)
        weights_k = two_layers(held_k)

    embed_q = jnp.transpose(own_pairs(query_embed, 1), (1, 0, 2))
    embed_k = jnp.transpose(own_pairs(key_embed, 1), (1, 0, 2))
    streams = {
        "q": dict(x=embed_q, scal=scal_q, w=weights_q, one=over_x, two=over_y, order=(0, 1, 2, 3)),
        "k": dict(x=embed_k, scal=scal_k, w=weights_k, one=over_y, two=over_x, order=(0, 2, 1, 3)),
    }
    saved = [{}, {}]
    rms_rows = []
    pooled = {}
    for layer in range(2):
        for name in ("q", "k"):
            st = streams[name]
            save = name == "q"
            wqkv, wout, small, wexp, wcon = st["w"][layer]
            with jax.named_scope("gather_in"):
                first, second = gather_stream(st["x"], st["one"], st["two"])
            p0, p1, p2, *kept = attn_forward(
                st["scal"], st["x"], first, second, wqkv, wout, small, st["order"], save
            )
            with jax.named_scope("scatter_attn"):
                got2, got1 = scatter_stream(p1, p2, st["one"], st["two"])
            hidden, low, *kept_mid = norm_middle(st["scal"], p0, got2, got1, st["x"], small, save)
            if save:
                saved[layer].update(
                    x=[st["x"], first, second],
                    qkv=kept[0],
                    shares=kept[1],
                    context=kept[2],
                    mixed=kept_mid[0],
                )
            with jax.named_scope("gather_hidden"):
                first, second = gather_stream(low, st["one"], st["two"])
            p0, p1, p2, *kept = feed_forward(
                st["scal"], low, first, second, wexp, wcon, small, st["order"], save
            )
            with jax.named_scope("scatter_feed"):
                got2, got1 = scatter_stream(p1, p2, st["one"], st["two"])
            out, *kept_last = norm_last(st["scal"], p0, got2, got1, hidden, small, save, layer == 1)
            if save:
                saved[layer].update(
                    hidden=[low, first, second],
                    active=kept[0],
                    slope=kept[1],
                    summed=kept_last[0],
                )
                rms_rows += [kept_mid[1], kept_last[1]]
            if layer == 0:
                st["x"] = out
            else:
                pooled[name] = out

    queue = negative_queue.astype(F32)
    queue_unit = bf(queue * lax.rsqrt(jnp.sum(queue * queue, axis=-1, keepdims=True) + NORM_EPS))
    live = own_pairs(pair_mask, 0).astype(F32)
    with jax.named_scope("loss"):
        loss_part, d_pool = loss_section(
            jnp.stack([pooled["q"], pooled["k"]]), own_counts.astype(F32), live, queue_unit, section
        )

    feed_grads, attn_grads, norm_rows, bias_rows = [None] * 2, [None] * 2, [None] * 2, [None] * 2
    residual, pieces = None, None
    for layer in (1, 0):
        wqkv, wout, small, wexp, wcon = weights_q[layer]
        kept = saved[layer]
        if layer == 1:
            d_summed, low_a, low_b, rows_last = last_backward(
                scal_q, kept["summed"], small, pooled=d_pool
            )
        else:
            d_summed, low_a, low_b, rows_last = last_backward(
                scal_q, kept["summed"], small, residual=residual, pieces=pieces
            )
        with jax.named_scope("gather_dfeed"):
            grads = gather_halves(low_a, low_b)
        *parts, d_inner, exp_row = feed_backward(scal_q, grads, kept["slope"], wexp, wcon)
        with jax.named_scope("scatter_dhidden"):
            pieces = [parts[0]] + scatter_halves(*parts[1:])
        feed_grads[layer] = feed_weights(
            scal_q, grads, kept["hidden"], kept["active"], d_inner, blocks
        )
        d_mixed, low_a, low_b, rows_mid = middle_backward(
            scal_q, kept["mixed"], small, d_summed, pieces
        )
        with jax.named_scope("gather_dattn"):
            grads = gather_halves(low_a, low_b)
        *parts, d_project, in_row = attn_backward(
            scal_q, grads, kept["qkv"], kept["shares"], kept["context"], wqkv, wout
        )
        with jax.named_scope("scatter_dx"):
            pieces = [parts[0]] + scatter_halves(*parts[1:])
        residual = d_mixed
        attn_grads[layer] = attn_weights(scal_q, grads, kept["x"], kept["context"], d_project, blocks)
        norm_rows[layer] = jnp.concatenate(
            [rows_mid[0:1], rows_last[0:1], rows_mid[2:3], rows_mid[1:2], rows_last[2:3], rows_last[1:2]]
        )
        bias_rows[layer] = jnp.concatenate([exp_row, in_row])

    half = pairs // 2
    p0, rga, rgb, rfa, rfb = pieces
    arrived = jnp.concatenate([rga[0], rgb[0]]).astype(F32) + jnp.concatenate([rfa, rfb]).astype(F32)
    d_in = bf(residual + p0 + arrived)
    with jax.named_scope("input_grad"):
        half_width = width // 2
        mine = lax.dynamic_slice_in_dim(d_in, section * half_width, half_width, 2)
        other = lax.dynamic_slice_in_dim(d_in, (1 - section) * half_width, half_width, 2)
        other = over_core(other)
        ordered = jnp.where(
            section == 0, jnp.concatenate([mine, other]), jnp.concatenate([other, mine])
        )
        input_grad = jnp.transpose(ordered, (1, 0, 2))

    with jax.named_scope("weight_grads"):
        if blocks > 1:
            feed_a, feed_b = both_halves(section, *[reduce_blocks(g) for g in feed_grads])
            attn_a, attn_b = both_halves(section, *[reduce_blocks(g) for g in attn_grads])
            feed_sum = jnp.concatenate([feed_a, feed_b], axis=1)
            attn_sum = jnp.concatenate([attn_a, attn_b], axis=0)
        else:
            def owned(layers):
                return layers[0].astype(F32), layers[1].astype(F32)

            def reduce_plain(layers):
                zero, one = owned(layers)
                mine = jnp.where(section == 0, zero, one)
                other = over_core(bf(jnp.where(section == 0, one, zero)))
                return bf(mine + other.astype(F32))

            feed_sum = lax.psum_scatter(
                reduce_plain(feed_grads), "dp", scatter_dimension=1, tiled=True
            ).astype(F32)
            attn_sum = lax.psum_scatter(
                reduce_plain(attn_grads), "dp", scatter_dimension=0, tiled=True
            ).astype(F32)
    grad_contract = jnp.transpose(feed_sum[0])[None]
    grad_expand = feed_sum[1][None]
    grad_inproj = attn_sum[:, : 3 * local].reshape(1, -1, 3, local)
    grad_outproj = jnp.transpose(attn_sum[:, 3 * local :])[None]

    with jax.named_scope("small_grads"):
        across = jnp.concatenate(norm_rows + rms_rows)
        across = summed_over(across, "heads")
        tokens = jnp.sum(own_counts[:, 0]).astype(F32)
        scalar_row = jnp.zeros((1, width), F32).at[0, 0].set(loss_part).at[0, 1].set(tokens)
        table = jnp.concatenate([across] + bias_rows + [scalar_row])
        table = summed_over(table, "section")
        table = summed_over(table, "dp")
    scalars = table[-1]
    loss_total = scalars[0]
    rms_total = jnp.sum(table[12:18], axis=1).reshape(2, 3)
    rms_values = jnp.sqrt(rms_total / (scalars[1] * width))
    norms = jnp.where(section == 0, table[0:6], table[6:12])
    biases = jnp.where(section == 0, table[18:20], table[20:22])
    cut = width // (dp_count * lax.axis_size("heads"))
    norms = lax.dynamic_slice_in_dim(norms, (data * lax.axis_size("heads") + head) * cut, cut, 1)
    exp_shape, in_shape = online_expbias.shape, online_inbias.shape
    grad_expbias = lax.dynamic_slice_in_dim(
        biases[0].reshape(exp_shape), data * (exp_shape[2] // dp_count), exp_shape[2] // dp_count, 2
    )
    grad_inbias = lax.dynamic_slice_in_dim(
        biases[1, : 2 * local].reshape(in_shape),
        data * (in_shape[3] // dp_count),
        in_shape[3] // dp_count,
        3,
    )
    return (
        loss_total,
        input_grad,
        grad_inproj,
        grad_inbias,
        grad_outproj,
        norms[None, 0:2],
        norms[None, 2:6],
        grad_expand,
        grad_expbias,
        grad_contract,
        rms_values,
    )


def solution(mesh):
    placed = (
        P("heads", "dp", None),
        P("heads", "dp", None),
        P("dp", None),
        P("dp"),
        P("dp", None),
        P("section", None, None, "heads"),
        P("section", None, "heads", None),
        P("section", "heads", None),
        P("section", None, None),
        P("section", None, None),
        P("section", None, "heads"),
        P("section", "heads", None),
        P("section", "heads", None),
        P("section", None, None, "heads"),
        P("section", None, "heads", None),
        P("section", "heads", None),
        P("section", None, None),
        P("section", None, None),
        P("section", None, "heads"),
        P("section", "heads", None),
        P("section", "heads", None),
    )
    return jax.shard_map(
        per_device,
        mesh=mesh,
        in_specs=placed,
        out_specs=(
            P(),
            P("heads", "dp", "section"),
            P("section", "dp", None, "heads"),
            P("section", None, "heads", "dp"),
            P("section", "heads", "dp"),
            P("section", None, ("dp", "heads")),
            P("section", None, ("dp", "heads")),
            P("section", "dp", "heads"),
            P("section", "heads", "dp"),
            P("section", "heads", "dp"),
            P(),
        ),
        check_vma=False,
    )
```

```python
import functools
import types

import jax
import jax.numpy as jnp
from jax import lax
from jax.experimental import pallas as pl
from jax.experimental.pallas import tpu as pltpu
from jax.sharding import PartitionSpec as P

TEMPER = 0.05
NORM_EPS = 1e-06
NEG_FILL = -1000000000.0
F32 = jnp.float32
LOW = jnp.bfloat16
HEADS, SECTION, DP = "heads", "section", "dp"
VMEM_SPARE = 6 * 1024 * 1024
EXTRA = 16

ROW_GAIN = 0
ROW_SHIFT = 2
ROW_EXP = 6
ROW_IN = 7


def dot_nn(a, b):
    return lax.dot_general(a, b, (((1,), (0,)), ((), ())), preferred_element_type=F32)


def dot_nt(a, b):
    return lax.dot_general(a, b, (((1,), (1,)), ((), ())), preferred_element_type=F32)


def dot_tn(a, b):
    return lax.dot_general(a, b, (((0,), (0,)), ((), ())), preferred_element_type=F32)


def bytes_of(shape, dtype):
    return functools.reduce(lambda x, y: x * y, shape, 1) * jnp.dtype(dtype).itemsize


class Loaded:
    def __init__(self, source, buffer, sem):
        self.copy = pltpu.make_async_copy(source, buffer, sem)
        self.copy.start()
        self.buffer = buffer
        self.shape = buffer.shape
        self.waiting = True

    def ready(self):
        if self.waiting:
            self.copy.wait()
            self.waiting = False
        return self.buffer

    def __getitem__(self, index):
        return self.ready()[index]

    @property
    def at(self):
        return self.ready().at


class Stored:
    def __init__(self, target, buffer, sems):
        self.target, self.buffer, self.sems = target, buffer, sems
        self.shape, self.dtype = buffer.shape, buffer.dtype
        self.copies = []

    def __setitem__(self, index, value):
        self.buffer[index] = value

    def send(self, start=0, size=None):
        run = pl.ds(start, self.shape[0] if size is None else size)
        copy = pltpu.make_async_copy(
            self.buffer.at[run], self.target.at[run], self.sems.at[len(self.copies)]
        )
        copy.start()
        self.copies.append(copy)

    def finish(self):
        for copy in self.copies:
            copy.wait()


def kernel_call(
    body, outs, scalars, arrays, flops, name, loads=(), stores=(), distant=(), weights=0
):
    side = distant[-1].shape[-1] if weights else 0
    buffers = [(a.shape, a.dtype) for a in loads] + list(stores)
    if weights:
        buffers.append(((weights, side, side), LOW))
    held = sum(bytes_of(*x) for x in [(a.shape, a.dtype) for a in arrays] + list(outs) + buffers)
    sems = [pltpu.SemaphoreType.DMA((max(1, len(loads) + 2 * len(stores)),))]
    if weights:
        sems.append(pltpu.SemaphoreType.DMA((2 * weights,)))
    counts = [len(scalars), len(arrays), len(loads), len(distant), len(outs), len(stores)]

    def whole(*refs):
        groups = []
        for count in counts + [len(loads), len(stores)]:
            groups.append(list(refs[:count]))
            refs = refs[count:]
        scal, near, load_r, far, out_r, store_r, load_b, store_b = groups
        extra = list(refs[:1]) if weights else []
        sem = refs[1] if weights else refs[0]
        loaded = [Loaded(a, b, sem.at[i]) for i, (a, b) in enumerate(zip(load_r, load_b))]
        base = len(loaded)
        stored = [
            Stored(a, b, sem.at[pl.ds(base + 2 * i, 2)]) for i, (a, b) in enumerate(zip(store_r, store_b))
        ]
        if weights:
            extra.append(refs[2])
        body(*scal, *near, *loaded, *far, *out_r, *stored, *extra)
        for item in loaded:
            item.ready()
        for item in stored:
            if not item.copies:
                item.send()
        for item in stored:
            item.finish()

    hbm = pl.BlockSpec(memory_space=pltpu.HBM)
    vmem = pl.BlockSpec(memory_space=pltpu.VMEM)
    in_specs = [pl.BlockSpec(memory_space=pltpu.SMEM)] * len(scalars)
    in_specs += [vmem] * len(arrays) + [hbm] * (len(loads) + len(distant))
    apart = [pltpu.with_memory_space_constraint(d, pltpu.HBM) for d in [*loads, *distant]]
    return pl.pallas_call(
        whole,
        out_shape=[jax.ShapeDtypeStruct(s, d) for s, d in outs]
        + [pltpu.HBM(s, d) for s, d in stores],
        in_specs=in_specs,
        out_specs=[vmem] * len(outs) + [hbm] * len(stores),
        scratch_shapes=[pltpu.VMEM(s, d) for s, d in buffers] + sems,
        compiler_params=pltpu.CompilerParams(vmem_limit_bytes=held + VMEM_SPARE),
        cost_estimate=pl.CostEstimate(flops=flops, bytes_accessed=held, transcendentals=0),
        name=name,
    )(*scalars, *arrays, *apart)


def here():
    head, core, data = [lax.axis_index(a) for a in (HEADS, SECTION, DP)]
    near = jnp.where(core == 0, 1, 2)
    chosen = jnp.where(core == 0, head // 2, head % 2)
    return types.SimpleNamespace(head=head, core=core, data=data, near=near, chosen=chosen)


def count_of(at, counts, encoder, other=0):
    return counts[2 * at.core + jnp.bitwise_xor(at.chosen, other), encoder]


def table_row(at, tables, layer, encoder, row):
    held, came = [t[encoder, row : row + 1, :] for t in tables]
    return jnp.where(at.core == layer, held, came)


def start_fetch(at, layer, held, arrived, target, sem):
    @pl.when(at.core == layer)
    def _():
        pltpu.make_async_copy(held, target, sem).start()

    @pl.when(at.core != layer)
    def _():
        pltpu.make_async_copy(arrived, target, sem).start()

    return pltpu.make_async_copy(held, target, sem)


def start_copy(source, target, sem):
    copy = pltpu.make_async_copy(source, target, sem)
    copy.start()
    return copy


def fetch_attn(at, layer, encoder, refs, scratch, sems):
    cols, outp, cols_too, outp_too = refs[:4]
    cut = cols.shape[0]
    waits = [
        start_fetch(at, layer, cols, cols_too, scratch.at[0, pl.ds(0, cut)], sems.at[0]),
        start_fetch(at, layer, outp, outp_too, scratch.at[0, pl.ds(cut, outp.shape[0])], sems.at[1]),
    ]
    if len(refs) > 4:
        waits.append(start_copy(refs[4], scratch.at[1], sems.at[2]))
    return waits


def fetch_feed(at, layer, refs, scratch, sems):
    exp, con, exp_too, con_too = refs
    return [
        start_fetch(at, layer, exp, exp_too, scratch.at[0], sems.at[0]),
        start_fetch(at, layer, con, con_too, scratch.at[1], sems.at[1]),
    ]


def swap(value, axis, distance):
    count = lax.axis_size(axis)
    return lax.ppermute(value, axis, [(i, i ^ distance) for i in range(count)])


def hop(value, first_core, second_core):
    count = lax.axis_size(HEADS)
    route = [(i, i ^ first_core) for i in range(count)]
    route += [(count + i, count + (i ^ second_core)) for i in range(count)]
    return lax.ppermute(value, (SECTION, HEADS), route)


def hop_one(value):
    return hop(value, 1, 2)


def hop_two(value):
    return hop(value, 2, 1)


def hop_both(value):
    return hop(value, 3, 3)


def over_core(value):
    return swap(value, SECTION, 1)


def behind(value, mark):
    return lax.optimization_barrier((value, mark))[0]


class Order:
    def __init__(self):
        self.last = None

    def tie(self, value):
        return value if self.last is None else behind(value, self.last)

    def mark(self, value):
        self.last = value


def bf(value):
    return value.astype(LOW)


def norm_parts(values):
    mean = jnp.mean(values, axis=-1, keepdims=True)
    center = values - mean
    spread = jnp.mean(center * center, axis=-1, keepdims=True)
    rstd = lax.rsqrt(spread + NORM_EPS)
    return center * rstd, rstd


def row_position(at, rows, shape, other):
    block_rows = rows // 2
    lane = lax.broadcasted_iota(jnp.int32, shape, 0 if shape[1] == 1 else 1)
    slot = lane // block_rows
    far = 3 - at.near
    block = jnp.bitwise_xor(jnp.bitwise_xor(at.head, other * far), (slot & 1) * far)
    block = jnp.bitwise_xor(block, (slot // 2) * at.near)
    return block * block_rows + lane - slot * block_rows


def row_keep(at, counts, encoder, rows):
    return row_position(at, rows, (rows, 1), 0) < count_of(at, counts, encoder)


def key_keep(at, counts, encoder, rows, other):
    return row_position(at, rows, (1, 2 * rows), other) < count_of(at, counts, encoder, other)


def row_groups(sources):
    if len(sources) == 2:
        return [list(sources)] * 2
    if len(sources[0].shape) == 2:
        own, one, two, far = sources
        return [[own, one], [two, far]]
    own, one, two, far = sources
    return [
        [own.at[0], two.at[1], one.at[0], far.at[1]],
        [two.at[0], own.at[1], far.at[0], one.at[1]],
    ]


def stack_rows(group):
    return jnp.concatenate([piece[...] for piece in group], axis=0)


def put_rows(targets, outs):
    if len(targets) == 4:
        half = outs[0].shape[0] // 2
        values = [outs[0][:half], outs[0][half:], outs[1][:half], outs[1][half:]]
    else:
        total = outs[0] + outs[1]
        half = total.shape[0] // 2
        values = [total[:half], total[half:]]
    for target, value in zip(targets, values):
        target[...] = value.astype(target.dtype)


def parts_shapes(rows, width, count):
    return [((rows, width), F32)] + [((rows, width), LOW)] * (count - 1)


def rows_of(sources):
    shape = sources[0].shape
    return (2 * shape[1], shape[2]) if len(shape) == 3 else shape


def attn_forward(counts, sources, tables, theirs, weights, layer, encoder, save):
    wide = len(sources) == 4
    rows, width = rows_of(sources)
    local = width // 4
    heads = local // 64
    full = 2 * rows
    count = len(sources)

    def body(s, *refs):
        at = here()
        tb, th_r, source, refs = refs[:2], refs[2], refs[3 : 3 + count], refs[3 + count :]
        w_refs, refs = refs[: len(weights)], refs[len(weights) :]
        targets, kept, (w_r, sems) = refs[:count], refs[count:-2], refs[-2:]
        waits = fetch_attn(at, layer, encoder, w_refs, w_r, sems)
        groups = row_groups(source)
        outs = []
        for unit in range(2):
            side = 0 if wide else unit
            rows_in = stack_rows(groups[unit])
            keep = key_keep(at, s, encoder, rows, unit if wide else 0)
            bias = th_r[...] if side else table_row(at, tb, layer, encoder, ROW_IN)
            if unit == 0:
                waits[0].wait()
            elif not wide:
                waits[2].wait()
            project = dot_nt(rows_in, w_r[side, : 3 * local, :])
            q = bf(project[:, :local] + bias[:, :local])
            k = bf(project[:, local : 2 * local])
            v = bf(project[:, 2 * local :] + bias[:, local : 2 * local])
            if save:
                kept[0][unit, :, :local] = q
                kept[0][unit, :, local : 2 * local] = k
                kept[0][unit, :, 2 * local :] = v
                kept[0].send(unit, 1)
            pieces = []
            for h in range(heads):
                cut = slice(64 * h, 64 * h + 64)
                scores = jnp.where(keep, dot_nt(q[:, cut] * 0.125, k[:, cut]), NEG_FILL)
                raised = jnp.exp(scores - jnp.max(scores, axis=-1, keepdims=True))
                shares = bf(raised / jnp.sum(raised, axis=-1, keepdims=True))
                if save:
                    kept[1][unit * heads + h] = shares
                pieces.append(bf(dot_nn(shares, v[:, cut])))
            context = jnp.concatenate(pieces, axis=1)
            if save:
                kept[2][unit] = context
                kept[1].send(unit * heads, heads)
                kept[2].send(unit, 1)
            if unit == 0:
                waits[1].wait()
            outs.append(dot_nn(context, w_r[side, 3 * local :, :]))
        put_rows(targets, outs)

    outs, stores = parts_shapes(rows, width, count), []
    if save:
        stores = [
            ((2, full, 3 * local), LOW),
            ((2 * heads, full, full), LOW),
            ((2, full, local), LOW),
        ]
    flops = 4 * full * (4 * local * width + 2 * local * full)
    got = kernel_call(
        body,
        outs,
        [counts],
        tables + [theirs] + sources,
        flops,
        "attn_forward",
        [],
        stores,
        weights,
        1 if wide else 2,
    )
    return got[:count], got[count:]


def feed_forward(counts, sources, tables, weights, layer, encoder, save):
    rows, width = rows_of(sources)
    units = weights[0].shape[1]
    full = 2 * rows
    count = len(sources)

    def body(s, *refs):
        at = here()
        tb, source, refs = refs[:2], refs[2 : 2 + count], refs[2 + count :]
        w_refs, refs = refs[: len(weights)], refs[len(weights) :]
        targets, kept, (w_r, sems) = refs[:count], refs[count:-2], refs[-2:]
        waits = fetch_feed(at, layer, w_refs, w_r, sems)
        groups = row_groups(source)
        bias = table_row(at, tb, layer, encoder, ROW_EXP)
        outs = []
        for unit in range(2):
            rows_in = stack_rows(groups[unit])
            if unit == 0:
                waits[0].wait()
            inner = dot_nn(rows_in, w_r[0]) + bias
            phi = 0.5 * (1.0 + lax.erf(inner * (0.5**0.5)))
            active = bf(inner * phi)
            if save:
                density = jnp.exp(-0.5 * inner * inner) * 0.3989422804014327
                kept[0][unit] = active
                kept[1][unit] = bf(phi + inner * density)
                kept[0].send(unit, 1)
                kept[1].send(unit, 1)
            if unit == 0:
                waits[1].wait()
            outs.append(dot_nn(active, w_r[1]))
        put_rows(targets, outs)

    outs, stores = parts_shapes(rows, width, count), []
    if save:
        stores = [((2, full, units), LOW), ((2, full, units), LOW)]
    flops = 8 * full * width * units
    near = tables + sources
    got = kernel_call(body, outs, [counts], near, flops, "feed_forward", [], stores, weights, 2)
    return got[:count], got[count:]


def masked_squares(at, counts, encoder, values, rows):
    return column_sum(jnp.where(row_keep(at, counts, encoder, rows), values * values, 0.0))


def norm_middle(counts, pieces, layer_in, tables, layer, encoder, save):
    rows, width = pieces[0].shape
    count, inputs = len(pieces), len(layer_in)

    def body(s, *refs):
        at = here()
        tb, added, refs = refs[:2], refs[2 : 2 + count], refs[2 + count :]
        x_refs, refs = refs[:inputs], refs[inputs:]
        (square_r, low_r, mixed_r) = refs if save else (None, refs[0], None)
        if inputs == 1:
            rows_in = x_refs[0][...]
        else:
            rows_in = jnp.concatenate([x_refs[0][0], x_refs[1][1]], axis=0)
        attn = scattered(*added) + table_row(at, tb, layer, encoder, ROW_SHIFT)
        mixed = rows_in.astype(F32) + attn
        if save:
            mixed_r[...] = mixed
            mixed_r.send()
        xhat, _ = norm_parts(mixed)
        gain = table_row(at, tb, layer, encoder, ROW_GAIN)
        low_r[...] = bf(xhat * gain + table_row(at, tb, layer, encoder, ROW_SHIFT + 1))
        if save:
            square_r[...] = masked_squares(at, s, encoder, attn, rows)

    outs, stores = [((rows, width), LOW)], []
    if save:
        outs, stores = [((1, width), F32)] + outs, [((rows, width), F32)]
    near = tables + pieces + layer_in
    return kernel_call(body, outs, [counts], near, 20 * rows * width, "norm_middle", [], stores)


def norm_last(counts, pieces, hidden, tables, layer, encoder, save):
    rows, width = hidden.shape
    count = len(pieces)
    pool = layer == 1

    def body(s, *refs):
        at = here()
        tb, added, h_r, refs = refs[:2], refs[2 : 2 + count], refs[2 + count], list(refs[3 + count :])
        out_r = refs.pop(0)
        square_r = refs.pop(0) if save else None
        feed = scattered(*added) + table_row(at, tb, layer, encoder, ROW_SHIFT + 2)
        summed = h_r[...].astype(F32) + feed
        if save:
            refs[0][...] = summed
            refs[0].send()
        xhat, _ = norm_parts(summed)
        gain = table_row(at, tb, layer, encoder, ROW_GAIN + 1)
        out = xhat * gain + table_row(at, tb, layer, encoder, ROW_SHIFT + 3)
        if pool:
            out_r[...] = column_sum(jnp.where(row_keep(at, s, encoder, rows), out, 0.0))
        else:
            out_r[...] = bf(out)
        if save:
            square_r[0:1, :] = masked_squares(at, s, encoder, feed, rows)
            square_r[1:2, :] = masked_squares(at, s, encoder, out, rows)

    outs, stores = [((1, width), F32) if pool else ((rows, width), LOW)], []
    if save:
        outs, stores = outs + [((2, width), F32)], [((rows, width), F32)]
    near = tables + pieces + [hidden]
    return kernel_call(body, outs, [counts], near, 20 * rows * width, "norm_last", [], stores)


def gather(own, wide):
    hops = (hop_one, hop_two, hop_both) if wide else (hop_one,)
    return [own] + [move(own) for move in hops]


def scatter(part, *others):
    hops = (hop_one, hop_two, hop_both)
    return [part] + [move(value) for move, value in zip(hops, others)]


def scattered(part, *others):
    total = part[...]
    for value in others:
        total = total + value[: part.shape[0], :].astype(F32)
    return total


def norm_backward(values, grad, gain_row):
    xhat, rstd = norm_parts(values)
    scaled = grad * gain_row
    d_values = rstd * (
        scaled
        - jnp.mean(scaled, axis=-1, keepdims=True)
        - xhat * jnp.mean(scaled * xhat, axis=-1, keepdims=True)
    )
    return d_values, jnp.sum(grad * xhat, axis=0, keepdims=True)


def column_sum(values):
    return jnp.sum(values, axis=0, keepdims=True)


def norm_gradient(y_r, grad, gain, low_r):
    d_values, d_gain = norm_backward(y_r[...], grad, gain)
    low_r[...] = bf(d_values)
    return d_gain, column_sum(grad), column_sum(d_values)


def last_backward(counts, summed, tables, layer, pooled=None, residual=None, pieces=None):
    rows, width = summed.shape
    near = [pooled] if pooled is not None else [residual] + pieces[1:]
    loads = [summed] if pooled is not None else [summed, pieces[0]]
    inputs = len(near)

    def body(s, held_r, came_r, *rest):
        at = here()
        near_r, (y_r, *part_r), (rows_r, low_r) = rest[:inputs], rest[inputs:-2], rest[-2:]
        if pooled is not None:
            grad = jnp.where(row_keep(at, s, 0, rows), near_r[0][...], 0.0)
        else:
            grad = bf(scattered(part_r[0], *near_r)).astype(F32)
        gain = table_row(at, (held_r, came_r), layer, 0, ROW_GAIN + 1)
        for i, row in enumerate(norm_gradient(y_r, grad, gain, low_r)):
            rows_r[i : i + 1, :] = row

    outs = [((3, width), F32), ((rows, width), LOW)]
    got = kernel_call(
        body, outs, [counts], tables + near, 30 * summed.size, "last_backward", loads
    )
    return got[1], got[0]


def middle_backward(counts, mixed, tables, layer, residual, pieces, last_rows, above):
    rows, width = mixed.shape
    known = [last_rows] + above

    def body(s, held_r, came_r, *rest):
        at = here()
        last_r, above_r, rest = rest[0], rest[1 : len(known)], rest[len(known) :]
        near_r, (y_r, part_r, rows_r, low_r) = rest[:-4], rest[-4:]
        grad = scattered(part_r, *near_r)
        gain = table_row(at, (held_r, came_r), layer, 0, ROW_GAIN)
        d_gain, in_sum, out_sum = norm_gradient(y_r, grad, gain, low_r)
        last = [last_r[i : i + 1, :] for i in range(3)]
        for i, row in enumerate((d_gain, last[0], out_sum, in_sum, last[2], last[1])):
            rows_r[i : i + 1, :] = row
        if above_r:
            rows_r[6:, :] = above_r[0][...]

    outs = [((6 + 6 * len(above), width), F32), ((rows, width), LOW)]
    near = tables + known + [residual] + pieces[1:]
    loads = [mixed, pieces[0]]
    got = kernel_call(body, outs, [counts], near, 30 * mixed.size, "middle_backward", loads)
    return got[1], got[0]


def feed_backward(counts, grads, slope, weights, layer):
    full, units = slope.shape[1:]
    rows, width = grads[0].shape
    count = len(grads)

    def body(s, *refs):
        source, sl_r, refs = refs[:count], refs[count], refs[count + 1 :]
        w_refs, refs = refs[: len(weights)], refs[len(weights) :]
        others, (bias_r, part, dinner_r, w_r, sems) = refs[: count - 1], refs[count - 1 :]
        targets = [part, *others]
        waits = fetch_feed(here(), layer, w_refs, w_r, sems)
        groups = row_groups(source)
        outs = []
        total = jnp.zeros((1, units), F32)
        for unit in range(2):
            if unit == 0:
                waits[1].wait()
            d_inner = dot_nt(stack_rows(groups[unit]), w_r[1]) * sl_r[unit].astype(F32)
            total = total + column_sum(d_inner)
            low = bf(d_inner)
            dinner_r[unit] = low
            dinner_r.send(unit, 1)
            if unit == 0:
                waits[0].wait()
            outs.append(dot_nt(low, w_r[0]))
        bias_r[...] = total
        put_rows(targets, outs)

    part, *outs = parts_shapes(rows, width, count)
    outs, stores = outs + [((1, units), F32)], [part, ((2, full, units), LOW)]
    flops = 8 * full * width * units
    got = kernel_call(
        body, outs, [counts], grads, flops, "feed_backward", [slope], stores, weights, 2
    )
    return [got[count], *got[: count - 1], got[count + 1], got[count - 1]]


def attn_backward(counts, grads, qkv, shares, context, weights, layer, known):
    wide = len(grads) == 4
    full, triple = qkv.shape[1:]
    local = triple // 3
    heads = local // 64
    rows, width = grads[0].shape
    count, extra = len(grads), len(known)

    def body(s, *refs):
        source, known_r, refs = refs[:count], refs[count : count + extra], refs[count + extra :]
        (qkv_r, sh_r, cx_r), refs = refs[:3], refs[3:]
        w_refs, refs = refs[: len(weights)], refs[len(weights) :]
        others, (bias_r, part, dproj_r, w_r, sems) = refs[: count - 1], refs[count - 1 :]
        targets = [part, *[other.at[:rows] for other in others]]
        for other in others[: extra * count]:
            spare = jnp.zeros((EXTRA - known_r[0].shape[0], width), F32)
            other[rows:, :] = bf(jnp.concatenate([known_r[0][...], spare], axis=0))
        waits = fetch_attn(here(), layer, 0, w_refs, w_r, sems)
        groups = row_groups(source)
        bias_r[...] = jnp.zeros((2, width), F32)
        outs = []
        for unit in range(2):
            side = 0 if wide else unit
            if unit == 0:
                waits[1].wait()
            elif not wide:
                waits[2].wait()
            d_context = bf(dot_nt(stack_rows(groups[unit]), w_r[side, triple:, :]))
            q = qkv_r[unit, :, :local]
            k = qkv_r[unit, :, local : 2 * local]
            v = qkv_r[unit, :, 2 * local :]
            weighted = d_context.astype(F32) * cx_r[unit].astype(F32)
            dqs, dks, dvs = [], [], []
            for h in range(heads):
                cut = slice(64 * h, 64 * h + 64)
                share = sh_r[unit * heads + h]
                dc = d_context[:, cut]
                dvs.append(dot_tn(share, dc))
                drop = jnp.sum(weighted[:, cut], axis=-1, keepdims=True)
                d_scores = bf(share.astype(F32) * (dot_nt(dc, v[:, cut]) - drop))
                dqs.append(dot_nn(d_scores, k[:, cut]) * 0.125)
                dks.append(dot_tn(d_scores, q[:, cut]) * 0.125)
            dq = jnp.concatenate(dqs, axis=1)
            dk = jnp.concatenate(dks, axis=1)
            dv = jnp.concatenate(dvs, axis=1)
            bias_r[unit : unit + 1, :local] = column_sum(dq)
            bias_r[unit : unit + 1, local : 2 * local] = column_sum(dv)
            d_project = bf(jnp.concatenate([dq, dk, dv], axis=1))
            dproj_r[unit] = d_project
            dproj_r.send(unit, 1)
            if unit == 0:
                waits[0].wait()
            outs.append(dot_nn(d_project, w_r[side, :triple, :]))
        put_rows(targets, outs)

    part = ((rows, width), F32)
    outs = [((rows + EXTRA * extra, width), LOW)] * (count - 1)
    outs, stores = outs + [((2, width), F32)], [part, ((2, full, triple), LOW)]
    flops = 4 * full * (4 * local * width + 4 * local * full)
    loads = [qkv, shares, context]
    side = 1 if wide else 2
    got = kernel_call(
        body, outs, [counts], grads + known, flops, "attn_backward", loads, stores, weights, side
    )
    return [got[count], *got[: count - 1], got[count + 1], got[count - 1]]


def put_blocks(at, out_ref, parts, extra, blocks, other):
    if extra.shape[0] < EXTRA:
        extra = jnp.concatenate([extra, jnp.zeros((EXTRA - extra.shape[0], extra.shape[1]), F32)], axis=0)
    extra = bf(extra)
    span = parts[0].shape[0] // blocks
    half = span // 2
    wanted = jnp.bitwise_xor(at.core, other)
    for block in range(blocks):
        for i, value in enumerate(parts):
            halves = [bf(value[block * span + j * half : block * span + (j + 1) * half]) for j in range(2)]
            out_ref[block, i * half : (i + 1) * half, :] = jnp.where(wanted == 0, *halves)
        out_ref[block, len(parts) * half :, :] = extra


def weight_grads(counts, grads, inputs, pairs, bias, blocks, name):
    count = len(grads)
    width = grads[0].shape[-1]
    attention = name == "attn_weights"
    columns = sum(p.shape[2] for p in pairs) if attention else pairs[0].shape[2]
    parts_count = 1 if attention else 2

    def body(s, *refs):
        at = here()
        bias_r, g_refs, refs = refs[0], refs[1 : 1 + count], refs[1 + count :]
        x_refs, (o_r, d_r), targets = refs[:count], refs[count : count + 2], refs[count + 2 :]
        g_rows = [stack_rows(g) for g in row_groups(g_refs)]
        back = dot_tn(g_rows[0], o_r[0]) + dot_tn(g_rows[1], o_r[1])
        x_rows = [stack_rows(x) for x in row_groups(x_refs)]
        ahead = dot_tn(x_rows[0], d_r[0]) + dot_tn(x_rows[1], d_r[1])
        row = bias_r[0:1, :] + bias_r[1:2, :] if bias_r.shape[0] == 2 else bias_r[...]
        parts = [jnp.concatenate([ahead, back], axis=1)] if attention else [back, ahead]
        if blocks > 1:
            put_blocks(at, targets[0], parts, row, blocks, 1)
            put_blocks(at, targets[1], parts, row, blocks, 0)
        else:
            for i, part in enumerate(parts):
                targets[0][i] = bf(part)

    if blocks > 1:
        shape = (blocks, parts_count * (width // blocks // 2) + EXTRA, columns)
        outs, stores = [(shape, LOW)], [(shape, LOW)]
    else:
        outs, stores = [((parts_count, width, columns), LOW)], []
    flops = sum(4 * p.shape[1] * width * p.shape[2] for p in pairs)
    loads = grads + inputs + pairs
    got = kernel_call(body, outs, [counts], [bias], flops, name, loads, stores)
    return [got[1], got[0]] if blocks > 1 else got


def add_cores(counts, mine, came, norms=()):
    blocks, rows = mine.shape[:2]
    start = rows - EXTRA

    def body(s, *refs):
        norm_r, (c_r, m_r, out_r) = refs[: len(norms)], refs[len(norms) :]
        for block in range(blocks):
            total = m_r[block].astype(F32) + c_r[block].astype(F32)
            if norms:
                summed = norm_r[0][...]
                for piece in norm_r[1:]:
                    arrived = piece[piece.shape[0] - EXTRA :, :].astype(F32)
                    summed = summed + arrived[: summed.shape[0]]
                spare = jnp.zeros((EXTRA - 1 - summed.shape[0], summed.shape[1]), F32)
                total = jnp.concatenate([total[: start + 1], summed, spare], axis=0)
            out_r[block] = bf(total)
            if block % 2:
                out_r.send(block - 1, 2)

    stores = [(mine.shape, LOW)]
    near = [*norms, came]
    return kernel_call(body, [], [counts], near, mine.size, "add_cores", [mine], stores)[0]


def trade_layers(counts, zero, one, rows_cut):
    rows, width = zero[0].shape

    def body(s, *refs):
        at = here()
        z_refs, refs = refs[: len(zero)], refs[len(zero) :]
        o_refs, refs = refs[: len(one)], refs[len(one) :]
        outs = [refs[-1], *refs[:-1]]
        sums = []
        for group in (z_refs, o_refs):
            total = group[0][...].astype(F32)
            for piece in group[1:]:
                total = total + piece[...].astype(F32)
            sums.append(total)
        own = at.core == 0
        outs[0][...] = jnp.where(own, sums[0], sums[1])
        outs[1][...] = bf(jnp.where(own, sums[1], sums[0]))
        if rows_cut:
            start = rows - EXTRA + 1
            norms = [sums[0][start + 6 * i : start + 6 * (i + 1), :] for i in range(2)]
            outs[2][...] = jnp.where(own, norms[0], norms[1])
            outs[1][start : start + 6, :] = bf(jnp.where(own, norms[1], norms[0]))

    outs, stores = [((rows, width), LOW)], [((rows, width), F32)]
    if rows_cut:
        outs.append(((6, width), F32))
    got = kernel_call(
        body, outs, [counts], [], 4 * rows * width, "trade_layers", zero + one, stores
    )
    return [got[-1], *got[:-1]]


def in_core_order(at, kept, came, start, size):
    mine = kept[start : start + size, :]
    other = came[start : start + size, :].astype(F32)
    own = at.core == 0
    return jnp.concatenate([jnp.where(own, mine, other), jnp.where(own, other, mine)], axis=0)


def place_feed(counts, kept, came):
    rows, width = kept.shape
    part = (rows - EXTRA) // 2

    def body(s, k_r, c_r, con_r, exp_r):
        at = here()
        con_r[...] = in_core_order(at, k_r, c_r, 0, part)
        exp_r[...] = in_core_order(at, k_r, c_r, part, part)

    stores = [((2 * part, width), F32)] * 2
    return kernel_call(
        body, [], [counts], [], 4 * rows * width, "place_feed", [kept, came], stores
    )


def place_attn(counts, kept, came, norms):
    rows, width = kept.shape
    part = rows - EXTRA
    local = width // 4

    def body(s, n_r, k_r, c_r, norm_r, in_r, out_r):
        norm_r[...] = n_r[...] + c_r[part + 1 : part + 7, :].astype(F32)
        both = in_core_order(here(), k_r, c_r, 0, part)
        for i in range(3):
            in_r[i] = both[:, i * local : (i + 1) * local]
        out_r[...] = both[:, 3 * local :].T

    stores = [((3, 2 * part, local), F32), ((local, 2 * part), F32)]
    outs = [((6, width), F32)]
    return kernel_call(
        body, outs, [counts], [norms], 4 * rows * width, "place_attn", [kept, came], stores
    )


def reduce_plain(layers, section, axis):
    mine = jnp.where(section == 0, layers[0], layers[1]).astype(F32)
    other = over_core(jnp.where(section == 0, layers[1], layers[0]))
    low = bf(mine + other.astype(F32))
    return lax.psum_scatter(low, DP, scatter_dimension=axis, tiled=True).astype(F32)


def summed_over(value, axis):
    count = lax.axis_size(axis)
    distance = 1
    while distance < count:
        value = value + swap(value, axis, distance)
        distance *= 2
    return value


def by_distance(entries, axis):
    count = entries.shape[0]
    order = jnp.bitwise_xor(jnp.arange(count), lax.axis_index(axis))
    chosen = (order[:, None] == jnp.arange(count)[None, :]).astype(entries.dtype)
    flat = jnp.dot(chosen, entries.reshape(count, -1), precision=lax.Precision.HIGHEST)
    return flat.astype(entries.dtype).reshape(entries.shape)


def loss_section(pooled, counts, live, queue_unit):
    count = lax.axis_size(DP)
    width = pooled.shape[-1]
    with jax.named_scope("pool"):
        pooled = pooled + hop_one(pooled)
    vectors = pooled / counts[:, None]
    inverse = lax.rsqrt(jnp.sum(vectors * vectors, axis=-1, keepdims=True) + NORM_EPS)
    units = vectors * inverse
    low = bf(units)
    flags = jnp.broadcast_to(bf(live), (1, width))
    packet = jnp.concatenate([low, flags], axis=0)
    with jax.named_scope("keys"):
        if count <= 8:
            lanes = jnp.stack([packet] + [swap(packet, DP, r) for r in range(1, count)])
        else:
            lanes = by_distance(lax.all_gather(packet, DP, axis=0), DP)
    queries = lanes[:, 0]
    with jax.named_scope("keys"):
        every = jnp.stack([lanes[:, 1:], hop_two(lanes[:, 1:])])
        every = jnp.stack([every, over_core(every)]).reshape(4 * count, 2, width)
    keys, alive = every[:, 0], every[:, 1, 0].astype(F32)
    raised = jnp.exp(dot_nt(queries, queue_unit) / TEMPER)
    mass = jnp.sum(raised, axis=1, keepdims=True)
    pull = dot_nn(bf(raised), queue_unit)
    spread = jnp.concatenate([pull, jnp.broadcast_to(mass, (count, 128))], axis=1)
    with jax.named_scope("pull"):
        if count <= 8:
            total = spread[0:1]
            for r in range(1, count):
                total = total + swap(spread[r : r + 1], DP, r)
        else:
            placed = by_distance(spread, DP)
            total = lax.psum_scatter(placed, DP, scatter_dimension=0, tiled=True)
    positive = dot_nt(low[0:1], keys) / TEMPER
    positive = jnp.where(alive[None, :] > 0, positive, NEG_FILL)
    pos_raised = jnp.exp(positive)
    mass = total[0, width] + jnp.sum(pos_raised)
    own_pair = (jnp.arange(keys.shape[0])[None, :] == 0).astype(F32)
    weight = live / jnp.sum(alive)
    loss_part = weight * (jnp.log(mass) - positive[0, 0])
    d_positive = bf(weight * (pos_raised / mass - own_pair) / TEMPER)
    d_unit = dot_nn(d_positive, keys) + (weight / mass / TEMPER) * total[:, :width]
    unit = units[0:1]
    d_vector = inverse[0:1] * (d_unit - unit * jnp.sum(unit * d_unit, axis=-1, keepdims=True))
    return loss_part, d_vector / counts[0]


def unit_row(total, count):
    vector = total / count.astype(F32)
    inverse = lax.rsqrt(jnp.sum(vector * vector, axis=-1, keepdims=True) + NORM_EPS)
    return vector * inverse, inverse


def queue_units(counts, queue):
    def body(s, x_r, out_r):
        values = x_r[...].astype(F32)
        out_r[...] = bf(values * lax.rsqrt(jnp.sum(values * values, axis=-1, keepdims=True) + NORM_EPS))

    stores = [(queue.shape, LOW)]
    return kernel_call(body, [], [counts], [], 4 * queue.size, "queue_units", [queue], stores)[0]


def live_flag(at, live):
    return live[2 * at.core + at.chosen].astype(F32)


def unit_packet(counts, live, sums):
    width = sums[0].shape[1]

    def body(s, lv, q_r, qc_r, k_r, kc_r, out_r):
        at = here()
        query, _ = unit_row(q_r[...] + qc_r[...], count_of(at, s, 0))
        key, _ = unit_row(k_r[...] + kc_r[...], count_of(at, s, 1))
        flag = jnp.zeros((1, width), F32) + live_flag(at, lv)
        out_r[...] = bf(jnp.concatenate([query, key, flag], axis=0))

    return kernel_call(body, [((3, width), LOW)], [counts, live], sums, 8 * width, "unit_packet")[0]


def queue_scores(counts, lanes, queue):
    count = len(lanes)
    width = queue.shape[1]

    def body(s, *refs):
        lane_r, q_r, outs, key_r = refs[:count], refs[count], refs[count + 1 : -1], refs[-1]
        packets = [lane[...] for lane in lane_r]
        queries = jnp.concatenate([p[0:1] for p in packets], axis=0)
        raised = jnp.exp(dot_nt(queries, q_r[...]) / TEMPER)
        mass = jnp.sum(raised, axis=1, keepdims=True)
        pull = dot_nn(bf(raised), q_r[...])
        for i in range(count):
            outs[i][:, :width] = pull[i : i + 1]
            outs[i][:, width:] = jnp.zeros((1, 128), F32) + mass[i : i + 1]
        key_r[...] = jnp.concatenate([p[1:2] for p in packets] + [p[2:3] for p in packets], axis=0)

    outs = [((1, width + 128), F32)] * count + [((2 * count, width), LOW)]
    return kernel_call(
        body, outs, [counts], lanes, 4 * count * queue.size, "queue_scores", [queue]
    )


def loss_end(counts, live, sums, keys, pulls, squares):
    width = sums[0].shape[1]
    rows = keys[0].shape[0] // 2
    n_keys, n_pulls = len(keys), len(pulls)

    def body(s, lv, q_r, qc_r, *refs):
        at = here()
        key_r, refs = refs[:n_keys], refs[n_keys:]
        pull_r, square_r, (grad_r, row_r) = refs[:n_pulls], refs[n_pulls:-2], refs[-2:]
        unit, inverse = unit_row(q_r[...] + qc_r[...], count_of(at, s, 0))
        low = bf(unit)
        total = pull_r[0][...]
        for piece in pull_r[1:]:
            total = total + piece[...]
        every = jnp.concatenate([k[0:rows] for k in key_r], axis=0)
        alive = jnp.concatenate([k[rows:] for k in key_r], axis=0).astype(F32)
        flags = dot_nt(jnp.ones((1, 128), F32), alive[:, :128]) * (1.0 / 128)
        positive = dot_nt(low, every) / TEMPER
        positive = jnp.where(flags > 0.5, positive, NEG_FILL)
        raised = jnp.exp(positive)
        mass = total[:, width : width + 1] + jnp.sum(raised, axis=-1, keepdims=True)
        weight = live_flag(at, lv) / jnp.sum(flags, axis=-1, keepdims=True)
        own = lax.broadcasted_iota(jnp.int32, positive.shape, 1) == 0
        self_logit = jnp.sum(jnp.where(own, positive, 0.0), axis=-1, keepdims=True)
        loss = weight * (jnp.log(mass) - self_logit)
        d_positive = bf(weight * (raised / mass - own.astype(F32)) / TEMPER)
        d_unit = dot_nn(d_positive, every) + (weight / mass / TEMPER) * total[:, :width]
        d_vector = inverse * (d_unit - unit * jnp.sum(unit * d_unit, axis=-1, keepdims=True))
        grad_r[...] = d_vector / count_of(at, s, 0).astype(F32)
        lane = lax.broadcasted_iota(jnp.int32, (1, 128), 1)
        tokens = 0.5 * count_of(at, s, 0).astype(F32)
        row = jnp.where(lane == 0, 0.5 * loss, jnp.where(lane == 1, tokens, 0.0))
        at_lane = 2
        for piece in square_r:
            values = jnp.sum(piece[...], axis=-1, keepdims=True)
            for i in range(piece.shape[0]):
                row = jnp.where(lane == at_lane, values[i : i + 1], row)
                at_lane += 1
        row_r[...] = row

    outs = [((1, width), F32), ((1, 128), F32)]
    arrays = sums + keys + pulls + squares
    return kernel_call(
        body, outs, [counts, live], arrays, 4 * n_keys * rows * width, "loss_end"
    )


def small_table(counts, encoders):
    width = encoders[0][0].shape[1]
    arrays = [a for e in encoders for a in e]

    def body(s, *refs):
        out_r = refs[-1]
        for e in range(2):
            gain_r, shift_r, exp_r, in_r = refs[4 * e : 4 * e + 4]
            out_r[e, ROW_GAIN : ROW_GAIN + 2, :] = gain_r[...].astype(F32)
            out_r[e, ROW_SHIFT : ROW_SHIFT + 4, :] = shift_r[...].astype(F32)
            groups, heads = exp_r.shape[0], in_r.shape[0]
            pieces = [exp_r[i : i + 1, :].astype(F32) for i in range(groups)]
            out_r[e, ROW_EXP : ROW_EXP + 1, :] = jnp.concatenate(pieces, axis=1)
            pieces = [in_r[h, i : i + 1, :].astype(F32) for i in range(2) for h in range(heads)]
            used = sum(p.shape[1] for p in pieces)
            pieces.append(jnp.zeros((1, width - used), F32))
            out_r[e, ROW_IN : ROW_IN + 1, :] = jnp.concatenate(pieces, axis=1)

    return kernel_call(body, [((2, 8, width), F32)], [counts], arrays, 64 * width, "small_table")[0]


def per_device(
    query_embed,
    key_embed,
    crop_counts,
    pair_mask,
    negative_queue,
    online_inproj,
    online_inbias,
    online_outproj,
    online_gains,
    online_shifts,
    online_expand,
    online_expbias,
    online_contract,
    momentum_inproj,
    momentum_inbias,
    momentum_outproj,
    momentum_gains,
    momentum_shifts,
    momentum_expand,
    momentum_expbias,
    momentum_contract,
):
    section = lax.axis_index(SECTION)
    head = lax.axis_index(HEADS)
    data = lax.axis_index(DP)
    dp_count = lax.axis_size(DP)
    rows, pairs_dev, width = query_embed.shape
    pairs = pairs_dev // lax.axis_size(SECTION)
    local = online_outproj.shape[1]
    blocks = dp_count if width % (dp_count * 32) == 0 and dp_count <= 8 else 1
    few = blocks > 1
    first = section == 0
    counts = crop_counts
    chosen = jnp.where(first, head // 2, head % 2)

    def pair_of(table, axis, pair):
        return lax.dynamic_index_in_dim(table, section * pairs + pair, axis, keepdims=False)

    order = Order()
    with jax.named_scope("in"):
        raw = []
        for table in (query_embed, key_embed):
            raw.append(jnp.stack([pair_of(table, 1, chosen), pair_of(table, 1, 1 - chosen)]))
    with jax.named_scope("ag0"):
        rows_first = [gather(r, True) for r in raw]
    order.mark(raw[1])

    held = [
        [
            jnp.transpose(inproj[0], (1, 2, 0)).reshape(3 * local, width),
            outproj[0],
            expand[0],
            contract[0],
        ]
        for inproj, outproj, expand, contract in (
            (online_inproj, online_outproj, online_expand, online_contract),
            (momentum_inproj, momentum_outproj, momentum_expand, momentum_contract),
        )
    ]
    with jax.named_scope("tab"):
        small = [
            [gains[0], shifts[0], expbias[0], jnp.transpose(inbias[0], (1, 0, 2))]
            for gains, shifts, expbias, inbias in (
                (online_gains, online_shifts, online_expbias, online_inbias),
                (momentum_gains, momentum_shifts, momentum_expbias, momentum_inbias),
            )
        ]
        table = small_table(order.tie(counts), small)
        order.mark(table)
        tables = [table, over_core(table)]
        neighbour_bias = jnp.where(first, tables[1], tables[0])[1, ROW_IN : ROW_IN + 1]
    with jax.named_scope("w"):
        came_weights = [[over_core(w) for w in held[e]] for e in range(2)]
        attn_sets = [held[e][:2] + came_weights[e][:2] for e in range(2)]
        feed_sets = [held[e][2:] + came_weights[e][2:] for e in range(2)]
    span = width // dp_count
    at_row = data * span
    cut = 3 * local

    def share_of(cols, outp):
        low_part = lax.dynamic_slice_in_dim(cols, jnp.minimum(at_row, cut - span), span, 0)
        high = lax.dynamic_slice_in_dim(outp, jnp.clip(at_row - cut, 0, local - span), span, 0)
        return jnp.where(at_row < cut, low_part, high)

    def layer_share(e):
        mine = share_of(held[e][0], held[e][1])
        other = share_of(came_weights[e][0], came_weights[e][1])
        return jnp.where(first, other, mine)

    with jax.named_scope("nb"):
        shares = layer_share(1)
    neighbour = types.SimpleNamespace()
    pooled_bias = jnp.zeros((1, width), F32)
    saved = [types.SimpleNamespace(), types.SimpleNamespace()]
    squares = []
    pooled = [None, None]

    def forward(e):
        save = e == 0
        layer_in = None
        for layer in range(2):
            if layer == 0:
                rows_in = rows_first[e]
                residual = [rows_in[0], rows_in[2]]
                attn_w, theirs = attn_sets[e], pooled_bias
            else:
                with jax.named_scope("ag1"):
                    rows_in = gather(layer_in, save)
                residual = [layer_in]
                attn_w, theirs = attn_sets[e], pooled_bias
                if not save:
                    attn_w, theirs = attn_w + [neighbour.attn], neighbour.bias
            yield
            parts, kept = attn_forward(
                order.tie(counts), rows_in, tables, theirs, attn_w, layer, e, save
            )
            order.mark(parts[0])
            with jax.named_scope("rs1"):
                pieces = scatter(*parts)
            if layer == 0 and e == 1:
                with jax.named_scope("nb"):
                    neighbour.bias = hop_two(behind(neighbour_bias, order.last))
                    neighbour.share = hop_two(behind(shares, order.last))
            yield
            *square, low = norm_middle(order.tie(counts), pieces, residual, tables, layer, e, save)
            if save:
                square, low, mixed = square[0], square[1], low
            order.mark(low)
            if layer == 0 and e == 1:
                with jax.named_scope("nb"):
                    share = behind(neighbour.share, order.last)
                    neighbour.attn = lax.all_gather(share, DP, axis=0, tiled=True)
            if save:
                vars(saved[layer]).update(
                    x=rows_in, qkv=kept[0], shares=kept[1], context=kept[2], mixed=mixed
                )
                squares.append(square)
            with jax.named_scope("ag2"):
                rows_in = gather(low, True)
            yield
            parts, kept = feed_forward(
                order.tie(counts), rows_in, tables, feed_sets[e], layer, e, save
            )
            order.mark(parts[0])
            with jax.named_scope("rs2"):
                pieces = scatter(*parts)
            yield
            outs = list(norm_last(order.tie(counts), pieces, low, tables, layer, e, save))
            out = outs.pop(0)
            order.mark(out)
            if save:
                vars(saved[layer]).update(hidden=rows_in, active=kept[0], slope=kept[1], summed=outs[1])
                squares.append(outs[0])
            layer_in = out
        pooled[e] = out

    threads = [forward(0), forward(1)]
    step = 0
    queue_unit = None
    while threads:
        for thread in list(threads):
            if next(thread, 0) == 0:
                threads.remove(thread)
        step += 1
        if step == 5 and few:
            queue_unit = queue_units(order.tie(counts), negative_queue)
            order.mark(queue_unit)

    with jax.named_scope("loss"):
        if few:
            sums = [pooled[0], hop_one(pooled[0]), pooled[1], hop_one(pooled[1])]
            packet = unit_packet(order.tie(counts), pair_mask, sums)
            lanes = [packet] + [swap(packet, DP, r) for r in range(1, dp_count)]
            *spread, keys = queue_scores(counts, lanes, queue_unit)
            pulls = [spread[0]] + [swap(spread[r], DP, r) for r in range(1, dp_count)]
            keys_two = [keys, hop_two(behind(keys, pulls[1]))]
            keys_all = keys_two + [over_core(k) for k in keys_two]
            d_pool, scalar_row = loss_end(counts, pair_mask, sums[:2], keys_all, pulls, squares)
        else:
            queue = negative_queue.astype(F32)
            norm = lax.rsqrt(jnp.sum(queue * queue, axis=-1, keepdims=True) + NORM_EPS)
            live = pair_of(pair_mask, 0, chosen).astype(F32)
            own_counts = pair_of(crop_counts, 0, chosen).astype(F32)
            both = jnp.concatenate(pooled)
            loss_part, d_pool = loss_section(both, own_counts, live, bf(queue * norm))
            branch = jnp.sum(jnp.concatenate(squares), axis=1)
            scalars = jnp.concatenate([jnp.stack([0.5 * loss_part, 0.5 * own_counts[0]]), branch])
            scalar_row = jnp.zeros((1, 128), F32).at[0, : scalars.shape[0]].set(scalars)

    scalar_hops = [(HEADS, 1), (HEADS, 2), (SECTION, 1)]
    distance = 1
    while distance < dp_count:
        scalar_hops.append((DP, distance))
        distance *= 2

    def scalar_steps(mark, count):
        nonlocal scalar_row
        with jax.named_scope("sc"):
            for _ in range(min(count, len(scalar_hops))):
                axis, far = scalar_hops.pop(0)
                tied = behind(scalar_row, mark)
                scalar_row = tied + swap(tied, axis, far)
        order.mark((order.last, scalar_row))

    order = Order()
    order.mark(d_pool)
    got = {}
    waiting, summed = [], {}

    def share_grads(name, mine, other):
        waiting.append((name, mine, other))

    def add_waiting():
        for name, mine, other in waiting:
            came = over_core(order.tie(other))
            both = add_cores(order.tie(counts), mine, came)
            order.mark(both)
            summed[name] = both
        waiting.clear()

    def reduce_summed(mark):
        for name, both in summed.items():
            with jax.named_scope("rg"):
                both = behind(both, (mark, list(got.values())[-1:]))
                got[name] = lax.psum_scatter(both, DP, scatter_dimension=0, tiled=False)
        summed.clear()

    residual, pieces, rows_above = None, None, []
    plain = types.SimpleNamespace(feed=[None, None], attn=[None, None], bias=[None, None])
    attn_w, feed_w = attn_sets[0], feed_sets[0]
    for layer in (1, 0):
        kept = saved[layer]
        source = dict(pooled=d_pool) if layer == 1 else dict(residual=residual, pieces=pieces)
        low, rows_last = last_backward(
            order.tie(counts), kept.summed, tables, layer, **source
        )
        order.mark(low)
        with jax.named_scope("ag3"):
            grads = gather(low, True)
        add_waiting()
        reduce_summed(grads[1:])
        *parts, d_inner, exp_row = feed_backward(
            order.tie(counts), grads, kept.slope, feed_w, layer
        )
        order.mark(exp_row)
        with jax.named_scope("rs3"):
            pieces = scatter(*parts)
        feed_got = weight_grads(
            order.tie(counts),
            grads,
            kept.hidden,
            [kept.active, d_inner],
            exp_row,
            blocks,
            "feed_weights",
        )
        order.mark(feed_got[0])
        if few:
            share_grads(("feed", layer), *feed_got)
            scalar_steps(exp_row, 1)
        low, norm_rows = middle_backward(
            order.tie(counts), kept.mixed, tables, layer, low, pieces, rows_last, rows_above
        )
        residual = low
        order.mark(low)
        rows_above = [norm_rows]
        with jax.named_scope("ag4"):
            grads = gather(low, True)
        add_waiting()
        reduce_summed(grads[1:])
        *parts, d_project, in_rows = attn_backward(
            order.tie(counts),
            grads,
            kept.qkv,
            kept.shares,
            kept.context,
            attn_w,
            layer,
            [norm_rows] if few and layer == 0 else [],
        )
        order.mark(in_rows)
        with jax.named_scope("rs4"):
            pieces = scatter(*parts)
        attn_got = weight_grads(
            order.tie(counts),
            grads,
            kept.x,
            [kept.context, d_project],
            in_rows,
            blocks,
            "attn_weights",
        )
        order.mark(attn_got[0])
        if few:
            scalar_steps(in_rows, 1)
            if layer == 1:
                share_grads(("attn", layer), *attn_got)
        else:
            plain.feed[layer] = feed_got[0]
            plain.attn[layer] = attn_got[0]
            plain.bias[layer] = jnp.concatenate([exp_row, in_rows[0:1] + in_rows[1:2]])

    if not few:
        scalar_steps(in_rows, len(scalar_hops))

    if few:
        with jax.named_scope("lg"):
            both = add_cores(
                order.tie(counts), attn_got[0], over_core(attn_got[1]), [norm_rows] + pieces[1:]
            )
            order.mark(both)
            scalar_steps(both, len(scalar_hops))
            got["attn", 0] = lax.psum_scatter(both, DP, scatter_dimension=0, tiled=False)
        first_block = both
        d_in = bf(behind(residual, first_block).astype(F32) + scattered(*pieces))
        with jax.named_scope("dx"):
            came = hop_two(d_in[rows:])
            in_order = chosen == 0
            both = jnp.stack([jnp.where(in_order, d_in[:rows], came), jnp.where(in_order, came, d_in[:rows])])
            half_width = width // 2
            mine = lax.dynamic_slice_in_dim(both, section * half_width, half_width, 2)
            other = lax.dynamic_slice_in_dim(both, (1 - section) * half_width, half_width, 2)
            other = over_core(other)
            ordered = jnp.where(first, jnp.concatenate([mine, other]), jnp.concatenate([other, mine]))
            input_grad = jnp.transpose(ordered, (1, 0, 2))
        with jax.named_scope("fg"):
            kept_feed, sent_feed = trade_layers(
                order.tie(counts), [got["feed", 0]], [got["feed", 1]], False
            )
            contract, expand = place_feed(counts, kept_feed, over_core(sent_feed))
            order.mark(contract)
        with jax.named_scope("tg"):
            kept_attn, sent_attn, norms = trade_layers(
                order.tie(counts), [got["attn", 0]], [got["attn", 1]], True
            )
            norms, inproj, outproj = place_attn(counts, kept_attn, over_core(sent_attn), norms)
        exp_row, in_row = kept_feed[kept_feed.shape[0] - EXTRA], kept_attn[kept_attn.shape[0] - EXTRA]
    else:
        first_block = in_rows
        d_in = bf(behind(residual, first_block).astype(F32) + scattered(*pieces))
        with jax.named_scope("dx"):
            came = hop_two(d_in[rows:])
            in_order = chosen == 0
            both = jnp.stack([jnp.where(in_order, d_in[:rows], came), jnp.where(in_order, came, d_in[:rows])])
            half_width = width // 2
            mine = lax.dynamic_slice_in_dim(both, section * half_width, half_width, 2)
            other = lax.dynamic_slice_in_dim(both, (1 - section) * half_width, half_width, 2)
            other = over_core(other)
            ordered = jnp.where(first, jnp.concatenate([mine, other]), jnp.concatenate([other, mine]))
            input_grad = jnp.transpose(ordered, (1, 0, 2))
        contract, expand = reduce_plain(plain.feed, section, 1)
        attn_sum = reduce_plain(plain.attn, section, 1)[0]
        inproj = jnp.transpose(attn_sum[:, :cut].reshape(-1, 3, local), (1, 0, 2))
        outproj = jnp.transpose(attn_sum[:, cut:])
        biases = lax.psum(jnp.stack(plain.bias), (SECTION, DP))
        exp_row, in_row = jnp.where(first, biases[0], biases[1])
        norms = lax.psum(norm_rows, (HEADS, SECTION, DP))
        norms = jnp.where(first, norms[:6], norms[6:])
    loss_total = scalar_row[0, 0]
    rms_values = jnp.sqrt(scalar_row[0, 2:8].reshape(2, 3) / (scalar_row[0, 1] * width))
    piece = width // (dp_count * lax.axis_size(HEADS))
    norms = lax.dynamic_slice_in_dim(norms, (data * lax.axis_size(HEADS) + head) * piece, piece, 1)
    exp_shape, in_shape = online_expbias.shape, online_inbias.shape
    grad_expbias = lax.dynamic_slice_in_dim(
        exp_row.reshape(exp_shape), data * (exp_shape[2] // dp_count), exp_shape[2] // dp_count, 2
    )
    grad_inbias = lax.dynamic_slice_in_dim(
        in_row[: 2 * local].reshape(in_shape),
        data * (in_shape[3] // dp_count),
        in_shape[3] // dp_count,
        3,
    )
    return (
        loss_total,
        input_grad,
        jnp.transpose(inproj, (1, 0, 2))[None],
        grad_inbias,
        outproj[None],
        norms[None, 0:2],
        norms[None, 2:6],
        expand[None],
        grad_expbias,
        jnp.transpose(contract)[None],
        rms_values,
    )


def solution(mesh):
    placed = (
        P(HEADS, DP, None),
        P(HEADS, DP, None),
        P(DP, None),
        P(DP),
        P(DP, None),
        P(SECTION, None, None, HEADS),
        P(SECTION, None, HEADS, None),
        P(SECTION, HEADS, None),
        P(SECTION, None, None),
        P(SECTION, None, None),
        P(SECTION, None, HEADS),
        P(SECTION, HEADS, None),
        P(SECTION, HEADS, None),
        P(SECTION, None, None, HEADS),
        P(SECTION, None, HEADS, None),
        P(SECTION, HEADS, None),
        P(SECTION, None, None),
        P(SECTION, None, None),
        P(SECTION, None, HEADS),
        P(SECTION, HEADS, None),
        P(SECTION, HEADS, None),
    )
    return jax.shard_map(
        per_device,
        mesh=mesh,
        in_specs=placed,
        out_specs=(
            P(),
            P(HEADS, DP, SECTION),
            P(SECTION, DP, None, HEADS),
            P(SECTION, None, HEADS, DP),
            P(SECTION, HEADS, DP),
            P(SECTION, None, (DP, HEADS)),
            P(SECTION, None, (DP, HEADS)),
            P(SECTION, DP, HEADS),
            P(SECTION, HEADS, DP),
            P(SECTION, HEADS, DP),
            P(),
        ),
        check_vma=False,
    )
```

```python
import functools
import types

import jax
import jax.numpy as jnp
from jax import lax
from jax.experimental import pallas as pl
from jax.experimental.pallas import tpu as pltpu
from jax.sharding import PartitionSpec as P

TEMPER = 0.05
NORM_EPS = 1e-06
NEG_FILL = -1000000000.0
F32 = jnp.float32
LOW = jnp.bfloat16
HEADS, SECTION, DP = "heads", "section", "dp"
VMEM_SPARE = 6 * 1024 * 1024
EXTRA = 16

ROW_GAIN = 0
ROW_SHIFT = 2
ROW_EXP = 6
ROW_IN = 7


def dot_nn(a, b):
    return lax.dot_general(a, b, (((1,), (0,)), ((), ())), preferred_element_type=F32)


def dot_nt(a, b):
    return lax.dot_general(a, b, (((1,), (1,)), ((), ())), preferred_element_type=F32)


def dot_tn(a, b):
    return lax.dot_general(a, b, (((0,), (0,)), ((), ())), preferred_element_type=F32)


def bytes_of(shape, dtype):
    return functools.reduce(lambda x, y: x * y, shape, 1) * jnp.dtype(dtype).itemsize


class Loaded:
    def __init__(self, source, buffer, sem):
        self.copy = pltpu.make_async_copy(source, buffer, sem)
        self.copy.start()
        self.buffer = buffer
        self.shape = buffer.shape
        self.waiting = True

    def ready(self):
        if self.waiting:
            self.copy.wait()
            self.waiting = False
        return self.buffer

    def __getitem__(self, index):
        return self.ready()[index]

    @property
    def at(self):
        return self.ready().at


class Stored:
    def __init__(self, target, buffer, sems):
        self.target, self.buffer, self.sems = target, buffer, sems
        self.shape, self.dtype = buffer.shape, buffer.dtype
        self.copies = []

    def __setitem__(self, index, value):
        self.buffer[index] = value

    def send(self, start=0, size=None):
        run = pl.ds(start, self.shape[0] if size is None else size)
        copy = pltpu.make_async_copy(
            self.buffer.at[run], self.target.at[run], self.sems.at[len(self.copies)]
        )
        copy.start()
        self.copies.append(copy)

    def finish(self):
        for copy in self.copies:
            copy.wait()


def kernel_call(
    body, outs, scalars, arrays, flops, name, loads=(), stores=(), distant=(), weights=0
):
    side = distant[-1].shape[-1] if weights else 0
    buffers = [(a.shape, a.dtype) for a in loads] + list(stores)
    if weights:
        buffers.append(((weights, side, side), LOW))
    held = sum(bytes_of(*x) for x in [(a.shape, a.dtype) for a in arrays] + list(outs) + buffers)
    sems = [pltpu.SemaphoreType.DMA((max(1, len(loads) + 2 * len(stores)),))]
    if weights:
        sems.append(pltpu.SemaphoreType.DMA((2 * weights,)))
    counts = [len(scalars), len(arrays), len(loads), len(distant), len(outs), len(stores)]

    def whole(*refs):
        groups = []
        for count in counts + [len(loads), len(stores)]:
            groups.append(list(refs[:count]))
            refs = refs[count:]
        scal, near, load_r, far, out_r, store_r, load_b, store_b = groups
        extra = list(refs[:1]) if weights else []
        sem = refs[1] if weights else refs[0]
        loaded = [Loaded(a, b, sem.at[i]) for i, (a, b) in enumerate(zip(load_r, load_b))]
        base = len(loaded)
        stored = [
            Stored(a, b, sem.at[pl.ds(base + 2 * i, 2)]) for i, (a, b) in enumerate(zip(store_r, store_b))
        ]
        if weights:
            extra.append(refs[2])
        body(*scal, *near, *loaded, *far, *out_r, *stored, *extra)
        for item in loaded:
            item.ready()
        for item in stored:
            if not item.copies:
                item.send()
        for item in stored:
            item.finish()

    hbm = pl.BlockSpec(memory_space=pltpu.HBM)
    vmem = pl.BlockSpec(memory_space=pltpu.VMEM)
    in_specs = [pl.BlockSpec(memory_space=pltpu.SMEM)] * len(scalars)
    in_specs += [vmem] * len(arrays) + [hbm] * (len(loads) + len(distant))
    apart = [pltpu.with_memory_space_constraint(d, pltpu.HBM) for d in [*loads, *distant]]
    return pl.pallas_call(
        whole,
        out_shape=[jax.ShapeDtypeStruct(s, d) for s, d in outs]
        + [pltpu.HBM(s, d) for s, d in stores],
        in_specs=in_specs,
        out_specs=[vmem] * len(outs) + [hbm] * len(stores),
        scratch_shapes=[pltpu.VMEM(s, d) for s, d in buffers] + sems,
        compiler_params=pltpu.CompilerParams(vmem_limit_bytes=held + VMEM_SPARE),
        cost_estimate=pl.CostEstimate(flops=flops, bytes_accessed=held, transcendentals=0),
        name=name,
    )(*scalars, *arrays, *apart)


def here():
    head, core, data = [lax.axis_index(a) for a in (HEADS, SECTION, DP)]
    near = jnp.where(core == 0, 1, 2)
    chosen = jnp.where(core == 0, head // 2, head % 2)
    return types.SimpleNamespace(head=head, core=core, data=data, near=near, chosen=chosen)


def count_of(at, counts, encoder, other=0):
    return counts[2 * at.core + jnp.bitwise_xor(at.chosen, other), encoder]


def table_row(at, tables, layer, encoder, row):
    held, came = [t[encoder, row : row + 1, :] for t in tables]
    return jnp.where(at.core == layer, held, came)


def start_fetch(at, layer, held, arrived, target, sem):
    @pl.when(at.core == layer)
    def _():
        pltpu.make_async_copy(held, target, sem).start()

    @pl.when(at.core != layer)
    def _():
        pltpu.make_async_copy(arrived, target, sem).start()

    return pltpu.make_async_copy(held, target, sem)


def start_copy(source, target, sem):
    copy = pltpu.make_async_copy(source, target, sem)
    copy.start()
    return copy


def fetch_attn(at, layer, encoder, refs, scratch, sems):
    cols, outp, cols_too, outp_too = refs[:4]
    cut = cols.shape[0]
    waits = [
        start_fetch(at, layer, cols, cols_too, scratch.at[0, pl.ds(0, cut)], sems.at[0]),
        start_fetch(at, layer, outp, outp_too, scratch.at[0, pl.ds(cut, outp.shape[0])], sems.at[1]),
    ]
    if len(refs) > 4:
        waits.append(start_copy(refs[4], scratch.at[1], sems.at[2]))
    return waits


def fetch_feed(at, layer, refs, scratch, sems):
    exp, con, exp_too, con_too = refs
    return [
        start_fetch(at, layer, exp, exp_too, scratch.at[0], sems.at[0]),
        start_fetch(at, layer, con, con_too, scratch.at[1], sems.at[1]),
    ]


def swap(value, axis, distance):
    count = lax.axis_size(axis)
    return lax.ppermute(value, axis, [(i, i ^ distance) for i in range(count)])


def hop(value, first_core, second_core):
    count = lax.axis_size(HEADS)
    route = [(i, i ^ first_core) for i in range(count)]
    route += [(count + i, count + (i ^ second_core)) for i in range(count)]
    return lax.ppermute(value, (SECTION, HEADS), route)


def hop_one(value):
    return hop(value, 1, 2)


def hop_two(value):
    return hop(value, 2, 1)


def hop_both(value):
    return hop(value, 3, 3)


def over_core(value):
    return swap(value, SECTION, 1)


def behind(value, mark):
    return lax.optimization_barrier((value, mark))[0]


class Order:
    def __init__(self):
        self.last = None

    def tie(self, value):
        return value if self.last is None else behind(value, self.last)

    def mark(self, value):
        self.last = value


def bf(value):
    return value.astype(LOW)


def norm_parts(values):
    mean = jnp.mean(values, axis=-1, keepdims=True)
    center = values - mean
    spread = jnp.mean(center * center, axis=-1, keepdims=True)
    rstd = lax.rsqrt(spread + NORM_EPS)
    return center * rstd, rstd


def row_position(at, rows, shape, other):
    block_rows = rows // 2
    lane = lax.broadcasted_iota(jnp.int32, shape, 0 if shape[1] == 1 else 1)
    slot = lane // block_rows
    far = 3 - at.near
    block = jnp.bitwise_xor(jnp.bitwise_xor(at.head, other * far), (slot & 1) * far)
    block = jnp.bitwise_xor(block, (slot // 2) * at.near)
    return block * block_rows + lane - slot * block_rows


def row_keep(at, counts, encoder, rows):
    return row_position(at, rows, (rows, 1), 0) < count_of(at, counts, encoder)


def key_keep(at, counts, encoder, rows, other):
    return row_position(at, rows, (1, 2 * rows), other) < count_of(at, counts, encoder, other)


def row_groups(sources):
    if len(sources) == 2:
        return [list(sources)] * 2
    if len(sources[0].shape) == 2:
        own, one, two, far = sources
        return [[own, one], [two, far]]
    own, one, two, far = sources
    return [
        [own.at[0], two.at[1], one.at[0], far.at[1]],
        [two.at[0], own.at[1], far.at[0], one.at[1]],
    ]


def stack_rows(group):
    return jnp.concatenate([piece[...] for piece in group], axis=0)


def put_rows(targets, outs):
    if len(targets) == 4:
        half = outs[0].shape[0] // 2
        values = [outs[0][:half], outs[0][half:], outs[1][:half], outs[1][half:]]
    else:
        total = outs[0] + outs[1]
        half = total.shape[0] // 2
        values = [total[:half], total[half:]]
    for target, value in zip(targets, values):
        target[...] = value.astype(target.dtype)


def parts_shapes(rows, width, count):
    return [((rows, width), F32)] + [((rows, width), LOW)] * (count - 1)


def rows_of(sources):
    shape = sources[0].shape
    return (2 * shape[1], shape[2]) if len(shape) == 3 else shape


def attn_forward(counts, sources, tables, theirs, weights, layer, encoder, save):
    wide = len(sources) == 4
    rows, width = rows_of(sources)
    local = width // 4
    heads = local // 64
    full = 2 * rows
    count = len(sources)

    def body(s, *refs):
        at = here()
        tb, th_r, source, refs = refs[:2], refs[2], refs[3 : 3 + count], refs[3 + count :]
        w_refs, refs = refs[: len(weights)], refs[len(weights) :]
        targets, kept, (w_r, sems) = refs[:count], refs[count:-2], refs[-2:]
        waits = fetch_attn(at, layer, encoder, w_refs, w_r, sems)
        groups = row_groups(source)
        outs = []
        for unit in range(2):
            side = 0 if wide else unit
            rows_in = stack_rows(groups[unit])
            keep = key_keep(at, s, encoder, rows, unit if wide else 0)
            bias = th_r[...] if side else table_row(at, tb, layer, encoder, ROW_IN)
            if unit == 0:
                waits[0].wait()
            elif not wide:
                waits[2].wait()
            project = dot_nt(rows_in, w_r[side, : 3 * local, :])
            q = bf(project[:, :local] + bias[:, :local])
            k = bf(project[:, local : 2 * local])
            v = bf(project[:, 2 * local :] + bias[:, local : 2 * local])
            if save:
                kept[0][unit, :, :local] = q
                kept[0][unit, :, local : 2 * local] = k
                kept[0][unit, :, 2 * local :] = v
                kept[0].send(unit, 1)
            pieces = []
            for h in range(heads):
                cut = slice(64 * h, 64 * h + 64)
                scores = jnp.where(keep, dot_nt(q[:, cut] * 0.125, k[:, cut]), NEG_FILL)
                raised = jnp.exp(scores - jnp.max(scores, axis=-1, keepdims=True))
                shares = bf(raised / jnp.sum(raised, axis=-1, keepdims=True))
                if save:
                    kept[1][unit * heads + h] = shares
                pieces.append(bf(dot_nn(shares, v[:, cut])))
            context = jnp.concatenate(pieces, axis=1)
            if save:
                kept[2][unit] = context
                kept[1].send(unit * heads, heads)
                kept[2].send(unit, 1)
            if unit == 0:
                waits[1].wait()
            outs.append(dot_nn(context, w_r[side, 3 * local :, :]))
        put_rows(targets, outs)

    outs, stores = parts_shapes(rows, width, count), []
    if save:
        stores = [
            ((2, full, 3 * local), LOW),
            ((2 * heads, full, full), LOW),
            ((2, full, local), LOW),
        ]
    flops = 4 * full * (4 * local * width + 2 * local * full)
    got = kernel_call(
        body,
        outs,
        [counts],
        tables + [theirs] + sources,
        flops,
        "attn_forward",
        [],
        stores,
        weights,
        1 if wide else 2,
    )
    return got[:count], got[count:]


def feed_forward(counts, sources, tables, weights, layer, encoder, save):
    rows, width = rows_of(sources)
    units = weights[0].shape[1]
    full = 2 * rows
    count = len(sources)

    def body(s, *refs):
        at = here()
        tb, source, refs = refs[:2], refs[2 : 2 + count], refs[2 + count :]
        w_refs, refs = refs[: len(weights)], refs[len(weights) :]
        targets, kept, (w_r, sems) = refs[:count], refs[count:-2], refs[-2:]
        waits = fetch_feed(at, layer, w_refs, w_r, sems)
        groups = row_groups(source)
        bias = table_row(at, tb, layer, encoder, ROW_EXP)
        outs = []
        for unit in range(2):
            rows_in = stack_rows(groups[unit])
            if unit == 0:
                waits[0].wait()
            inner = dot_nn(rows_in, w_r[0]) + bias
            phi = 0.5 * (1.0 + lax.erf(inner * (0.5**0.5)))
            active = bf(inner * phi)
            if save:
                density = jnp.exp(-0.5 * inner * inner) * 0.3989422804014327
                kept[0][unit] = active
                kept[1][unit] = bf(phi + inner * density)
                kept[0].send(unit, 1)
                kept[1].send(unit, 1)
            if unit == 0:
                waits[1].wait()
            outs.append(dot_nn(active, w_r[1]))
        put_rows(targets, outs)

    outs, stores = parts_shapes(rows, width, count), []
    if save:
        stores = [((2, full, units), LOW), ((2, full, units), LOW)]
    flops = 8 * full * width * units
    near = tables + sources
    got = kernel_call(body, outs, [counts], near, flops, "feed_forward", [], stores, weights, 2)
    return got[:count], got[count:]


def masked_squares(at, counts, encoder, values, rows):
    return column_sum(jnp.where(row_keep(at, counts, encoder, rows), values * values, 0.0))


def norm_middle(counts, pieces, layer_in, tables, layer, encoder, save):
    rows, width = pieces[0].shape
    count, inputs = len(pieces), len(layer_in)

    def body(s, *refs):
        at = here()
        tb, added, refs = refs[:2], refs[2 : 2 + count], refs[2 + count :]
        x_refs, refs = refs[:inputs], refs[inputs:]
        (square_r, low_r, mixed_r) = refs if save else (None, refs[0], None)
        if inputs == 1:
            rows_in = x_refs[0][...]
        else:
            rows_in = jnp.concatenate([x_refs[0][0], x_refs[1][1]], axis=0)
        attn = scattered(*added) + table_row(at, tb, layer, encoder, ROW_SHIFT)
        mixed = rows_in.astype(F32) + attn
        if save:
            mixed_r[...] = mixed
            mixed_r.send()
        xhat, _ = norm_parts(mixed)
        gain = table_row(at, tb, layer, encoder, ROW_GAIN)
        low_r[...] = bf(xhat * gain + table_row(at, tb, layer, encoder, ROW_SHIFT + 1))
        if save:
            square_r[...] = masked_squares(at, s, encoder, attn, rows)

    outs, stores = [((rows, width), LOW)], []
    if save:
        outs, stores = [((1, width), F32)] + outs, [((rows, width), F32)]
    near = tables + pieces + layer_in
    return kernel_call(body, outs, [counts], near, 20 * rows * width, "norm_middle", [], stores)


def norm_last(counts, pieces, hidden, tables, layer, encoder, save):
    rows, width = hidden.shape
    count = len(pieces)
    pool = layer == 1

    def body(s, *refs):
        at = here()
        tb, added, h_r, refs = refs[:2], refs[2 : 2 + count], refs[2 + count], list(refs[3 + count :])
        out_r = refs.pop(0)
        square_r = refs.pop(0) if save else None
        feed = scattered(*added) + table_row(at, tb, layer, encoder, ROW_SHIFT + 2)
        summed = h_r[...].astype(F32) + feed
        if save:
            refs[0][...] = summed
            refs[0].send()
        xhat, _ = norm_parts(summed)
        gain = table_row(at, tb, layer, encoder, ROW_GAIN + 1)
        out = xhat * gain + table_row(at, tb, layer, encoder, ROW_SHIFT + 3)
        if pool:
            out_r[...] = column_sum(jnp.where(row_keep(at, s, encoder, rows), out, 0.0))
        else:
            out_r[...] = bf(out)
        if save:
            square_r[0:1, :] = masked_squares(at, s, encoder, feed, rows)
            square_r[1:2, :] = masked_squares(at, s, encoder, out, rows)

    outs, stores = [((1, width), F32) if pool else ((rows, width), LOW)], []
    if save:
        outs, stores = outs + [((2, width), F32)], [((rows, width), F32)]
    near = tables + pieces + [hidden]
    return kernel_call(body, outs, [counts], near, 20 * rows * width, "norm_last", [], stores)


def gather(own, wide):
    hops = (hop_one, hop_two, hop_both) if wide else (hop_one,)
    return [own] + [move(own) for move in hops]


def scatter(part, *others):
    hops = (hop_one, hop_two, hop_both)
    return [part] + [move(value) for move, value in zip(hops, others)]


def scattered(part, *others):
    total = part[...]
    for value in others:
        total = total + value[: part.shape[0], :].astype(F32)
    return total


def norm_backward(values, grad, gain_row):
    xhat, rstd = norm_parts(values)
    scaled = grad * gain_row
    d_values = rstd * (
        scaled
        - jnp.mean(scaled, axis=-1, keepdims=True)
        - xhat * jnp.mean(scaled * xhat, axis=-1, keepdims=True)
    )
    return d_values, jnp.sum(grad * xhat, axis=0, keepdims=True)


def column_sum(values):
    return jnp.sum(values, axis=0, keepdims=True)


def norm_gradient(y_r, grad, gain, low_r):
    d_values, d_gain = norm_backward(y_r[...], grad, gain)
    low_r[...] = bf(d_values)
    return d_gain, column_sum(grad), column_sum(d_values)


def last_backward(counts, summed, tables, layer, pooled=None, residual=None, pieces=None):
    rows, width = summed.shape
    near = [pooled] if pooled is not None else [residual] + pieces[1:]
    loads = [summed] if pooled is not None else [summed, pieces[0]]
    inputs = len(near)

    def body(s, held_r, came_r, *rest):
        at = here()
        near_r, (y_r, *part_r), (rows_r, low_r) = rest[:inputs], rest[inputs:-2], rest[-2:]
        if pooled is not None:
            grad = jnp.where(row_keep(at, s, 0, rows), near_r[0][...], 0.0)
        else:
            grad = bf(scattered(part_r[0], *near_r)).astype(F32)
        gain = table_row(at, (held_r, came_r), layer, 0, ROW_GAIN + 1)
        for i, row in enumerate(norm_gradient(y_r, grad, gain, low_r)):
            rows_r[i : i + 1, :] = row

    outs = [((3, width), F32), ((rows, width), LOW)]
    got = kernel_call(
        body, outs, [counts], tables + near, 30 * summed.size, "last_backward", loads
    )
    return got[1], got[0]


def middle_backward(counts, mixed, tables, layer, residual, pieces, last_rows, above, ride):
    rows, width = mixed.shape
    known = [last_rows] + above
    total = 6 + 6 * len(above)

    def body(s, held_r, came_r, *rest):
        at = here()
        last_r, above_r, rest = rest[0], rest[1 : len(known)], rest[len(known) :]
        near_r, (y_r, part_r, rows_r, low_r) = rest[:-4], rest[-4:]
        grad = scattered(part_r, *near_r)
        gain = table_row(at, (held_r, came_r), layer, 0, ROW_GAIN)
        d_gain, in_sum, out_sum = norm_gradient(y_r, grad, gain, low_r.at[pl.ds(0, rows)])
        last = [last_r[i : i + 1, :] for i in range(3)]
        for i, row in enumerate((d_gain, last[0], out_sum, in_sum, last[2], last[1])):
            rows_r[i : i + 1, :] = row
        if above_r:
            rows_r[6:, :] = above_r[0][...]
        if ride:
            spare = jnp.zeros((EXTRA - total, width), F32)
            low_r[rows:, :] = bf(jnp.concatenate([rows_r[...], spare], axis=0))

    outs = [((total, width), F32), ((rows + EXTRA * ride, width), LOW)]
    near = tables + known + [residual] + pieces[1:]
    loads = [mixed, pieces[0]]
    got = kernel_call(body, outs, [counts], near, 30 * mixed.size, "middle_backward", loads)
    return got[1], got[0]


def feed_backward(counts, grads, slope, weights, layer):
    full, units = slope.shape[1:]
    rows, width = grads[0].shape
    count = len(grads)

    def body(s, *refs):
        source, sl_r, refs = refs[:count], refs[count], refs[count + 1 :]
        w_refs, refs = refs[: len(weights)], refs[len(weights) :]
        others, (bias_r, part, dinner_r, w_r, sems) = refs[: count - 1], refs[count - 1 :]
        targets = [part, *others]
        waits = fetch_feed(here(), layer, w_refs, w_r, sems)
        groups = row_groups(source)
        outs = []
        total = jnp.zeros((1, units), F32)
        for unit in range(2):
            if unit == 0:
                waits[1].wait()
            d_inner = dot_nt(stack_rows(groups[unit]), w_r[1]) * sl_r[unit].astype(F32)
            total = total + column_sum(d_inner)
            low = bf(d_inner)
            dinner_r[unit] = low
            dinner_r.send(unit, 1)
            if unit == 0:
                waits[0].wait()
            outs.append(dot_nt(low, w_r[0]))
        bias_r[...] = total
        put_rows(targets, outs)

    part, *outs = parts_shapes(rows, width, count)
    outs, stores = outs + [((1, units), F32)], [part, ((2, full, units), LOW)]
    flops = 8 * full * width * units
    got = kernel_call(
        body, outs, [counts], grads, flops, "feed_backward", [slope], stores, weights, 2
    )
    return [got[count], *got[: count - 1], got[count + 1], got[count - 1]]


def attn_backward(counts, grads, qkv, shares, context, weights, layer):
    wide = len(grads) == 4
    full, triple = qkv.shape[1:]
    local = triple // 3
    heads = local // 64
    rows, width = full // 2, grads[0].shape[1]
    count = len(grads)

    def body(s, *refs):
        source, refs = [g.at[pl.ds(0, rows)] for g in refs[:count]], refs[count:]
        (qkv_r, sh_r, cx_r), refs = refs[:3], refs[3:]
        w_refs, refs = refs[: len(weights)], refs[len(weights) :]
        others, (bias_r, part, dproj_r, w_r, sems) = refs[: count - 1], refs[count - 1 :]
        targets = [part, *others]
        waits = fetch_attn(here(), layer, 0, w_refs, w_r, sems)
        groups = row_groups(source)
        bias_r[...] = jnp.zeros((2, width), F32)
        outs = []
        for unit in range(2):
            side = 0 if wide else unit
            if unit == 0:
                waits[1].wait()
            elif not wide:
                waits[2].wait()
            d_context = bf(dot_nt(stack_rows(groups[unit]), w_r[side, triple:, :]))
            q = qkv_r[unit, :, :local]
            k = qkv_r[unit, :, local : 2 * local]
            v = qkv_r[unit, :, 2 * local :]
            weighted = d_context.astype(F32) * cx_r[unit].astype(F32)
            dqs, dks, dvs = [], [], []
            for h in range(heads):
                cut = slice(64 * h, 64 * h + 64)
                share = sh_r[unit * heads + h]
                dc = d_context[:, cut]
                dvs.append(dot_tn(share, dc))
                drop = jnp.sum(weighted[:, cut], axis=-1, keepdims=True)
                d_scores = bf(share.astype(F32) * (dot_nt(dc, v[:, cut]) - drop))
                dqs.append(dot_nn(d_scores, k[:, cut]) * 0.125)
                dks.append(dot_tn(d_scores, q[:, cut]) * 0.125)
            dq = jnp.concatenate(dqs, axis=1)
            dk = jnp.concatenate(dks, axis=1)
            dv = jnp.concatenate(dvs, axis=1)
            bias_r[unit : unit + 1, :local] = column_sum(dq)
            bias_r[unit : unit + 1, local : 2 * local] = column_sum(dv)
            d_project = bf(jnp.concatenate([dq, dk, dv], axis=1))
            dproj_r[unit] = d_project
            dproj_r.send(unit, 1)
            if unit == 0:
                waits[0].wait()
            outs.append(dot_nn(d_project, w_r[side, :triple, :]))
        put_rows(targets, outs)

    part = ((rows, width), F32)
    outs = [((rows, width), LOW)] * (count - 1)
    outs, stores = outs + [((2, width), F32)], [part, ((2, full, triple), LOW)]
    flops = 4 * full * (4 * local * width + 4 * local * full)
    loads = [qkv, shares, context]
    side = 1 if wide else 2
    got = kernel_call(
        body, outs, [counts], grads, flops, "attn_backward", loads, stores, weights, side
    )
    return [got[count], *got[: count - 1], got[count + 1], got[count - 1]]


def put_blocks(at, out_ref, parts, extra, blocks, other):
    if extra.shape[0] < EXTRA:
        extra = jnp.concatenate([extra, jnp.zeros((EXTRA - extra.shape[0], extra.shape[1]), F32)], axis=0)
    extra = bf(extra)
    span = parts[0].shape[0] // blocks
    half = span // 2
    wanted = jnp.bitwise_xor(at.core, other)
    for block in range(blocks):
        for i, value in enumerate(parts):
            halves = [bf(value[block * span + j * half : block * span + (j + 1) * half]) for j in range(2)]
            out_ref[block, i * half : (i + 1) * half, :] = jnp.where(wanted == 0, *halves)
        out_ref[block, len(parts) * half :, :] = extra


def weight_grads(counts, grads, inputs, pairs, bias, blocks, name):
    count = len(grads)
    width = grads[0].shape[-1]
    attention = name == "attn_weights"
    columns = sum(p.shape[2] for p in pairs) if attention else pairs[0].shape[2]
    parts_count = 1 if attention else 2

    def body(s, *refs):
        at = here()
        bias_r, g_refs, refs = refs[0], refs[1 : 1 + count], refs[1 + count :]
        x_refs, (o_r, d_r), targets = refs[:count], refs[count : count + 2], refs[count + 2 :]
        half = pairs[0].shape[1] // 2
        g_rows = [stack_rows(g) for g in row_groups([g.at[pl.ds(0, half)] for g in g_refs])]
        back = dot_tn(g_rows[0], o_r[0]) + dot_tn(g_rows[1], o_r[1])
        x_rows = [stack_rows(x) for x in row_groups(x_refs)]
        ahead = dot_tn(x_rows[0], d_r[0]) + dot_tn(x_rows[1], d_r[1])
        row = bias_r[0:1, :] + bias_r[1:2, :] if bias_r.shape[0] == 2 else bias_r[...]
        parts = [jnp.concatenate([ahead, back], axis=1)] if attention else [back, ahead]
        if blocks > 1:
            put_blocks(at, targets[0], parts, row, blocks, 1)
            put_blocks(at, targets[1], parts, row, blocks, 0)
        else:
            for i, part in enumerate(parts):
                targets[0][i] = bf(part)

    if blocks > 1:
        shape = (blocks, parts_count * (width // blocks // 2) + EXTRA, columns)
        outs, stores = [(shape, LOW)], [(shape, LOW)]
    else:
        outs, stores = [((parts_count, width, columns), LOW)], []
    flops = sum(4 * p.shape[1] * width * p.shape[2] for p in pairs)
    loads = grads + inputs + pairs
    got = kernel_call(body, outs, [counts], [bias], flops, name, loads, stores)
    return [got[1], got[0]] if blocks > 1 else got


def add_cores(counts, mine, came, norms=(), arrived=()):
    blocks, rows = mine.shape[:2]
    start = rows - EXTRA

    def body(s, *refs):
        norm_r, (c_r, m_r, *arrived_r, out_r) = refs[: len(norms)], refs[len(norms) :]
        for block in range(blocks):
            total = m_r[block].astype(F32) + c_r[block].astype(F32)
            if norms:
                summed = norm_r[0][...]
                for piece in arrived_r:
                    rows_there = piece[piece.shape[0] - EXTRA :, :].astype(F32)
                    summed = summed + rows_there[: summed.shape[0]]
                spare = jnp.zeros((EXTRA - 1 - summed.shape[0], summed.shape[1]), F32)
                total = jnp.concatenate([total[: start + 1], summed, spare], axis=0)
            out_r[block] = bf(total)
            if block % 2:
                out_r.send(block - 1, 2)

    stores = [(mine.shape, LOW)]
    near, loads = [*norms, came], [mine, *arrived]
    return kernel_call(body, [], [counts], near, mine.size, "add_cores", loads, stores)[0]


def in_core_order(at, refs, start, size):
    run = slice(start, start + size)
    mine = jnp.where(at.core == 0, refs[0][run, :], refs[2][run, :]).astype(F32)
    other = jnp.where(at.core == 0, refs[1][run, :], refs[3][run, :]).astype(F32)
    own = at.core == 0
    return jnp.concatenate([jnp.where(own, mine, other), jnp.where(own, other, mine)], axis=0)


def own_row(at, refs, row):
    return jnp.where(at.core == 0, refs[0][row : row + 1, :], refs[2][row : row + 1, :]).astype(F32)


def place_feed(counts, shares):
    rows, width = shares[0].shape
    part = (rows - EXTRA) // 2

    def body(s, *refs):
        at = here()
        refs, (row_r, con_r, exp_r) = refs[:4], refs[4:]
        con_r[...] = in_core_order(at, refs, 0, part)
        con_r.send()
        exp_r[...] = in_core_order(at, refs, part, part)
        row_r[...] = own_row(at, refs, 2 * part)

    outs, stores = [((1, width), F32)], [((2 * part, width), F32)] * 2
    return kernel_call(
        body, outs, [counts], [], 4 * rows * width, "place_feed", shares, stores
    )


def place_attn(counts, shares):
    rows, width = shares[0].shape
    part = rows - EXTRA
    local = width // 4

    def body(s, *refs):
        at = here()
        refs, (row_r, norm_r, in_r, out_r) = refs[:4], refs[4:]
        both = in_core_order(at, refs, 0, part)
        for i in range(3):
            in_r[i] = both[:, i * local : (i + 1) * local]
        in_r.send()
        out_r[...] = both[:, 3 * local :].T
        row_r[...] = own_row(at, refs, part)
        norms = refs[0][part + 1 : part + 13, :].astype(F32) + refs[1][part + 1 : part + 13, :].astype(F32)
        norm_r[...] = jnp.where(at.core == 0, norms[:6], norms[6:])

    outs = [((1, width), F32), ((6, width), F32)]
    stores = [((3, 2 * part, local), F32), ((local, 2 * part), F32)]
    return kernel_call(
        body, outs, [counts], [], 4 * rows * width, "place_attn", shares, stores
    )


def reduce_plain(layers, section, axis):
    mine = jnp.where(section == 0, layers[0], layers[1]).astype(F32)
    other = over_core(jnp.where(section == 0, layers[1], layers[0]))
    low = bf(mine + other.astype(F32))
    return lax.psum_scatter(low, DP, scatter_dimension=axis, tiled=True).astype(F32)


def summed_over(value, axis):
    count = lax.axis_size(axis)
    distance = 1
    while distance < count:
        value = value + swap(value, axis, distance)
        distance *= 2
    return value


def by_distance(entries, axis):
    count = entries.shape[0]
    order = jnp.bitwise_xor(jnp.arange(count), lax.axis_index(axis))
    chosen = (order[:, None] == jnp.arange(count)[None, :]).astype(entries.dtype)
    flat = jnp.dot(chosen, entries.reshape(count, -1), precision=lax.Precision.HIGHEST)
    return flat.astype(entries.dtype).reshape(entries.shape)


def loss_section(pooled, counts, live, queue_unit):
    count = lax.axis_size(DP)
    width = pooled.shape[-1]
    with jax.named_scope("pool"):
        pooled = pooled + hop_one(pooled)
    vectors = pooled / counts[:, None]
    inverse = lax.rsqrt(jnp.sum(vectors * vectors, axis=-1, keepdims=True) + NORM_EPS)
    units = vectors * inverse
    low = bf(units)
    flags = jnp.broadcast_to(bf(live), (1, width))
    packet = jnp.concatenate([low, flags], axis=0)
    with jax.named_scope("keys"):
        if count <= 8:
            lanes = jnp.stack([packet] + [swap(packet, DP, r) for r in range(1, count)])
        else:
            lanes = by_distance(lax.all_gather(packet, DP, axis=0), DP)
    queries = lanes[:, 0]
    with jax.named_scope("keys"):
        every = jnp.stack([lanes[:, 1:], hop_two(lanes[:, 1:])])
        every = jnp.stack([every, over_core(every)]).reshape(4 * count, 2, width)
    keys, alive = every[:, 0], every[:, 1, 0].astype(F32)
    raised = jnp.exp(dot_nt(queries, queue_unit) / TEMPER)
    mass = jnp.sum(raised, axis=1, keepdims=True)
    pull = dot_nn(bf(raised), queue_unit)
    spread = jnp.concatenate([pull, jnp.broadcast_to(mass, (count, 128))], axis=1)
    with jax.named_scope("pull"):
        if count <= 8:
            total = spread[0:1]
            for r in range(1, count):
                total = total + swap(spread[r : r + 1], DP, r)
        else:
            placed = by_distance(spread, DP)
            total = lax.psum_scatter(placed, DP, scatter_dimension=0, tiled=True)
    positive = dot_nt(low[0:1], keys) / TEMPER
    positive = jnp.where(alive[None, :] > 0, positive, NEG_FILL)
    pos_raised = jnp.exp(positive)
    mass = total[0, width] + jnp.sum(pos_raised)
    own_pair = (jnp.arange(keys.shape[0])[None, :] == 0).astype(F32)
    weight = live / jnp.sum(alive)
    loss_part = weight * (jnp.log(mass) - positive[0, 0])
    d_positive = bf(weight * (pos_raised / mass - own_pair) / TEMPER)
    d_unit = dot_nn(d_positive, keys) + (weight / mass / TEMPER) * total[:, :width]
    unit = units[0:1]
    d_vector = inverse[0:1] * (d_unit - unit * jnp.sum(unit * d_unit, axis=-1, keepdims=True))
    return loss_part, d_vector / counts[0]


def unit_row(total, count):
    vector = total / count.astype(F32)
    inverse = lax.rsqrt(jnp.sum(vector * vector, axis=-1, keepdims=True) + NORM_EPS)
    return vector * inverse, inverse


def queue_units(counts, queue):
    def body(s, x_r, out_r):
        values = x_r[...].astype(F32)
        out_r[...] = bf(values * lax.rsqrt(jnp.sum(values * values, axis=-1, keepdims=True) + NORM_EPS))

    stores = [(queue.shape, LOW)]
    return kernel_call(body, [], [counts], [], 4 * queue.size, "queue_units", [queue], stores)[0]


def live_flag(at, live):
    return live[2 * at.core + at.chosen].astype(F32)


def unit_packet(counts, live, sums):
    width = sums[0].shape[1]

    def body(s, lv, q_r, qc_r, k_r, kc_r, out_r):
        at = here()
        query, _ = unit_row(q_r[...] + qc_r[...], count_of(at, s, 0))
        key, _ = unit_row(k_r[...] + kc_r[...], count_of(at, s, 1))
        flag = jnp.zeros((1, width), F32) + live_flag(at, lv)
        out_r[...] = bf(jnp.concatenate([query, key, flag], axis=0))

    return kernel_call(body, [((3, width), LOW)], [counts, live], sums, 8 * width, "unit_packet")[0]


def queue_scores(counts, lanes, queue):
    count = len(lanes)
    width = queue.shape[1]

    def body(s, *refs):
        lane_r, q_r, outs, key_r = refs[:count], refs[count], refs[count + 1 : -1], refs[-1]
        packets = [lane[...] for lane in lane_r]
        queries = jnp.concatenate([p[0:1] for p in packets], axis=0)
        raised = jnp.exp(dot_nt(queries, q_r[...]) / TEMPER)
        mass = jnp.sum(raised, axis=1, keepdims=True)
        pull = dot_nn(bf(raised), q_r[...])
        for i in range(count):
            outs[i][:, :width] = pull[i : i + 1]
            outs[i][:, width:] = jnp.zeros((1, 128), F32) + mass[i : i + 1]
        key_r[...] = jnp.concatenate([p[1:2] for p in packets] + [p[2:3] for p in packets], axis=0)

    outs = [((1, width + 128), F32)] * count + [((2 * count, width), LOW)]
    return kernel_call(
        body, outs, [counts], lanes, 4 * count * queue.size, "queue_scores", [queue]
    )


def loss_end(counts, live, sums, keys, pulls, squares):
    width = sums[0].shape[1]
    rows = keys[0].shape[0] // 2
    n_keys, n_pulls = len(keys), len(pulls)

    def body(s, lv, q_r, qc_r, *refs):
        at = here()
        key_r, refs = refs[:n_keys], refs[n_keys:]
        pull_r, square_r, (grad_r, row_r) = refs[:n_pulls], refs[n_pulls:-2], refs[-2:]
        unit, inverse = unit_row(q_r[...] + qc_r[...], count_of(at, s, 0))
        low = bf(unit)
        total = pull_r[0][...]
        for piece in pull_r[1:]:
            total = total + piece[...]
        every = jnp.concatenate([k[0:rows] for k in key_r], axis=0)
        alive = jnp.concatenate([k[rows:] for k in key_r], axis=0).astype(F32)
        flags = dot_nt(jnp.ones((1, 128), F32), alive[:, :128]) * (1.0 / 128)
        positive = dot_nt(low, every) / TEMPER
        positive = jnp.where(flags > 0.5, positive, NEG_FILL)
        raised = jnp.exp(positive)
        mass = total[:, width : width + 1] + jnp.sum(raised, axis=-1, keepdims=True)
        weight = live_flag(at, lv) / jnp.sum(flags, axis=-1, keepdims=True)
        own = lax.broadcasted_iota(jnp.int32, positive.shape, 1) == 0
        self_logit = jnp.sum(jnp.where(own, positive, 0.0), axis=-1, keepdims=True)
        loss = weight * (jnp.log(mass) - self_logit)
        d_positive = bf(weight * (raised / mass - own.astype(F32)) / TEMPER)
        d_unit = dot_nn(d_positive, every) + (weight / mass / TEMPER) * total[:, :width]
        d_vector = inverse * (d_unit - unit * jnp.sum(unit * d_unit, axis=-1, keepdims=True))
        grad_r[...] = d_vector / count_of(at, s, 0).astype(F32)
        lane = lax.broadcasted_iota(jnp.int32, (1, 128), 1)
        tokens = 0.5 * count_of(at, s, 0).astype(F32)
        row = jnp.where(lane == 0, 0.5 * loss, jnp.where(lane == 1, tokens, 0.0))
        at_lane = 2
        for piece in square_r:
            values = jnp.sum(piece[...], axis=-1, keepdims=True)
            for i in range(piece.shape[0]):
                row = jnp.where(lane == at_lane, values[i : i + 1], row)
                at_lane += 1
        row_r[...] = row

    outs = [((1, width), F32), ((1, 128), F32)]
    arrays = sums + keys + pulls + squares
    return kernel_call(
        body, outs, [counts, live], arrays, 4 * n_keys * rows * width, "loss_end"
    )


def small_table(counts, encoders):
    width = encoders[0][0].shape[1]
    arrays = [a for e in encoders for a in e]

    def body(s, *refs):
        out_r = refs[-1]
        for e in range(2):
            gain_r, shift_r, exp_r, in_r = refs[4 * e : 4 * e + 4]
            out_r[e, ROW_GAIN : ROW_GAIN + 2, :] = gain_r[...].astype(F32)
            out_r[e, ROW_SHIFT : ROW_SHIFT + 4, :] = shift_r[...].astype(F32)
            groups, heads = exp_r.shape[0], in_r.shape[0]
            pieces = [exp_r[i : i + 1, :].astype(F32) for i in range(groups)]
            out_r[e, ROW_EXP : ROW_EXP + 1, :] = jnp.concatenate(pieces, axis=1)
            pieces = [in_r[h, i : i + 1, :].astype(F32) for i in range(2) for h in range(heads)]
            used = sum(p.shape[1] for p in pieces)
            pieces.append(jnp.zeros((1, width - used), F32))
            out_r[e, ROW_IN : ROW_IN + 1, :] = jnp.concatenate(pieces, axis=1)

    return kernel_call(body, [((2, 8, width), F32)], [counts], arrays, 64 * width, "small_table")[0]


def per_device(
    query_embed,
    key_embed,
    crop_counts,
    pair_mask,
    negative_queue,
    online_inproj,
    online_inbias,
    online_outproj,
    online_gains,
    online_shifts,
    online_expand,
    online_expbias,
    online_contract,
    momentum_inproj,
    momentum_inbias,
    momentum_outproj,
    momentum_gains,
    momentum_shifts,
    momentum_expand,
    momentum_expbias,
    momentum_contract,
):
    section = lax.axis_index(SECTION)
    head = lax.axis_index(HEADS)
    data = lax.axis_index(DP)
    dp_count = lax.axis_size(DP)
    rows, pairs_dev, width = query_embed.shape
    pairs = pairs_dev // lax.axis_size(SECTION)
    local = online_outproj.shape[1]
    blocks = dp_count if width % (dp_count * 32) == 0 and dp_count <= 8 else 1
    few = blocks > 1
    first = section == 0
    counts = crop_counts
    chosen = jnp.where(first, head // 2, head % 2)

    def pair_of(table, axis, pair):
        return lax.dynamic_index_in_dim(table, section * pairs + pair, axis, keepdims=False)

    order = Order()
    with jax.named_scope("in"):
        raw = []
        for table in (query_embed, key_embed):
            raw.append(jnp.stack([pair_of(table, 1, chosen), pair_of(table, 1, 1 - chosen)]))
    with jax.named_scope("ag0"):
        rows_first = [gather(r, True) for r in raw]
    order.mark(raw[1])

    held = [
        [
            jnp.transpose(inproj[0], (1, 2, 0)).reshape(3 * local, width),
            outproj[0],
            expand[0],
            contract[0],
        ]
        for inproj, outproj, expand, contract in (
            (online_inproj, online_outproj, online_expand, online_contract),
            (momentum_inproj, momentum_outproj, momentum_expand, momentum_contract),
        )
    ]
    with jax.named_scope("tab"):
        small = [
            [gains[0], shifts[0], expbias[0], jnp.transpose(inbias[0], (1, 0, 2))]
            for gains, shifts, expbias, inbias in (
                (online_gains, online_shifts, online_expbias, online_inbias),
                (momentum_gains, momentum_shifts, momentum_expbias, momentum_inbias),
            )
        ]
        table = small_table(order.tie(counts), small)
        order.mark(table)
        tables = [table, over_core(table)]
        neighbour_bias = jnp.where(first, tables[1], tables[0])[1, ROW_IN : ROW_IN + 1]
    with jax.named_scope("w"):
        came_weights = [[over_core(w) for w in held[e]] for e in range(2)]
        attn_sets = [held[e][:2] + came_weights[e][:2] for e in range(2)]
        feed_sets = [held[e][2:] + came_weights[e][2:] for e in range(2)]
    span = width // dp_count
    at_row = data * span
    cut = 3 * local

    def share_of(cols, outp):
        low_part = lax.dynamic_slice_in_dim(cols, jnp.minimum(at_row, cut - span), span, 0)
        high = lax.dynamic_slice_in_dim(outp, jnp.clip(at_row - cut, 0, local - span), span, 0)
        return jnp.where(at_row < cut, low_part, high)

    def layer_share(e):
        mine = share_of(held[e][0], held[e][1])
        other = share_of(came_weights[e][0], came_weights[e][1])
        return jnp.where(first, other, mine)

    with jax.named_scope("nb"):
        shares = layer_share(1)
    order.mark((order.last, shares))
    neighbour = types.SimpleNamespace()
    pooled_bias = jnp.zeros((1, width), F32)
    saved = [types.SimpleNamespace(), types.SimpleNamespace()]
    squares = []
    pooled = [None, None]

    def forward(e):
        save = e == 0
        layer_in = None
        for layer in range(2):
            if layer == 0:
                rows_in = rows_first[e]
                residual = [rows_in[0], rows_in[2]]
                attn_w, theirs = attn_sets[e], pooled_bias
            else:
                with jax.named_scope("ag1"):
                    rows_in = gather(layer_in, save)
                residual = [layer_in]
                attn_w, theirs = attn_sets[e], pooled_bias
                if not save:
                    attn_w, theirs = attn_w + [neighbour.attn], neighbour.bias
            yield
            parts, kept = attn_forward(
                order.tie(counts), rows_in, tables, theirs, attn_w, layer, e, save
            )
            order.mark(parts[0])
            with jax.named_scope("rs1"):
                pieces = scatter(*parts)
            if layer == 0 and e == 1:
                with jax.named_scope("nb"):
                    neighbour.bias = hop_two(behind(neighbour_bias, order.last))
                    neighbour.share = hop_two(behind(shares, order.last))
            yield
            *square, low = norm_middle(order.tie(counts), pieces, residual, tables, layer, e, save)
            if save:
                square, low, mixed = square[0], square[1], low
            order.mark(low)
            if layer == 0 and e == 1:
                with jax.named_scope("nb"):
                    share = behind(neighbour.share, order.last)
                    neighbour.attn = lax.all_gather(share, DP, axis=0, tiled=True)
            if save:
                vars(saved[layer]).update(
                    x=rows_in, qkv=kept[0], shares=kept[1], context=kept[2], mixed=mixed
                )
                squares.append(square)
            with jax.named_scope("ag2"):
                rows_in = gather(low, True)
            yield
            parts, kept = feed_forward(
                order.tie(counts), rows_in, tables, feed_sets[e], layer, e, save
            )
            order.mark(parts[0])
            with jax.named_scope("rs2"):
                pieces = scatter(*parts)
            yield
            outs = list(norm_last(order.tie(counts), pieces, low, tables, layer, e, save))
            out = outs.pop(0)
            order.mark(out)
            if save:
                vars(saved[layer]).update(hidden=rows_in, active=kept[0], slope=kept[1], summed=outs[1])
                squares.append(outs[0])
            layer_in = out
        pooled[e] = out

    threads = [forward(0), forward(1)]
    step = 0
    queue_unit = None
    while threads:
        for thread in list(threads):
            if next(thread, 0) == 0:
                threads.remove(thread)
        step += 1
        if step == 5 and few:
            queue_unit = queue_units(order.tie(counts), negative_queue)
            order.mark(queue_unit)

    with jax.named_scope("loss"):
        if few:
            sums = [pooled[0], hop_one(pooled[0]), pooled[1], hop_one(pooled[1])]
            packet = unit_packet(order.tie(counts), pair_mask, sums)
            lanes = [packet] + [swap(packet, DP, r) for r in range(1, dp_count)]
            *spread, keys = queue_scores(counts, lanes, queue_unit)
            pulls = [spread[0]] + [swap(spread[r], DP, r) for r in range(1, dp_count)]
            keys_two = [keys, hop_two(behind(keys, pulls[1]))]
            keys_all = keys_two + [over_core(k) for k in keys_two]
            d_pool, scalar_row = loss_end(counts, pair_mask, sums[:2], keys_all, pulls, squares)
        else:
            queue = negative_queue.astype(F32)
            norm = lax.rsqrt(jnp.sum(queue * queue, axis=-1, keepdims=True) + NORM_EPS)
            live = pair_of(pair_mask, 0, chosen).astype(F32)
            own_counts = pair_of(crop_counts, 0, chosen).astype(F32)
            both = jnp.concatenate(pooled)
            loss_part, d_pool = loss_section(both, own_counts, live, bf(queue * norm))
            branch = jnp.sum(jnp.concatenate(squares), axis=1)
            scalars = jnp.concatenate([jnp.stack([0.5 * loss_part, 0.5 * own_counts[0]]), branch])
            scalar_row = jnp.zeros((1, 128), F32).at[0, : scalars.shape[0]].set(scalars)

    scalar_hops = [(HEADS, 1), (HEADS, 2), (SECTION, 1)]
    distance = 1
    while distance < dp_count:
        scalar_hops.append((DP, distance))
        distance *= 2

    def scalar_steps(mark, count):
        nonlocal scalar_row
        with jax.named_scope("sc"):
            for _ in range(min(count, len(scalar_hops))):
                axis, far = scalar_hops.pop(0)
                tied = behind(scalar_row, mark)
                scalar_row = tied + swap(tied, axis, far)
        order.mark((order.last, scalar_row))

    order = Order()
    order.mark(d_pool)
    got = {}
    waiting, summed = [], {}

    def share_grads(name, mine, other):
        waiting.append((name, mine, other))

    def add_waiting():
        for name, mine, other in waiting:
            came = over_core(order.tie(other))
            both = add_cores(order.tie(counts), mine, came)
            order.mark(both)
            summed[name] = both
        waiting.clear()

    def reduce_summed(mark):
        for name, both in summed.items():
            with jax.named_scope("rg"):
                both = behind(both, (mark, list(got.values())[-1:]))
                got[name] = lax.psum_scatter(both, DP, scatter_dimension=0, tiled=False)
        summed.clear()

    residual, pieces, rows_above = None, None, []
    plain = types.SimpleNamespace(feed=[None, None], attn=[None, None], bias=[None, None])
    attn_w, feed_w = attn_sets[0], feed_sets[0]
    for layer in (1, 0):
        kept = saved[layer]
        source = dict(pooled=d_pool) if layer == 1 else dict(residual=residual, pieces=pieces)
        low, rows_last = last_backward(
            order.tie(counts), kept.summed, tables, layer, **source
        )
        order.mark(low)
        with jax.named_scope("ag3"):
            grads = gather(low, True)
        add_waiting()
        reduce_summed(grads[1:])
        *parts, d_inner, exp_row = feed_backward(
            order.tie(counts), grads, kept.slope, feed_w, layer
        )
        order.mark(exp_row)
        with jax.named_scope("rs3"):
            pieces = scatter(*parts)
        feed_got = weight_grads(
            order.tie(counts),
            grads,
            kept.hidden,
            [kept.active, d_inner],
            exp_row,
            blocks,
            "feed_weights",
        )
        order.mark(feed_got[0])
        if few:
            share_grads(("feed", layer), *feed_got)
            scalar_steps(exp_row, 1)
        low, norm_rows = middle_backward(
            order.tie(counts),
            kept.mixed,
            tables,
            layer,
            low,
            pieces,
            rows_last,
            rows_above,
            int(few and layer == 0),
        )
        residual = low
        order.mark(low)
        rows_above = [norm_rows]
        with jax.named_scope("ag4"):
            grads = gather(low, True)
        add_waiting()
        reduce_summed(grads[1] if layer == 0 else grads[1:])
        *parts, d_project, in_rows = attn_backward(
            order.tie(counts),
            grads,
            kept.qkv,
            kept.shares,
            kept.context,
            attn_w,
            layer,
        )
        order.mark(in_rows)
        with jax.named_scope("rs4"):
            pieces = scatter(*parts)
        attn_got = weight_grads(
            order.tie(counts),
            grads,
            kept.x,
            [kept.context, d_project],
            in_rows,
            blocks,
            "attn_weights",
        )
        order.mark(attn_got[0])
        if few:
            scalar_steps(in_rows, 1)
            if layer == 1:
                share_grads(("attn", layer), *attn_got)
        else:
            plain.feed[layer] = feed_got[0]
            plain.attn[layer] = attn_got[0]
            plain.bias[layer] = jnp.concatenate([exp_row, in_rows[0:1] + in_rows[1:2]])

    if not few:
        scalar_steps(in_rows, len(scalar_hops))

    if few:
        with jax.named_scope("lg"):
            both = add_cores(
                order.tie(counts), attn_got[0], over_core(attn_got[1]), [norm_rows], grads[1:]
            )
            order.mark(both)
            scalar_steps(both, len(scalar_hops))
            got["attn", 0] = lax.psum_scatter(both, DP, scatter_dimension=0, tiled=False)
        first_block = both
        d_in = bf(behind(residual[: 2 * rows], first_block).astype(F32) + scattered(*pieces))
        with jax.named_scope("dx"):
            came = hop_two(d_in[rows:])
            in_order = chosen == 0
            both = jnp.stack([jnp.where(in_order, d_in[:rows], came), jnp.where(in_order, came, d_in[:rows])])
            half_width = width // 2
            mine = lax.dynamic_slice_in_dim(both, section * half_width, half_width, 2)
            other = lax.dynamic_slice_in_dim(both, (1 - section) * half_width, half_width, 2)
            other = over_core(other)
            ordered = jnp.where(first, jnp.concatenate([mine, other]), jnp.concatenate([other, mine]))
            input_grad = jnp.transpose(ordered, (1, 0, 2))
        def shares_of(name):
            mine = [got[name, layer] for layer in range(2)]
            return [mine[0], over_core(mine[0]), mine[1], over_core(mine[1])]

        with jax.named_scope("fg"):
            exp_row, contract, expand = place_feed(order.tie(counts), shares_of("feed"))
            order.mark(contract)
        with jax.named_scope("tg"):
            got["attn", 0] = behind(got["attn", 0], contract)
            in_row, norms, inproj, outproj = place_attn(order.tie(counts), shares_of("attn"))
        exp_row, in_row = exp_row[0], in_row[0]
    else:
        first_block = in_rows
        d_in = bf(behind(residual[: 2 * rows], first_block).astype(F32) + scattered(*pieces))
        with jax.named_scope("dx"):
            came = hop_two(d_in[rows:])
            in_order = chosen == 0
            both = jnp.stack([jnp.where(in_order, d_in[:rows], came), jnp.where(in_order, came, d_in[:rows])])
            half_width = width // 2
            mine = lax.dynamic_slice_in_dim(both, section * half_width, half_width, 2)
            other = lax.dynamic_slice_in_dim(both, (1 - section) * half_width, half_width, 2)
            other = over_core(other)
            ordered = jnp.where(first, jnp.concatenate([mine, other]), jnp.concatenate([other, mine]))
            input_grad = jnp.transpose(ordered, (1, 0, 2))
        contract, expand = reduce_plain(plain.feed, section, 1)
        attn_sum = reduce_plain(plain.attn, section, 1)[0]
        inproj = jnp.transpose(attn_sum[:, :cut].reshape(-1, 3, local), (1, 0, 2))
        outproj = jnp.transpose(attn_sum[:, cut:])
        biases = lax.psum(jnp.stack(plain.bias), (SECTION, DP))
        exp_row, in_row = jnp.where(first, biases[0], biases[1])
        norms = lax.psum(norm_rows, (HEADS, SECTION, DP))
        norms = jnp.where(first, norms[:6], norms[6:])
    loss_total = scalar_row[0, 0]
    rms_values = jnp.sqrt(scalar_row[0, 2:8].reshape(2, 3) / (scalar_row[0, 1] * width))
    piece = width // (dp_count * lax.axis_size(HEADS))
    norms = lax.dynamic_slice_in_dim(norms, (data * lax.axis_size(HEADS) + head) * piece, piece, 1)
    exp_shape, in_shape = online_expbias.shape, online_inbias.shape
    grad_expbias = lax.dynamic_slice_in_dim(
        exp_row.reshape(exp_shape), data * (exp_shape[2] // dp_count), exp_shape[2] // dp_count, 2
    )
    grad_inbias = lax.dynamic_slice_in_dim(
        in_row[: 2 * local].reshape(in_shape),
        data * (in_shape[3] // dp_count),
        in_shape[3] // dp_count,
        3,
    )
    return (
        loss_total,
        input_grad,
        jnp.transpose(inproj, (1, 0, 2))[None],
        grad_inbias,
        outproj[None],
        norms[None, 0:2],
        norms[None, 2:6],
        expand[None],
        grad_expbias,
        jnp.transpose(contract)[None],
        rms_values,
    )


def solution(mesh):
    placed = (
        P(HEADS, DP, None),
        P(HEADS, DP, None),
        P(DP, None),
        P(DP),
        P(DP, None),
        P(SECTION, None, None, HEADS),
        P(SECTION, None, HEADS, None),
        P(SECTION, HEADS, None),
        P(SECTION, None, None),
        P(SECTION, None, None),
        P(SECTION, None, HEADS),
        P(SECTION, HEADS, None),
        P(SECTION, HEADS, None),
        P(SECTION, None, None, HEADS),
        P(SECTION, None, HEADS, None),
        P(SECTION, HEADS, None),
        P(SECTION, None, None),
        P(SECTION, None, None),
        P(SECTION, None, HEADS),
        P(SECTION, HEADS, None),
        P(SECTION, HEADS, None),
    )
    return jax.shard_map(
        per_device,
        mesh=mesh,
        in_specs=placed,
        out_specs=(
            P(),
            P(HEADS, DP, SECTION),
            P(SECTION, DP, None, HEADS),
            P(SECTION, None, HEADS, DP),
            P(SECTION, HEADS, DP),
            P(SECTION, None, (DP, HEADS)),
            P(SECTION, None, (DP, HEADS)),
            P(SECTION, DP, HEADS),
            P(SECTION, HEADS, DP),
            P(SECTION, HEADS, DP),
            P(),
        ),
        check_vma=False,
    )
```

```python
import functools
import types

import jax
import jax.numpy as jnp
from jax import lax
from jax.experimental import pallas as pl
from jax.experimental.pallas import tpu as pltpu
from jax.sharding import PartitionSpec as P

TEMPER = 0.05
NORM_EPS = 1e-06
NEG_FILL = -1000000000.0
F32 = jnp.float32
LOW = jnp.bfloat16
HEADS, SECTION, DP = "heads", "section", "dp"
VMEM_SPARE = 6 * 1024 * 1024
EXTRA = 16

ROW_GAIN = 0
ROW_SHIFT = 2
ROW_EXP = 6
ROW_IN = 7


def dot_nn(a, b):
    return lax.dot_general(a, b, (((1,), (0,)), ((), ())), preferred_element_type=F32)


def dot_nt(a, b):
    return lax.dot_general(a, b, (((1,), (1,)), ((), ())), preferred_element_type=F32)


def dot_tn(a, b):
    return lax.dot_general(a, b, (((0,), (0,)), ((), ())), preferred_element_type=F32)


def bytes_of(shape, dtype):
    return functools.reduce(lambda x, y: x * y, shape, 1) * jnp.dtype(dtype).itemsize


class Loaded:
    def __init__(self, source, buffer, sem):
        self.copy = pltpu.make_async_copy(source, buffer, sem)
        self.copy.start()
        self.buffer = buffer
        self.shape = buffer.shape
        self.waiting = True

    def ready(self):
        if self.waiting:
            self.copy.wait()
            self.waiting = False
        return self.buffer

    def __getitem__(self, index):
        return self.ready()[index]

    @property
    def at(self):
        return self.ready().at


class Stored:
    def __init__(self, target, buffer, sems):
        self.target, self.buffer, self.sems = target, buffer, sems
        self.shape, self.dtype = buffer.shape, buffer.dtype
        self.copies = []

    def __setitem__(self, index, value):
        self.buffer[index] = value

    def send(self, start=0, size=None):
        run = pl.ds(start, self.shape[0] if size is None else size)
        copy = pltpu.make_async_copy(
            self.buffer.at[run], self.target.at[run], self.sems.at[len(self.copies)]
        )
        copy.start()
        self.copies.append(copy)

    def finish(self):
        for copy in self.copies:
            copy.wait()


def kernel_call(
    body, outs, scalars, arrays, flops, name, loads=(), stores=(), distant=(), weights=0
):
    side = distant[-1].shape[-1] if weights else 0
    buffers = [(a.shape, a.dtype) for a in loads] + list(stores)
    if weights:
        buffers.append(((weights, side, side), LOW))
    held = sum(bytes_of(*x) for x in [(a.shape, a.dtype) for a in arrays] + list(outs) + buffers)
    sems = [pltpu.SemaphoreType.DMA((max(1, len(loads) + 2 * len(stores)),))]
    if weights:
        sems.append(pltpu.SemaphoreType.DMA((2 * weights,)))
    counts = [len(scalars), len(arrays), len(loads), len(distant), len(outs), len(stores)]

    def whole(*refs):
        groups = []
        for count in counts + [len(loads), len(stores)]:
            groups.append(list(refs[:count]))
            refs = refs[count:]
        scal, near, load_r, far, out_r, store_r, load_b, store_b = groups
        extra = list(refs[:1]) if weights else []
        sem = refs[1] if weights else refs[0]
        loaded = [Loaded(a, b, sem.at[i]) for i, (a, b) in enumerate(zip(load_r, load_b))]
        base = len(loaded)
        stored = [
            Stored(a, b, sem.at[pl.ds(base + 2 * i, 2)]) for i, (a, b) in enumerate(zip(store_r, store_b))
        ]
        if weights:
            extra.append(refs[2])
        body(*scal, *near, *loaded, *far, *out_r, *stored, *extra)
        for item in loaded:
            item.ready()
        for item in stored:
            if not item.copies:
                item.send()
        for item in stored:
            item.finish()

    hbm = pl.BlockSpec(memory_space=pltpu.HBM)
    vmem = pl.BlockSpec(memory_space=pltpu.VMEM)
    in_specs = [pl.BlockSpec(memory_space=pltpu.SMEM)] * len(scalars)
    in_specs += [vmem] * len(arrays) + [hbm] * (len(loads) + len(distant))
    apart = [pltpu.with_memory_space_constraint(d, pltpu.HBM) for d in [*loads, *distant]]
    return pl.pallas_call(
        whole,
        out_shape=[jax.ShapeDtypeStruct(s, d) for s, d in outs]
        + [pltpu.HBM(s, d) for s, d in stores],
        in_specs=in_specs,
        out_specs=[vmem] * len(outs) + [hbm] * len(stores),
        scratch_shapes=[pltpu.VMEM(s, d) for s, d in buffers] + sems,
        compiler_params=pltpu.CompilerParams(vmem_limit_bytes=held + VMEM_SPARE),
        cost_estimate=pl.CostEstimate(flops=flops, bytes_accessed=held, transcendentals=0),
        name=name,
    )(*scalars, *arrays, *apart)


def here():
    head, core, data = [lax.axis_index(a) for a in (HEADS, SECTION, DP)]
    near = jnp.where(core == 0, 1, 2)
    chosen = jnp.where(core == 0, head // 2, head % 2)
    return types.SimpleNamespace(head=head, core=core, data=data, near=near, chosen=chosen)


def count_of(at, counts, encoder, other=0):
    return counts[2 * at.core + jnp.bitwise_xor(at.chosen, other), encoder]


def table_row(at, tables, layer, encoder, row):
    held, came = [t[encoder, row : row + 1, :] for t in tables]
    return jnp.where(at.core == layer, held, came)


def start_fetch(at, layer, held, arrived, target, sem):
    @pl.when(at.core == layer)
    def _():
        pltpu.make_async_copy(held, target, sem).start()

    @pl.when(at.core != layer)
    def _():
        pltpu.make_async_copy(arrived, target, sem).start()

    return pltpu.make_async_copy(held, target, sem)


def start_copy(source, target, sem):
    copy = pltpu.make_async_copy(source, target, sem)
    copy.start()
    return copy


def fetch_attn(at, layer, encoder, refs, scratch, sems):
    cols, outp, cols_too, outp_too = refs[:4]
    cut = cols.shape[0]
    waits = [
        start_fetch(at, layer, cols, cols_too, scratch.at[0, pl.ds(0, cut)], sems.at[0]),
        start_fetch(at, layer, outp, outp_too, scratch.at[0, pl.ds(cut, outp.shape[0])], sems.at[1]),
    ]
    if len(refs) > 4:
        waits.append(start_copy(refs[4], scratch.at[1], sems.at[2]))
    return waits


def fetch_feed(at, layer, refs, scratch, sems):
    exp, con, exp_too, con_too = refs
    return [
        start_fetch(at, layer, exp, exp_too, scratch.at[0], sems.at[0]),
        start_fetch(at, layer, con, con_too, scratch.at[1], sems.at[1]),
    ]


def swap(value, axis, distance):
    count = lax.axis_size(axis)
    return lax.ppermute(value, axis, [(i, i ^ distance) for i in range(count)])


def hop(value, first_core, second_core):
    count = lax.axis_size(HEADS)
    route = [(i, i ^ first_core) for i in range(count)]
    route += [(count + i, count + (i ^ second_core)) for i in range(count)]
    return lax.ppermute(value, (SECTION, HEADS), route)


def hop_one(value):
    return hop(value, 1, 2)


def hop_two(value):
    return hop(value, 2, 1)


def hop_both(value):
    return hop(value, 3, 3)


def over_core(value):
    return swap(value, SECTION, 1)


def behind(value, mark):
    return lax.optimization_barrier((value, mark))[0]


class Order:
    def __init__(self):
        self.last = None

    def tie(self, value):
        return value if self.last is None else behind(value, self.last)

    def mark(self, value):
        self.last = value


def bf(value):
    return value.astype(LOW)


def norm_parts(values):
    mean = jnp.mean(values, axis=-1, keepdims=True)
    center = values - mean
    spread = jnp.mean(center * center, axis=-1, keepdims=True)
    rstd = lax.rsqrt(spread + NORM_EPS)
    return center * rstd, rstd


def row_position(at, rows, shape, other):
    block_rows = rows // 2
    lane = lax.broadcasted_iota(jnp.int32, shape, 0 if shape[1] == 1 else 1)
    slot = lane // block_rows
    far = 3 - at.near
    block = jnp.bitwise_xor(jnp.bitwise_xor(at.head, other * far), (slot & 1) * far)
    block = jnp.bitwise_xor(block, (slot // 2) * at.near)
    return block * block_rows + lane - slot * block_rows


def row_keep(at, counts, encoder, rows):
    return row_position(at, rows, (rows, 1), 0) < count_of(at, counts, encoder)


def key_keep(at, counts, encoder, rows, other):
    return row_position(at, rows, (1, 2 * rows), other) < count_of(at, counts, encoder, other)


def row_groups(sources):
    if len(sources) == 2:
        return [list(sources)] * 2
    if len(sources[0].shape) == 2:
        own, one, two, far = sources
        return [[own, one], [two, far]]
    own, one, two, far = sources
    return [
        [own.at[0], two.at[1], one.at[0], far.at[1]],
        [two.at[0], own.at[1], far.at[0], one.at[1]],
    ]


def stack_rows(group):
    return jnp.concatenate([piece[...] for piece in group], axis=0)


def put_rows(targets, outs):
    if len(targets) == 4:
        half = outs[0].shape[0] // 2
        values = [outs[0][:half], outs[0][half:], outs[1][:half], outs[1][half:]]
    else:
        total = outs[0] + outs[1]
        half = total.shape[0] // 2
        values = [total[:half], total[half:]]
    for target, value in zip(targets, values):
        target[...] = value.astype(target.dtype)


def parts_shapes(rows, width, count):
    return [((rows, width), F32)] + [((rows, width), LOW)] * (count - 1)


def rows_of(sources):
    shape = sources[0].shape
    return (2 * shape[1], shape[2]) if len(shape) == 3 else shape


def attn_forward(counts, sources, tables, theirs, weights, layer, encoder, save):
    wide = len(sources) == 4
    rows, width = rows_of(sources)
    local = width // 4
    heads = local // 64
    full = 2 * rows
    count = len(sources)

    def body(s, *refs):
        at = here()
        tb, th_r, source, refs = refs[:2], refs[2], refs[3 : 3 + count], refs[3 + count :]
        w_refs, refs = refs[: len(weights)], refs[len(weights) :]
        targets, kept, (w_r, sems) = refs[:count], refs[count:-2], refs[-2:]
        waits = fetch_attn(at, layer, encoder, w_refs, w_r, sems)
        groups = row_groups(source)
        outs = []
        for unit in range(2):
            side = 0 if wide else unit
            rows_in = stack_rows(groups[unit])
            keep = key_keep(at, s, encoder, rows, unit if wide else 0)
            bias = th_r[...] if side else table_row(at, tb, layer, encoder, ROW_IN)
            if unit == 0:
                waits[0].wait()
            elif not wide:
                waits[2].wait()
            project = dot_nt(rows_in, w_r[side, : 3 * local, :])
            q = bf(project[:, :local] + bias[:, :local])
            k = bf(project[:, local : 2 * local])
            v = bf(project[:, 2 * local :] + bias[:, local : 2 * local])
            if save:
                kept[0][unit, :, :local] = q
                kept[0][unit, :, local : 2 * local] = k
                kept[0][unit, :, 2 * local :] = v
                kept[0].send(unit, 1)
            pieces = []
            for h in range(heads):
                cut = slice(64 * h, 64 * h + 64)
                scores = jnp.where(keep, dot_nt(q[:, cut] * 0.125, k[:, cut]), NEG_FILL)
                raised = jnp.exp(scores - jnp.max(scores, axis=-1, keepdims=True))
                shares = bf(raised / jnp.sum(raised, axis=-1, keepdims=True))
                if save:
                    kept[1][unit * heads + h] = shares
                pieces.append(bf(dot_nn(shares, v[:, cut])))
            context = jnp.concatenate(pieces, axis=1)
            if save:
                kept[2][unit] = context
                kept[1].send(unit * heads, heads)
                kept[2].send(unit, 1)
            if unit == 0:
                waits[1].wait()
            outs.append(dot_nn(context, w_r[side, 3 * local :, :]))
        put_rows(targets, outs)

    outs, stores = parts_shapes(rows, width, count), []
    if save:
        stores = [
            ((2, full, 3 * local), LOW),
            ((2 * heads, full, full), LOW),
            ((2, full, local), LOW),
        ]
    flops = 4 * full * (4 * local * width + 2 * local * full)
    got = kernel_call(
        body,
        outs,
        [counts],
        tables + [theirs] + sources,
        flops,
        "attn_forward",
        [],
        stores,
        weights,
        1 if wide else 2,
    )
    return got[:count], got[count:]


def feed_forward(counts, sources, tables, weights, layer, encoder, save):
    rows, width = rows_of(sources)
    units = weights[0].shape[1]
    full = 2 * rows
    count = len(sources)

    def body(s, *refs):
        at = here()
        tb, source, refs = refs[:2], refs[2 : 2 + count], refs[2 + count :]
        w_refs, refs = refs[: len(weights)], refs[len(weights) :]
        targets, kept, (w_r, sems) = refs[:count], refs[count:-2], refs[-2:]
        waits = fetch_feed(at, layer, w_refs, w_r, sems)
        groups = row_groups(source)
        bias = table_row(at, tb, layer, encoder, ROW_EXP)
        outs = []
        for unit in range(2):
            rows_in = stack_rows(groups[unit])
            if unit == 0:
                waits[0].wait()
            inner = dot_nn(rows_in, w_r[0]) + bias
            phi = 0.5 * (1.0 + lax.erf(inner * (0.5**0.5)))
            active = bf(inner * phi)
            if save:
                density = jnp.exp(-0.5 * inner * inner) * 0.3989422804014327
                kept[0][unit] = active
                kept[1][unit] = bf(phi + inner * density)
                kept[0].send(unit, 1)
                kept[1].send(unit, 1)
            if unit == 0:
                waits[1].wait()
            outs.append(dot_nn(active, w_r[1]))
        put_rows(targets, outs)

    outs, stores = parts_shapes(rows, width, count), []
    if save:
        stores = [((2, full, units), LOW), ((2, full, units), LOW)]
    flops = 8 * full * width * units
    near = tables + sources
    got = kernel_call(body, outs, [counts], near, flops, "feed_forward", [], stores, weights, 2)
    return got[:count], got[count:]


def masked_squares(at, counts, encoder, values, rows):
    return column_sum(jnp.where(row_keep(at, counts, encoder, rows), values * values, 0.0))


def norm_middle(counts, pieces, layer_in, tables, layer, encoder, save):
    rows, width = pieces[0].shape
    count, inputs = len(pieces), len(layer_in)

    def body(s, *refs):
        at = here()
        tb, added, refs = refs[:2], refs[2 : 2 + count], refs[2 + count :]
        x_refs, refs = refs[:inputs], refs[inputs:]
        (square_r, low_r, mixed_r) = refs if save else (None, refs[0], None)
        if inputs == 1:
            rows_in = x_refs[0][...]
        else:
            rows_in = jnp.concatenate([x_refs[0][0], x_refs[1][1]], axis=0)
        attn = scattered(*added) + table_row(at, tb, layer, encoder, ROW_SHIFT)
        mixed = rows_in.astype(F32) + attn
        if save:
            mixed_r[...] = mixed
            mixed_r.send()
        xhat, _ = norm_parts(mixed)
        gain = table_row(at, tb, layer, encoder, ROW_GAIN)
        low_r[...] = bf(xhat * gain + table_row(at, tb, layer, encoder, ROW_SHIFT + 1))
        if save:
            square_r[...] = masked_squares(at, s, encoder, attn, rows)

    outs, stores = [((rows, width), LOW)], []
    if save:
        outs, stores = [((1, width), F32)] + outs, [((rows, width), F32)]
    near = tables + pieces + layer_in
    return kernel_call(body, outs, [counts], near, 20 * rows * width, "norm_middle", [], stores)


def norm_last(counts, pieces, hidden, tables, layer, encoder, save):
    rows, width = hidden.shape
    count = len(pieces)
    pool = layer == 1

    def body(s, *refs):
        at = here()
        tb, added, h_r, refs = refs[:2], refs[2 : 2 + count], refs[2 + count], list(refs[3 + count :])
        out_r = refs.pop(0)
        square_r = refs.pop(0) if save else None
        feed = scattered(*added) + table_row(at, tb, layer, encoder, ROW_SHIFT + 2)
        summed = h_r[...].astype(F32) + feed
        if save:
            refs[0][...] = summed
            refs[0].send()
        xhat, _ = norm_parts(summed)
        gain = table_row(at, tb, layer, encoder, ROW_GAIN + 1)
        out = xhat * gain + table_row(at, tb, layer, encoder, ROW_SHIFT + 3)
        if pool:
            out_r[...] = column_sum(jnp.where(row_keep(at, s, encoder, rows), out, 0.0))
        else:
            out_r[...] = bf(out)
        if save:
            square_r[0:1, :] = masked_squares(at, s, encoder, feed, rows)
            square_r[1:2, :] = masked_squares(at, s, encoder, out, rows)

    outs, stores = [((1, width), F32) if pool else ((rows, width), LOW)], []
    if save:
        outs, stores = outs + [((2, width), F32)], [((rows, width), F32)]
    near = tables + pieces + [hidden]
    return kernel_call(body, outs, [counts], near, 20 * rows * width, "norm_last", [], stores)


def gather(own, wide):
    hops = (hop_one, hop_two, hop_both) if wide else (hop_one,)
    return [own] + [move(own) for move in hops]


def scatter(part, *others):
    hops = (hop_one, hop_two, hop_both)
    return [part] + [move(value) for move, value in zip(hops, others)]


def scattered(part, *others):
    total = part[...]
    for value in others:
        total = total + value[: part.shape[0], :].astype(F32)
    return total


def norm_backward(values, grad, gain_row):
    xhat, rstd = norm_parts(values)
    scaled = grad * gain_row
    d_values = rstd * (
        scaled
        - jnp.mean(scaled, axis=-1, keepdims=True)
        - xhat * jnp.mean(scaled * xhat, axis=-1, keepdims=True)
    )
    return d_values, jnp.sum(grad * xhat, axis=0, keepdims=True)


def column_sum(values):
    return jnp.sum(values, axis=0, keepdims=True)


def norm_gradient(y_r, grad, gain, low_r):
    d_values, d_gain = norm_backward(y_r[...], grad, gain)
    low_r[...] = bf(d_values)
    return d_gain, column_sum(grad), column_sum(d_values)


def last_backward(counts, summed, tables, layer, pooled=None, residual=None, pieces=None):
    rows, width = summed.shape
    near = [pooled] if pooled is not None else [residual] + pieces[1:]
    loads = [summed] if pooled is not None else [summed, pieces[0]]
    inputs = len(near)

    def body(s, held_r, came_r, *rest):
        at = here()
        near_r, (y_r, *part_r), (rows_r, low_r) = rest[:inputs], rest[inputs:-2], rest[-2:]
        if pooled is not None:
            grad = jnp.where(row_keep(at, s, 0, rows), near_r[0][...], 0.0)
        else:
            grad = bf(scattered(part_r[0], *near_r)).astype(F32)
        gain = table_row(at, (held_r, came_r), layer, 0, ROW_GAIN + 1)
        for i, row in enumerate(norm_gradient(y_r, grad, gain, low_r)):
            rows_r[i : i + 1, :] = row

    outs = [((3, width), F32), ((rows, width), LOW)]
    got = kernel_call(
        body, outs, [counts], tables + near, 30 * summed.size, "last_backward", loads
    )
    return got[1], got[0]


def middle_backward(counts, mixed, tables, layer, residual, pieces, last_rows, above, ride):
    rows, width = mixed.shape
    known = [last_rows] + above
    total = 6 + 6 * len(above)

    def body(s, held_r, came_r, *rest):
        at = here()
        last_r, above_r, rest = rest[0], rest[1 : len(known)], rest[len(known) :]
        near_r, (y_r, part_r, rows_r, low_r) = rest[:-4], rest[-4:]
        grad = scattered(part_r, *near_r)
        gain = table_row(at, (held_r, came_r), layer, 0, ROW_GAIN)
        d_gain, in_sum, out_sum = norm_gradient(y_r, grad, gain, low_r.at[pl.ds(0, rows)])
        last = [last_r[i : i + 1, :] for i in range(3)]
        for i, row in enumerate((d_gain, last[0], out_sum, in_sum, last[2], last[1])):
            rows_r[i : i + 1, :] = row
        if above_r:
            rows_r[6:, :] = above_r[0][...]
        if ride:
            spare = jnp.zeros((EXTRA - total, width), F32)
            low_r[rows:, :] = bf(jnp.concatenate([rows_r[...], spare], axis=0))

    outs = [((total, width), F32), ((rows + EXTRA * ride, width), LOW)]
    near = tables + known + [residual] + pieces[1:]
    loads = [mixed, pieces[0]]
    got = kernel_call(body, outs, [counts], near, 30 * mixed.size, "middle_backward", loads)
    return got[1], got[0]


def feed_backward(counts, grads, slope, weights, layer):
    full, units = slope.shape[1:]
    rows, width = grads[0].shape
    count = len(grads)

    def body(s, *refs):
        source, sl_r, refs = refs[:count], refs[count], refs[count + 1 :]
        w_refs, refs = refs[: len(weights)], refs[len(weights) :]
        others, (bias_r, part, dinner_r, w_r, sems) = refs[: count - 1], refs[count - 1 :]
        targets = [part, *others]
        waits = fetch_feed(here(), layer, w_refs, w_r, sems)
        groups = row_groups(source)
        outs = []
        total = jnp.zeros((1, units), F32)
        for unit in range(2):
            if unit == 0:
                waits[1].wait()
            d_inner = dot_nt(stack_rows(groups[unit]), w_r[1]) * sl_r[unit].astype(F32)
            total = total + column_sum(d_inner)
            low = bf(d_inner)
            dinner_r[unit] = low
            dinner_r.send(unit, 1)
            if unit == 0:
                waits[0].wait()
            outs.append(dot_nt(low, w_r[0]))
        bias_r[...] = total
        put_rows(targets, outs)

    part, *outs = parts_shapes(rows, width, count)
    outs, stores = outs + [((1, units), F32)], [part, ((2, full, units), LOW)]
    flops = 8 * full * width * units
    got = kernel_call(
        body, outs, [counts], grads, flops, "feed_backward", [slope], stores, weights, 2
    )
    return [got[count], *got[: count - 1], got[count + 1], got[count - 1]]


def attn_backward(counts, grads, qkv, shares, context, weights, layer):
    wide = len(grads) == 4
    full, triple = qkv.shape[1:]
    local = triple // 3
    heads = local // 64
    rows, width = full // 2, grads[0].shape[1]
    count = len(grads)

    def body(s, *refs):
        source, refs = [g.at[pl.ds(0, rows)] for g in refs[:count]], refs[count:]
        (qkv_r, sh_r, cx_r), refs = refs[:3], refs[3:]
        w_refs, refs = refs[: len(weights)], refs[len(weights) :]
        others, (bias_r, part, dproj_r, w_r, sems) = refs[: count - 1], refs[count - 1 :]
        targets = [part, *others]
        waits = fetch_attn(here(), layer, 0, w_refs, w_r, sems)
        groups = row_groups(source)
        bias_r[...] = jnp.zeros((2, width), F32)
        outs = []
        for unit in range(2):
            side = 0 if wide else unit
            if unit == 0:
                waits[1].wait()
            elif not wide:
                waits[2].wait()
            d_context = bf(dot_nt(stack_rows(groups[unit]), w_r[side, triple:, :]))
            q = qkv_r[unit, :, :local]
            k = qkv_r[unit, :, local : 2 * local]
            v = qkv_r[unit, :, 2 * local :]
            weighted = d_context.astype(F32) * cx_r[unit].astype(F32)
            dqs, dks, dvs = [], [], []
            for h in range(heads):
                cut = slice(64 * h, 64 * h + 64)
                share = sh_r[unit * heads + h]
                dc = d_context[:, cut]
                dvs.append(dot_tn(share, dc))
                drop = jnp.sum(weighted[:, cut], axis=-1, keepdims=True)
                d_scores = bf(share.astype(F32) * (dot_nt(dc, v[:, cut]) - drop))
                dqs.append(dot_nn(d_scores, k[:, cut]) * 0.125)
                dks.append(dot_tn(d_scores, q[:, cut]) * 0.125)
            dq = jnp.concatenate(dqs, axis=1)
            dk = jnp.concatenate(dks, axis=1)
            dv = jnp.concatenate(dvs, axis=1)
            bias_r[unit : unit + 1, :local] = column_sum(dq)
            bias_r[unit : unit + 1, local : 2 * local] = column_sum(dv)
            d_project = bf(jnp.concatenate([dq, dk, dv], axis=1))
            dproj_r[unit] = d_project
            dproj_r.send(unit, 1)
            if unit == 0:
                waits[0].wait()
            outs.append(dot_nn(d_project, w_r[side, :triple, :]))
        put_rows(targets, outs)

    part = ((rows, width), F32)
    outs = [((rows, width), LOW)] * (count - 1)
    outs, stores = outs + [((2, width), F32)], [part, ((2, full, triple), LOW)]
    flops = 4 * full * (4 * local * width + 4 * local * full)
    loads = [qkv, shares, context]
    side = 1 if wide else 2
    got = kernel_call(
        body, outs, [counts], grads, flops, "attn_backward", loads, stores, weights, side
    )
    return [got[count], *got[: count - 1], got[count + 1], got[count - 1]]


def put_blocks(at, out_ref, parts, extra, blocks, other):
    if extra.shape[0] < EXTRA:
        extra = jnp.concatenate([extra, jnp.zeros((EXTRA - extra.shape[0], extra.shape[1]), F32)], axis=0)
    extra = bf(extra)
    span = parts[0].shape[0] // blocks
    half = span // 2
    wanted = jnp.bitwise_xor(at.core, other)
    for block in range(blocks):
        for i, value in enumerate(parts):
            halves = [bf(value[block * span + j * half : block * span + (j + 1) * half]) for j in range(2)]
            out_ref[block, i * half : (i + 1) * half, :] = jnp.where(wanted == 0, *halves)
        out_ref[block, len(parts) * half :, :] = extra


def weight_grads(counts, grads, inputs, pairs, bias, blocks, name):
    count = len(grads)
    width = grads[0].shape[-1]
    attention = name == "attn_weights"
    columns = sum(p.shape[2] for p in pairs) if attention else pairs[0].shape[2]
    parts_count = 1 if attention else 2

    def body(s, *refs):
        at = here()
        bias_r, g_refs, refs = refs[0], refs[1 : 1 + count], refs[1 + count :]
        x_refs, (o_r, d_r), targets = refs[:count], refs[count : count + 2], refs[count + 2 :]
        half = pairs[0].shape[1] // 2
        g_rows = [stack_rows(g) for g in row_groups([g.at[pl.ds(0, half)] for g in g_refs])]
        back = dot_tn(g_rows[0], o_r[0]) + dot_tn(g_rows[1], o_r[1])
        x_rows = [stack_rows(x) for x in row_groups(x_refs)]
        ahead = dot_tn(x_rows[0], d_r[0]) + dot_tn(x_rows[1], d_r[1])
        row = bias_r[0:1, :] + bias_r[1:2, :] if bias_r.shape[0] == 2 else bias_r[...]
        parts = [jnp.concatenate([ahead, back], axis=1)] if attention else [back, ahead]
        if blocks > 1:
            put_blocks(at, targets[0], parts, row, blocks, 1)
            put_blocks(at, targets[1], parts, row, blocks, 0)
        else:
            for i, part in enumerate(parts):
                targets[0][i] = bf(part)

    if blocks > 1:
        shape = (blocks, parts_count * (width // blocks // 2) + EXTRA, columns)
        outs, stores = [(shape, LOW)], [(shape, LOW)]
    else:
        outs, stores = [((parts_count, width, columns), LOW)], []
    flops = sum(4 * p.shape[1] * width * p.shape[2] for p in pairs)
    loads = grads + inputs + pairs
    got = kernel_call(body, outs, [counts], [bias], flops, name, loads, stores)
    return [got[1], got[0]] if blocks > 1 else got


def add_cores(counts, mine, came, norms=(), arrived=()):
    blocks, rows = mine.shape[:2]
    start = rows - EXTRA

    def body(s, *refs):
        norm_r, (c_r, m_r, *arrived_r, out_r) = refs[: len(norms)], refs[len(norms) :]
        for block in range(blocks):
            total = m_r[block].astype(F32) + c_r[block].astype(F32)
            if norms:
                summed = norm_r[0][...]
                for piece in arrived_r:
                    rows_there = piece[piece.shape[0] - EXTRA :, :].astype(F32)
                    summed = summed + rows_there[: summed.shape[0]]
                spare = jnp.zeros((EXTRA - 1 - summed.shape[0], summed.shape[1]), F32)
                total = jnp.concatenate([total[: start + 1], summed, spare], axis=0)
            out_r[block] = bf(total)
            if block % 2:
                out_r.send(block - 1, 2)

    stores = [(mine.shape, LOW)]
    near, loads = [*norms, came], [mine, *arrived]
    return kernel_call(body, [], [counts], near, mine.size, "add_cores", loads, stores)[0]


def in_core_order(at, refs, start, size):
    run = slice(start, start + size)
    mine = jnp.where(at.core == 0, refs[0][run, :], refs[2][run, :]).astype(F32)
    other = jnp.where(at.core == 0, refs[1][run, :], refs[3][run, :]).astype(F32)
    own = at.core == 0
    return jnp.concatenate([jnp.where(own, mine, other), jnp.where(own, other, mine)], axis=0)


def own_row(at, refs, row):
    return jnp.where(at.core == 0, refs[0][row : row + 1, :], refs[2][row : row + 1, :]).astype(F32)


def place_feed(counts, shares):
    rows, width = shares[0].shape
    part = (rows - EXTRA) // 2

    def body(s, *refs):
        at = here()
        refs, (row_r, con_r, exp_r) = refs[:4], refs[4:]
        con_r[...] = in_core_order(at, refs, 0, part)
        con_r.send()
        exp_r[...] = in_core_order(at, refs, part, part)
        row_r[...] = own_row(at, refs, 2 * part)

    outs, stores = [((1, width), F32)], [((2 * part, width), F32)] * 2
    return kernel_call(
        body, outs, [counts], [], 4 * rows * width, "place_feed", shares, stores
    )


def place_attn(counts, shares):
    rows, width = shares[0].shape
    part = rows - EXTRA
    local = width // 4

    def body(s, *refs):
        at = here()
        refs, (row_r, norm_r, in_r, out_r) = refs[:4], refs[4:]
        both = in_core_order(at, refs, 0, part)
        for i in range(3):
            in_r[i] = both[:, i * local : (i + 1) * local]
        in_r.send()
        out_r[...] = both[:, 3 * local :].T
        row_r[...] = own_row(at, refs, part)
        norms = refs[0][part + 1 : part + 13, :].astype(F32) + refs[1][part + 1 : part + 13, :].astype(F32)
        norm_r[...] = jnp.where(at.core == 0, norms[:6], norms[6:])

    outs = [((1, width), F32), ((6, width), F32)]
    stores = [((3, 2 * part, local), F32), ((local, 2 * part), F32)]
    return kernel_call(
        body, outs, [counts], [], 4 * rows * width, "place_attn", shares, stores
    )


def reduce_plain(layers, section, axis):
    mine = jnp.where(section == 0, layers[0], layers[1]).astype(F32)
    other = over_core(jnp.where(section == 0, layers[1], layers[0]))
    low = bf(mine + other.astype(F32))
    return lax.psum_scatter(low, DP, scatter_dimension=axis, tiled=True).astype(F32)


def summed_over(value, axis):
    count = lax.axis_size(axis)
    distance = 1
    while distance < count:
        value = value + swap(value, axis, distance)
        distance *= 2
    return value


def by_distance(entries, axis):
    count = entries.shape[0]
    order = jnp.bitwise_xor(jnp.arange(count), lax.axis_index(axis))
    chosen = (order[:, None] == jnp.arange(count)[None, :]).astype(entries.dtype)
    flat = jnp.dot(chosen, entries.reshape(count, -1), precision=lax.Precision.HIGHEST)
    return flat.astype(entries.dtype).reshape(entries.shape)


def loss_section(pooled, counts, live, queue_unit):
    count = lax.axis_size(DP)
    width = pooled.shape[-1]
    with jax.named_scope("pool"):
        pooled = pooled + hop_one(pooled)
    vectors = pooled / counts[:, None]
    inverse = lax.rsqrt(jnp.sum(vectors * vectors, axis=-1, keepdims=True) + NORM_EPS)
    units = vectors * inverse
    low = bf(units)
    flags = jnp.broadcast_to(bf(live), (1, width))
    packet = jnp.concatenate([low, flags], axis=0)
    with jax.named_scope("keys"):
        if count <= 8:
            lanes = jnp.stack([packet] + [swap(packet, DP, r) for r in range(1, count)])
        else:
            lanes = by_distance(lax.all_gather(packet, DP, axis=0), DP)
    queries = lanes[:, 0]
    with jax.named_scope("keys"):
        every = jnp.stack([lanes[:, 1:], hop_two(lanes[:, 1:])])
        every = jnp.stack([every, over_core(every)]).reshape(4 * count, 2, width)
    keys, alive = every[:, 0], every[:, 1, 0].astype(F32)
    raised = jnp.exp(dot_nt(queries, queue_unit) / TEMPER)
    mass = jnp.sum(raised, axis=1, keepdims=True)
    pull = dot_nn(bf(raised), queue_unit)
    spread = jnp.concatenate([pull, jnp.broadcast_to(mass, (count, 128))], axis=1)
    with jax.named_scope("pull"):
        if count <= 8:
            total = spread[0:1]
            for r in range(1, count):
                total = total + swap(spread[r : r + 1], DP, r)
        else:
            placed = by_distance(spread, DP)
            total = lax.psum_scatter(placed, DP, scatter_dimension=0, tiled=True)
    positive = dot_nt(low[0:1], keys) / TEMPER
    positive = jnp.where(alive[None, :] > 0, positive, NEG_FILL)
    pos_raised = jnp.exp(positive)
    mass = total[0, width] + jnp.sum(pos_raised)
    own_pair = (jnp.arange(keys.shape[0])[None, :] == 0).astype(F32)
    weight = live / jnp.sum(alive)
    loss_part = weight * (jnp.log(mass) - positive[0, 0])
    d_positive = bf(weight * (pos_raised / mass - own_pair) / TEMPER)
    d_unit = dot_nn(d_positive, keys) + (weight / mass / TEMPER) * total[:, :width]
    unit = units[0:1]
    d_vector = inverse[0:1] * (d_unit - unit * jnp.sum(unit * d_unit, axis=-1, keepdims=True))
    return loss_part, d_vector / counts[0]


def unit_row(total, count):
    vector = total / count.astype(F32)
    inverse = lax.rsqrt(jnp.sum(vector * vector, axis=-1, keepdims=True) + NORM_EPS)
    return vector * inverse, inverse


def queue_units(counts, queue):
    def body(s, x_r, out_r):
        values = x_r[...].astype(F32)
        out_r[...] = bf(values * lax.rsqrt(jnp.sum(values * values, axis=-1, keepdims=True) + NORM_EPS))

    stores = [(queue.shape, LOW)]
    return kernel_call(body, [], [counts], [], 4 * queue.size, "queue_units", [queue], stores)[0]


def live_flag(at, live):
    return live[2 * at.core + at.chosen].astype(F32)


def unit_packet(counts, live, sums):
    width = sums[0].shape[1]

    def body(s, lv, q_r, qc_r, k_r, kc_r, out_r):
        at = here()
        query, _ = unit_row(q_r[...] + qc_r[...], count_of(at, s, 0))
        key, _ = unit_row(k_r[...] + kc_r[...], count_of(at, s, 1))
        flag = jnp.zeros((1, width), F32) + live_flag(at, lv)
        out_r[...] = bf(jnp.concatenate([query, key, flag], axis=0))

    return kernel_call(body, [((3, width), LOW)], [counts, live], sums, 8 * width, "unit_packet")[0]


def queue_scores(counts, lanes, queue):
    count = len(lanes)
    width = queue.shape[1]

    def body(s, *refs):
        lane_r, q_r, outs, key_r = refs[:count], refs[count], refs[count + 1 : -1], refs[-1]
        packets = [lane[...] for lane in lane_r]
        queries = jnp.concatenate([p[0:1] for p in packets], axis=0)
        raised = jnp.exp(dot_nt(queries, q_r[...]) / TEMPER)
        mass = jnp.sum(raised, axis=1, keepdims=True)
        pull = dot_nn(bf(raised), q_r[...])
        for i in range(count):
            outs[i][:, :width] = pull[i : i + 1]
            outs[i][:, width:] = jnp.zeros((1, 128), F32) + mass[i : i + 1]
        key_r[...] = jnp.concatenate([p[1:2] for p in packets] + [p[2:3] for p in packets], axis=0)

    outs = [((1, width + 128), F32)] * count + [((2 * count, width), LOW)]
    return kernel_call(
        body, outs, [counts], lanes, 4 * count * queue.size, "queue_scores", [queue]
    )


def loss_end(counts, live, sums, keys, pulls, squares):
    width = sums[0].shape[1]
    rows = keys[0].shape[0] // 2
    n_keys, n_pulls = len(keys), len(pulls)

    def body(s, lv, q_r, qc_r, *refs):
        at = here()
        key_r, refs = refs[:n_keys], refs[n_keys:]
        pull_r, square_r, (grad_r, row_r) = refs[:n_pulls], refs[n_pulls:-2], refs[-2:]
        unit, inverse = unit_row(q_r[...] + qc_r[...], count_of(at, s, 0))
        low = bf(unit)
        total = pull_r[0][...]
        for piece in pull_r[1:]:
            total = total + piece[...]
        every = jnp.concatenate([k[0:rows] for k in key_r], axis=0)
        alive = jnp.concatenate([k[rows:] for k in key_r], axis=0).astype(F32)
        flags = dot_nt(jnp.ones((1, 128), F32), alive[:, :128]) * (1.0 / 128)
        positive = dot_nt(low, every) / TEMPER
        positive = jnp.where(flags > 0.5, positive, NEG_FILL)
        raised = jnp.exp(positive)
        mass = total[:, width : width + 1] + jnp.sum(raised, axis=-1, keepdims=True)
        weight = live_flag(at, lv) / jnp.sum(flags, axis=-1, keepdims=True)
        own = lax.broadcasted_iota(jnp.int32, positive.shape, 1) == 0
        self_logit = jnp.sum(jnp.where(own, positive, 0.0), axis=-1, keepdims=True)
        loss = weight * (jnp.log(mass) - self_logit)
        d_positive = bf(weight * (raised / mass - own.astype(F32)) / TEMPER)
        d_unit = dot_nn(d_positive, every) + (weight / mass / TEMPER) * total[:, :width]
        d_vector = inverse * (d_unit - unit * jnp.sum(unit * d_unit, axis=-1, keepdims=True))
        grad_r[...] = d_vector / count_of(at, s, 0).astype(F32)
        lane = lax.broadcasted_iota(jnp.int32, (1, 128), 1)
        tokens = 0.5 * count_of(at, s, 0).astype(F32)
        row = jnp.where(lane == 0, 0.5 * loss, jnp.where(lane == 1, tokens, 0.0))
        at_lane = 2
        for piece in square_r:
            values = jnp.sum(piece[...], axis=-1, keepdims=True)
            for i in range(piece.shape[0]):
                row = jnp.where(lane == at_lane, values[i : i + 1], row)
                at_lane += 1
        row_r[...] = row

    outs = [((1, width), F32), ((1, 128), F32)]
    arrays = sums + keys + pulls + squares
    return kernel_call(
        body, outs, [counts, live], arrays, 4 * n_keys * rows * width, "loss_end"
    )


def small_table(counts, encoders):
    width = encoders[0][0].shape[1]
    arrays = [a for e in encoders for a in e]

    def body(s, *refs):
        out_r = refs[-1]
        for e in range(2):
            gain_r, shift_r, exp_r, in_r = refs[4 * e : 4 * e + 4]
            out_r[e, ROW_GAIN : ROW_GAIN + 2, :] = gain_r[...].astype(F32)
            out_r[e, ROW_SHIFT : ROW_SHIFT + 4, :] = shift_r[...].astype(F32)
            groups, heads = exp_r.shape[0], in_r.shape[0]
            pieces = [exp_r[i : i + 1, :].astype(F32) for i in range(groups)]
            out_r[e, ROW_EXP : ROW_EXP + 1, :] = jnp.concatenate(pieces, axis=1)
            pieces = [in_r[h, i : i + 1, :].astype(F32) for i in range(2) for h in range(heads)]
            used = sum(p.shape[1] for p in pieces)
            pieces.append(jnp.zeros((1, width - used), F32))
            out_r[e, ROW_IN : ROW_IN + 1, :] = jnp.concatenate(pieces, axis=1)

    return kernel_call(body, [((2, 8, width), F32)], [counts], arrays, 64 * width, "small_table")[0]


def per_device(
    query_embed,
    key_embed,
    crop_counts,
    pair_mask,
    negative_queue,
    online_inproj,
    online_inbias,
    online_outproj,
    online_gains,
    online_shifts,
    online_expand,
    online_expbias,
    online_contract,
    momentum_inproj,
    momentum_inbias,
    momentum_outproj,
    momentum_gains,
    momentum_shifts,
    momentum_expand,
    momentum_expbias,
    momentum_contract,
):
    section = lax.axis_index(SECTION)
    head = lax.axis_index(HEADS)
    data = lax.axis_index(DP)
    dp_count = lax.axis_size(DP)
    rows, pairs_dev, width = query_embed.shape
    pairs = pairs_dev // lax.axis_size(SECTION)
    local = online_outproj.shape[1]
    blocks = dp_count if width % (dp_count * 32) == 0 and dp_count <= 8 else 1
    few = blocks > 1
    first = section == 0
    counts = crop_counts
    chosen = jnp.where(first, head // 2, head % 2)

    def pair_of(table, axis, pair):
        return lax.dynamic_index_in_dim(table, section * pairs + pair, axis, keepdims=False)

    order = Order()
    with jax.named_scope("in"):
        raw = []
        for table in (query_embed, key_embed):
            raw.append(jnp.stack([pair_of(table, 1, chosen), pair_of(table, 1, 1 - chosen)]))
    with jax.named_scope("ag0"):
        rows_first = [gather(r, True) for r in raw]
    order.mark(raw[1])

    held = [
        [
            jnp.transpose(inproj[0], (1, 2, 0)).reshape(3 * local, width),
            outproj[0],
            expand[0],
            contract[0],
        ]
        for inproj, outproj, expand, contract in (
            (online_inproj, online_outproj, online_expand, online_contract),
            (momentum_inproj, momentum_outproj, momentum_expand, momentum_contract),
        )
    ]
    with jax.named_scope("tab"):
        small = [
            [gains[0], shifts[0], expbias[0], jnp.transpose(inbias[0], (1, 0, 2))]
            for gains, shifts, expbias, inbias in (
                (online_gains, online_shifts, online_expbias, online_inbias),
                (momentum_gains, momentum_shifts, momentum_expbias, momentum_inbias),
            )
        ]
        table = small_table(order.tie(counts), small)
        order.mark(table)
        tables = [table, over_core(table)]
        neighbour_bias = jnp.where(first, tables[1], tables[0])[1, ROW_IN : ROW_IN + 1]
    with jax.named_scope("w"):
        came_weights = [[over_core(w) for w in held[e]] for e in range(2)]
        attn_sets = [held[e][:2] + came_weights[e][:2] for e in range(2)]
        feed_sets = [held[e][2:] + came_weights[e][2:] for e in range(2)]
    span = width // dp_count
    at_row = data * span
    cut = 3 * local

    def share_of(cols, outp):
        low_part = lax.dynamic_slice_in_dim(cols, jnp.minimum(at_row, cut - span), span, 0)
        high = lax.dynamic_slice_in_dim(outp, jnp.clip(at_row - cut, 0, local - span), span, 0)
        return jnp.where(at_row < cut, low_part, high)

    def layer_share(e):
        mine = share_of(held[e][0], held[e][1])
        other = share_of(came_weights[e][0], came_weights[e][1])
        return jnp.where(first, other, mine)

    with jax.named_scope("nb"):
        shares = layer_share(1)
    order.mark((order.last, shares))
    neighbour = types.SimpleNamespace()
    pooled_bias = jnp.zeros((1, width), F32)
    saved = [types.SimpleNamespace(), types.SimpleNamespace()]
    squares = []
    pooled = [None, None]

    def forward(e):
        save = e == 0
        layer_in = None
        for layer in range(2):
            if layer == 0:
                rows_in = rows_first[e]
                residual = [rows_in[0], rows_in[2]]
                attn_w, theirs = attn_sets[e], pooled_bias
            else:
                with jax.named_scope("ag1"):
                    rows_in = gather(layer_in, save)
                residual = [layer_in]
                attn_w, theirs = attn_sets[e], pooled_bias
                if not save:
                    attn_w, theirs = attn_w + [neighbour.attn], neighbour.bias
            yield
            parts, kept = attn_forward(
                order.tie(counts), rows_in, tables, theirs, attn_w, layer, e, save
            )
            order.mark(parts[0])
            with jax.named_scope("rs1"):
                pieces = scatter(*parts)
            if layer == 0 and e == 1:
                with jax.named_scope("nb"):
                    neighbour.bias = hop_two(behind(neighbour_bias, order.last))
                    neighbour.share = hop_two(behind(shares, order.last))
            yield
            *square, low = norm_middle(order.tie(counts), pieces, residual, tables, layer, e, save)
            if save:
                square, low, mixed = square[0], square[1], low
            order.mark(low)
            if layer == 0 and e == 1:
                with jax.named_scope("nb"):
                    share = behind(neighbour.share, order.last)
                    neighbour.attn = lax.all_gather(share, DP, axis=0, tiled=True)
            if save:
                vars(saved[layer]).update(
                    x=rows_in, qkv=kept[0], shares=kept[1], context=kept[2], mixed=mixed
                )
                squares.append(square)
            with jax.named_scope("ag2"):
                rows_in = gather(low, True)
            yield
            parts, kept = feed_forward(
                order.tie(counts), rows_in, tables, feed_sets[e], layer, e, save
            )
            order.mark(parts[0])
            with jax.named_scope("rs2"):
                pieces = scatter(*parts)
            yield
            outs = list(norm_last(order.tie(counts), pieces, low, tables, layer, e, save))
            out = outs.pop(0)
            order.mark(out)
            if save:
                vars(saved[layer]).update(hidden=rows_in, active=kept[0], slope=kept[1], summed=outs[1])
                squares.append(outs[0])
            layer_in = out
        pooled[e] = out

    threads = [forward(0), forward(1)]
    step = 0
    queue_unit = None
    while threads:
        for thread in list(threads):
            if next(thread, 0) == 0:
                threads.remove(thread)
        step += 1
        if step == 5 and few:
            queue_unit = queue_units(order.tie(counts), negative_queue)
            order.mark(queue_unit)

    with jax.named_scope("loss"):
        if few:
            sums = [pooled[0], hop_one(pooled[0]), pooled[1], hop_one(pooled[1])]
            packet = unit_packet(order.tie(counts), pair_mask, sums)
            lanes = [packet] + [swap(packet, DP, r) for r in range(1, dp_count)]
            *spread, keys = queue_scores(counts, lanes, queue_unit)
            pulls = [spread[0]] + [swap(spread[r], DP, r) for r in range(1, dp_count)]
            keys_two = [keys, hop_two(behind(keys, pulls[1]))]
            keys_all = keys_two + [over_core(k) for k in keys_two]
            d_pool, scalar_row = loss_end(counts, pair_mask, sums[:2], keys_all, pulls, squares)
        else:
            queue = negative_queue.astype(F32)
            norm = lax.rsqrt(jnp.sum(queue * queue, axis=-1, keepdims=True) + NORM_EPS)
            live = pair_of(pair_mask, 0, chosen).astype(F32)
            own_counts = pair_of(crop_counts, 0, chosen).astype(F32)
            both = jnp.concatenate(pooled)
            loss_part, d_pool = loss_section(both, own_counts, live, bf(queue * norm))
            branch = jnp.sum(jnp.concatenate(squares), axis=1)
            scalars = jnp.concatenate([jnp.stack([0.5 * loss_part, 0.5 * own_counts[0]]), branch])
            scalar_row = jnp.zeros((1, 128), F32).at[0, : scalars.shape[0]].set(scalars)

    scalar_hops = [(HEADS, 1), (HEADS, 2), (SECTION, 1)]
    distance = 1
    while distance < dp_count:
        scalar_hops.append((DP, distance))
        distance *= 2

    def scalar_steps(mark, count):
        nonlocal scalar_row
        with jax.named_scope("sc"):
            for _ in range(min(count, len(scalar_hops))):
                axis, far = scalar_hops.pop(0)
                tied = behind(scalar_row, mark)
                scalar_row = tied + swap(tied, axis, far)
        order.mark((order.last, scalar_row))

    order = Order()
    order.mark(d_pool)
    got = {}
    waiting, summed = [], {}

    def share_grads(name, mine, other):
        waiting.append((name, mine, other))

    def add_waiting():
        for name, mine, other in waiting:
            came = over_core(order.tie(other))
            both = add_cores(order.tie(counts), mine, came)
            order.mark(both)
            summed[name] = both
        waiting.clear()

    def reduce_summed(mark):
        for name, both in summed.items():
            with jax.named_scope("rg"):
                both = behind(both, (mark, list(got.values())[-1:]))
                got[name] = lax.psum_scatter(both, DP, scatter_dimension=0, tiled=False)
        summed.clear()

    residual, pieces, rows_above = None, None, []
    plain = types.SimpleNamespace(feed=[None, None], attn=[None, None], bias=[None, None])
    attn_w, feed_w = attn_sets[0], feed_sets[0]
    for layer in (1, 0):
        kept = saved[layer]
        source = dict(pooled=d_pool) if layer == 1 else dict(residual=residual, pieces=pieces)
        low, rows_last = last_backward(
            order.tie(counts), kept.summed, tables, layer, **source
        )
        order.mark(low)
        with jax.named_scope("ag3"):
            grads = gather(low, True)
        add_waiting()
        reduce_summed(grads[1])
        *parts, d_inner, exp_row = feed_backward(
            order.tie(counts), grads, kept.slope, feed_w, layer
        )
        order.mark(exp_row)
        with jax.named_scope("rs3"):
            pieces = scatter(*parts)
        feed_got = weight_grads(
            order.tie(counts),
            grads,
            kept.hidden,
            [kept.active, d_inner],
            exp_row,
            blocks,
            "feed_weights",
        )
        order.mark(feed_got[0])
        if few:
            share_grads(("feed", layer), *feed_got)
            scalar_steps(exp_row, 1)
            if layer == 0:
                add_waiting()
                reduce_summed(pieces[1:])
        low, norm_rows = middle_backward(
            order.tie(counts),
            kept.mixed,
            tables,
            layer,
            low,
            pieces,
            rows_last,
            rows_above,
            int(few and layer == 0),
        )
        residual = low
        order.mark(low)
        rows_above = [norm_rows]
        with jax.named_scope("ag4"):
            grads = gather(low, True)
        add_waiting()
        reduce_summed(grads[1:])
        *parts, d_project, in_rows = attn_backward(
            order.tie(counts),
            grads,
            kept.qkv,
            kept.shares,
            kept.context,
            attn_w,
            layer,
        )
        order.mark(in_rows)
        with jax.named_scope("rs4"):
            pieces = scatter(*parts)
        attn_got = weight_grads(
            order.tie(counts),
            grads,
            kept.x,
            [kept.context, d_project],
            in_rows,
            blocks,
            "attn_weights",
        )
        order.mark(attn_got[0])
        if few:
            scalar_steps(in_rows, 1)
            if layer == 1:
                share_grads(("attn", layer), *attn_got)
        else:
            plain.feed[layer] = feed_got[0]
            plain.attn[layer] = attn_got[0]
            plain.bias[layer] = jnp.concatenate([exp_row, in_rows[0:1] + in_rows[1:2]])

    if not few:
        scalar_steps(in_rows, len(scalar_hops))

    if few:
        with jax.named_scope("lg"):
            both = add_cores(
                order.tie(counts), attn_got[0], over_core(attn_got[1]), [norm_rows], grads[1:]
            )
            order.mark(both)
            scalar_steps(both, len(scalar_hops))
            got["attn", 0] = lax.psum_scatter(both, DP, scatter_dimension=0, tiled=False)
        first_block = both
        d_in = bf(behind(residual[: 2 * rows], first_block).astype(F32) + scattered(*pieces))
        with jax.named_scope("dx"):
            came = hop_two(d_in[rows:])
            in_order = chosen == 0
            both = jnp.stack([jnp.where(in_order, d_in[:rows], came), jnp.where(in_order, came, d_in[:rows])])
            half_width = width // 2
            mine = lax.dynamic_slice_in_dim(both, section * half_width, half_width, 2)
            other = lax.dynamic_slice_in_dim(both, (1 - section) * half_width, half_width, 2)
            other = over_core(other)
            ordered = jnp.where(first, jnp.concatenate([mine, other]), jnp.concatenate([other, mine]))
            input_grad = jnp.transpose(ordered, (1, 0, 2))
        def shares_of(name):
            mine = [got[name, layer] for layer in range(2)]
            return [mine[0], over_core(mine[0]), mine[1], over_core(mine[1])]

        with jax.named_scope("fg"):
            exp_row, contract, expand = place_feed(order.tie(counts), shares_of("feed"))
            order.mark(contract)
        with jax.named_scope("tg"):
            got["attn", 0] = behind(got["attn", 0], contract)
            in_row, norms, inproj, outproj = place_attn(order.tie(counts), shares_of("attn"))
        exp_row, in_row = exp_row[0], in_row[0]
    else:
        first_block = in_rows
        d_in = bf(behind(residual[: 2 * rows], first_block).astype(F32) + scattered(*pieces))
        with jax.named_scope("dx"):
            came = hop_two(d_in[rows:])
            in_order = chosen == 0
            both = jnp.stack([jnp.where(in_order, d_in[:rows], came), jnp.where(in_order, came, d_in[:rows])])
            half_width = width // 2
            mine = lax.dynamic_slice_in_dim(both, section * half_width, half_width, 2)
            other = lax.dynamic_slice_in_dim(both, (1 - section) * half_width, half_width, 2)
            other = over_core(other)
            ordered = jnp.where(first, jnp.concatenate([mine, other]), jnp.concatenate([other, mine]))
            input_grad = jnp.transpose(ordered, (1, 0, 2))
        contract, expand = reduce_plain(plain.feed, section, 1)
        attn_sum = reduce_plain(plain.attn, section, 1)[0]
        inproj = jnp.transpose(attn_sum[:, :cut].reshape(-1, 3, local), (1, 0, 2))
        outproj = jnp.transpose(attn_sum[:, cut:])
        biases = lax.psum(jnp.stack(plain.bias), (SECTION, DP))
        exp_row, in_row = jnp.where(first, biases[0], biases[1])
        norms = lax.psum(norm_rows, (HEADS, SECTION, DP))
        norms = jnp.where(first, norms[:6], norms[6:])
    loss_total = scalar_row[0, 0]
    rms_values = jnp.sqrt(scalar_row[0, 2:8].reshape(2, 3) / (scalar_row[0, 1] * width))
    piece = width // (dp_count * lax.axis_size(HEADS))
    norms = lax.dynamic_slice_in_dim(norms, (data * lax.axis_size(HEADS) + head) * piece, piece, 1)
    exp_shape, in_shape = online_expbias.shape, online_inbias.shape
    grad_expbias = lax.dynamic_slice_in_dim(
        exp_row.reshape(exp_shape), data * (exp_shape[2] // dp_count), exp_shape[2] // dp_count, 2
    )
    grad_inbias = lax.dynamic_slice_in_dim(
        in_row[: 2 * local].reshape(in_shape),
        data * (in_shape[3] // dp_count),
        in_shape[3] // dp_count,
        3,
    )
    return (
        loss_total,
        input_grad,
        jnp.transpose(inproj, (1, 0, 2))[None],
        grad_inbias,
        outproj[None],
        norms[None, 0:2],
        norms[None, 2:6],
        expand[None],
        grad_expbias,
        jnp.transpose(contract)[None],
        rms_values,
    )


def solution(mesh):
    placed = (
        P(HEADS, DP, None),
        P(HEADS, DP, None),
        P(DP, None),
        P(DP),
        P(DP, None),
        P(SECTION, None, None, HEADS),
        P(SECTION, None, HEADS, None),
        P(SECTION, HEADS, None),
        P(SECTION, None, None),
        P(SECTION, None, None),
        P(SECTION, None, HEADS),
        P(SECTION, HEADS, None),
        P(SECTION, HEADS, None),
        P(SECTION, None, None, HEADS),
        P(SECTION, None, HEADS, None),
        P(SECTION, HEADS, None),
        P(SECTION, None, None),
        P(SECTION, None, None),
        P(SECTION, None, HEADS),
        P(SECTION, HEADS, None),
        P(SECTION, HEADS, None),
    )
    return jax.shard_map(
        per_device,
        mesh=mesh,
        in_specs=placed,
        out_specs=(
            P(),
            P(HEADS, DP, SECTION),
            P(SECTION, DP, None, HEADS),
            P(SECTION, None, HEADS, DP),
            P(SECTION, HEADS, DP),
            P(SECTION, None, (DP, HEADS)),
            P(SECTION, None, (DP, HEADS)),
            P(SECTION, DP, HEADS),
            P(SECTION, HEADS, DP),
            P(SECTION, HEADS, DP),
            P(),
        ),
        check_vma=False,
    )
```

```python
import functools
import types

import jax
import jax.numpy as jnp
from jax import lax
from jax.experimental import pallas as pl
from jax.experimental.pallas import tpu as pltpu
from jax.sharding import PartitionSpec as P

TEMPER = 0.05
NORM_EPS = 1e-06
NEG_FILL = -1000000000.0
F32 = jnp.float32
LOW = jnp.bfloat16
HEADS, SECTION, DP = "heads", "section", "dp"
VMEM_SPARE = 6 * 1024 * 1024
EXTRA = 16

ROW_GAIN = 0
ROW_SHIFT = 2
ROW_EXP = 6
ROW_IN = 7


def dot_nn(a, b):
    return lax.dot_general(a, b, (((1,), (0,)), ((), ())), preferred_element_type=F32)


def dot_nt(a, b):
    return lax.dot_general(a, b, (((1,), (1,)), ((), ())), preferred_element_type=F32)


def dot_tn(a, b):
    return lax.dot_general(a, b, (((0,), (0,)), ((), ())), preferred_element_type=F32)


def bytes_of(shape, dtype):
    return functools.reduce(lambda x, y: x * y, shape, 1) * jnp.dtype(dtype).itemsize


class Loaded:
    def __init__(self, source, buffer, sem):
        self.copy = pltpu.make_async_copy(source, buffer, sem)
        self.copy.start()
        self.buffer = buffer
        self.shape = buffer.shape
        self.waiting = True

    def ready(self):
        if self.waiting:
            self.copy.wait()
            self.waiting = False
        return self.buffer

    def __getitem__(self, index):
        return self.ready()[index]

    @property
    def at(self):
        return self.ready().at


class Stored:
    def __init__(self, target, buffer, sems):
        self.target, self.buffer, self.sems = target, buffer, sems
        self.shape, self.dtype = buffer.shape, buffer.dtype
        self.copies = []

    def __setitem__(self, index, value):
        self.buffer[index] = value

    def send(self, start=0, size=None):
        run = pl.ds(start, self.shape[0] if size is None else size)
        copy = pltpu.make_async_copy(
            self.buffer.at[run], self.target.at[run], self.sems.at[len(self.copies)]
        )
        copy.start()
        self.copies.append(copy)

    def finish(self):
        for copy in self.copies:
            copy.wait()


def kernel_call(
    body, outs, scalars, arrays, flops, name, loads=(), stores=(), distant=(), weights=0
):
    side = distant[-1].shape[-1] if weights else 0
    buffers = [(a.shape, a.dtype) for a in loads] + list(stores)
    if weights:
        buffers.append(((weights, side, side), LOW))
    held = sum(bytes_of(*x) for x in [(a.shape, a.dtype) for a in arrays] + list(outs) + buffers)
    sems = [pltpu.SemaphoreType.DMA((max(1, len(loads) + 2 * len(stores)),))]
    if weights:
        sems.append(pltpu.SemaphoreType.DMA((2 * weights,)))
    counts = [len(scalars), len(arrays), len(loads), len(distant), len(outs), len(stores)]

    def whole(*refs):
        groups = []
        for count in counts + [len(loads), len(stores)]:
            groups.append(list(refs[:count]))
            refs = refs[count:]
        scal, near, load_r, far, out_r, store_r, load_b, store_b = groups
        extra = list(refs[:1]) if weights else []
        sem = refs[1] if weights else refs[0]
        loaded = [Loaded(a, b, sem.at[i]) for i, (a, b) in enumerate(zip(load_r, load_b))]
        base = len(loaded)
        stored = [
            Stored(a, b, sem.at[pl.ds(base + 2 * i, 2)]) for i, (a, b) in enumerate(zip(store_r, store_b))
        ]
        if weights:
            extra.append(refs[2])
        body(*scal, *near, *loaded, *far, *out_r, *stored, *extra)
        for item in loaded:
            item.ready()
        for item in stored:
            if not item.copies:
                item.send()
        for item in stored:
            item.finish()

    hbm = pl.BlockSpec(memory_space=pltpu.HBM)
    vmem = pl.BlockSpec(memory_space=pltpu.VMEM)
    in_specs = [pl.BlockSpec(memory_space=pltpu.SMEM)] * len(scalars)
    in_specs += [vmem] * len(arrays) + [hbm] * (len(loads) + len(distant))
    apart = [pltpu.with_memory_space_constraint(d, pltpu.HBM) for d in [*loads, *distant]]
    return pl.pallas_call(
        whole,
        out_shape=[jax.ShapeDtypeStruct(s, d) for s, d in outs]
        + [pltpu.HBM(s, d) for s, d in stores],
        in_specs=in_specs,
        out_specs=[vmem] * len(outs) + [hbm] * len(stores),
        scratch_shapes=[pltpu.VMEM(s, d) for s, d in buffers] + sems,
        compiler_params=pltpu.CompilerParams(vmem_limit_bytes=held + VMEM_SPARE),
        cost_estimate=pl.CostEstimate(flops=flops, bytes_accessed=held, transcendentals=0),
        name=name,
    )(*scalars, *arrays, *apart)


def here():
    head, core, data = [lax.axis_index(a) for a in (HEADS, SECTION, DP)]
    near = jnp.where(core == 0, 1, 2)
    chosen = jnp.where(core == 0, head // 2, head % 2)
    return types.SimpleNamespace(head=head, core=core, data=data, near=near, chosen=chosen)


def count_of(at, counts, encoder, other=0):
    return counts[2 * at.core + jnp.bitwise_xor(at.chosen, other), encoder]


def table_row(at, tables, layer, encoder, row):
    held, came = [t[encoder, row : row + 1, :] for t in tables]
    return jnp.where(at.core == layer, held, came)


def start_fetch(at, layer, held, arrived, target, sem):
    @pl.when(at.core == layer)
    def _():
        pltpu.make_async_copy(held, target, sem).start()

    @pl.when(at.core != layer)
    def _():
        pltpu.make_async_copy(arrived, target, sem).start()

    return pltpu.make_async_copy(held, target, sem)


def start_copy(source, target, sem):
    copy = pltpu.make_async_copy(source, target, sem)
    copy.start()
    return copy


def fetch_attn(at, layer, encoder, refs, scratch, sems):
    cols, outp, cols_too, outp_too = refs[:4]
    cut = cols.shape[0]
    waits = [
        start_fetch(at, layer, cols, cols_too, scratch.at[0, pl.ds(0, cut)], sems.at[0]),
        start_fetch(at, layer, outp, outp_too, scratch.at[0, pl.ds(cut, outp.shape[0])], sems.at[1]),
    ]
    if len(refs) > 4:
        waits.append(start_copy(refs[4], scratch.at[1], sems.at[2]))
    return waits


def fetch_feed(at, layer, refs, scratch, sems):
    exp, con, exp_too, con_too = refs
    return [
        start_fetch(at, layer, exp, exp_too, scratch.at[0], sems.at[0]),
        start_fetch(at, layer, con, con_too, scratch.at[1], sems.at[1]),
    ]


def swap(value, axis, distance):
    count = lax.axis_size(axis)
    return lax.ppermute(value, axis, [(i, i ^ distance) for i in range(count)])


def hop(value, first_core, second_core):
    count = lax.axis_size(HEADS)
    route = [(i, i ^ first_core) for i in range(count)]
    route += [(count + i, count + (i ^ second_core)) for i in range(count)]
    return lax.ppermute(value, (SECTION, HEADS), route)


def hop_one(value):
    return hop(value, 1, 2)


def hop_two(value):
    return hop(value, 2, 1)


def hop_both(value):
    return hop(value, 3, 3)


def over_core(value):
    return swap(value, SECTION, 1)


def behind(value, mark):
    return lax.optimization_barrier((value, mark))[0]


class Order:
    def __init__(self):
        self.last = None

    def tie(self, value):
        return value if self.last is None else behind(value, self.last)

    def mark(self, value):
        self.last = value


def bf(value):
    return value.astype(LOW)


def norm_parts(values):
    mean = jnp.mean(values, axis=-1, keepdims=True)
    center = values - mean
    spread = jnp.mean(center * center, axis=-1, keepdims=True)
    rstd = lax.rsqrt(spread + NORM_EPS)
    return center * rstd, rstd


def row_position(at, rows, shape, other):
    block_rows = rows // 2
    lane = lax.broadcasted_iota(jnp.int32, shape, 0 if shape[1] == 1 else 1)
    slot = lane // block_rows
    far = 3 - at.near
    block = jnp.bitwise_xor(jnp.bitwise_xor(at.head, other * far), (slot & 1) * far)
    block = jnp.bitwise_xor(block, (slot // 2) * at.near)
    return block * block_rows + lane - slot * block_rows


def row_keep(at, counts, encoder, rows):
    return row_position(at, rows, (rows, 1), 0) < count_of(at, counts, encoder)


def key_keep(at, counts, encoder, rows, other):
    return row_position(at, rows, (1, 2 * rows), other) < count_of(at, counts, encoder, other)


def row_groups(sources):
    if len(sources) == 2:
        return [list(sources)] * 2
    if len(sources[0].shape) == 2:
        own, one, two, far = sources
        return [[own, one], [two, far]]
    own, one, two, far = sources
    return [
        [own.at[0], two.at[1], one.at[0], far.at[1]],
        [two.at[0], own.at[1], far.at[0], one.at[1]],
    ]


def stack_rows(group):
    return jnp.concatenate([piece[...] for piece in group], axis=0)


def put_rows(targets, outs):
    if len(targets) == 4:
        half = outs[0].shape[0] // 2
        values = [outs[0][:half], outs[0][half:], outs[1][:half], outs[1][half:]]
    else:
        total = outs[0] + outs[1]
        half = total.shape[0] // 2
        values = [total[:half], total[half:]]
    for target, value in zip(targets, values):
        target[...] = value.astype(target.dtype)


def parts_shapes(rows, width, count):
    return [((rows, width), F32)] + [((rows, width), LOW)] * (count - 1)


def rows_of(sources):
    shape = sources[0].shape
    return (2 * shape[1], shape[2]) if len(shape) == 3 else shape


def attn_forward(counts, sources, tables, theirs, weights, layer, encoder, save):
    wide = len(sources) == 4
    rows, width = rows_of(sources)
    local = width // 4
    heads = local // 64
    full = 2 * rows
    count = len(sources)

    def body(s, *refs):
        at = here()
        tb, th_r, source, refs = refs[:2], refs[2], refs[3 : 3 + count], refs[3 + count :]
        w_refs, refs = refs[: len(weights)], refs[len(weights) :]
        targets, kept, (w_r, sems) = refs[:count], refs[count:-2], refs[-2:]
        waits = fetch_attn(at, layer, encoder, w_refs, w_r, sems)
        groups = row_groups(source)
        outs = []
        for unit in range(2):
            side = 0 if wide else unit
            rows_in = stack_rows(groups[unit])
            keep = key_keep(at, s, encoder, rows, unit if wide else 0)
            bias = th_r[...] if side else table_row(at, tb, layer, encoder, ROW_IN)
            if unit == 0:
                waits[0].wait()
            elif not wide:
                waits[2].wait()
            project = dot_nt(rows_in, w_r[side, : 3 * local, :])
            q = bf(project[:, :local] + bias[:, :local])
            k = bf(project[:, local : 2 * local])
            v = bf(project[:, 2 * local :] + bias[:, local : 2 * local])
            if save:
                kept[0][unit, :, :local] = q
                kept[0][unit, :, local : 2 * local] = k
                kept[0][unit, :, 2 * local :] = v
                kept[0].send(unit, 1)
            pieces = []
            for h in range(heads):
                cut = slice(64 * h, 64 * h + 64)
                scores = jnp.where(keep, dot_nt(q[:, cut] * 0.125, k[:, cut]), NEG_FILL)
                raised = jnp.exp(scores - jnp.max(scores, axis=-1, keepdims=True))
                shares = bf(raised / jnp.sum(raised, axis=-1, keepdims=True))
                if save:
                    kept[1][unit * heads + h] = shares
                pieces.append(bf(dot_nn(shares, v[:, cut])))
            context = jnp.concatenate(pieces, axis=1)
            if save:
                kept[2][unit] = context
                kept[1].send(unit * heads, heads)
                kept[2].send(unit, 1)
            if unit == 0:
                waits[1].wait()
            outs.append(dot_nn(context, w_r[side, 3 * local :, :]))
        put_rows(targets, outs)

    outs, stores = parts_shapes(rows, width, count), []
    if save:
        stores = [
            ((2, full, 3 * local), LOW),
            ((2 * heads, full, full), LOW),
            ((2, full, local), LOW),
        ]
    flops = 4 * full * (4 * local * width + 2 * local * full)
    got = kernel_call(
        body,
        outs,
        [counts],
        tables + [theirs] + sources,
        flops,
        "attn_forward",
        [],
        stores,
        weights,
        1 if wide else 2,
    )
    return got[:count], got[count:]


def feed_forward(counts, sources, tables, weights, layer, encoder, save):
    rows, width = rows_of(sources)
    units = weights[0].shape[1]
    full = 2 * rows
    count = len(sources)

    def body(s, *refs):
        at = here()
        tb, source, refs = refs[:2], refs[2 : 2 + count], refs[2 + count :]
        w_refs, refs = refs[: len(weights)], refs[len(weights) :]
        targets, kept, (w_r, sems) = refs[:count], refs[count:-2], refs[-2:]
        waits = fetch_feed(at, layer, w_refs, w_r, sems)
        groups = row_groups(source)
        bias = table_row(at, tb, layer, encoder, ROW_EXP)
        outs = []
        for unit in range(2):
            rows_in = stack_rows(groups[unit])
            if unit == 0:
                waits[0].wait()
            inner = dot_nn(rows_in, w_r[0]) + bias
            phi = 0.5 * (1.0 + lax.erf(inner * (0.5**0.5)))
            active = bf(inner * phi)
            if save:
                density = jnp.exp(-0.5 * inner * inner) * 0.3989422804014327
                kept[0][unit] = active
                kept[1][unit] = bf(phi + inner * density)
                kept[0].send(unit, 1)
                kept[1].send(unit, 1)
            if unit == 0:
                waits[1].wait()
            outs.append(dot_nn(active, w_r[1]))
        put_rows(targets, outs)

    outs, stores = parts_shapes(rows, width, count), []
    if save:
        stores = [((2, full, units), LOW), ((2, full, units), LOW)]
    flops = 8 * full * width * units
    near = tables + sources
    got = kernel_call(body, outs, [counts], near, flops, "feed_forward", [], stores, weights, 2)
    return got[:count], got[count:]


def masked_squares(at, counts, encoder, values, rows):
    return column_sum(jnp.where(row_keep(at, counts, encoder, rows), values * values, 0.0))


def norm_middle(counts, pieces, layer_in, tables, layer, encoder, save):
    rows, width = pieces[0].shape
    count, inputs = len(pieces), len(layer_in)

    def body(s, *refs):
        at = here()
        tb, added, refs = refs[:2], refs[2 : 2 + count], refs[2 + count :]
        x_refs, refs = refs[:inputs], refs[inputs:]
        (square_r, low_r, mixed_r) = refs if save else (None, refs[0], None)
        if inputs == 1:
            rows_in = x_refs[0][...]
        else:
            rows_in = jnp.concatenate([x_refs[0][0], x_refs[1][1]], axis=0)
        attn = scattered(*added) + table_row(at, tb, layer, encoder, ROW_SHIFT)
        mixed = rows_in.astype(F32) + attn
        if save:
            mixed_r[...] = mixed
            mixed_r.send()
        xhat, _ = norm_parts(mixed)
        gain = table_row(at, tb, layer, encoder, ROW_GAIN)
        low_r[...] = bf(xhat * gain + table_row(at, tb, layer, encoder, ROW_SHIFT + 1))
        if save:
            square_r[...] = masked_squares(at, s, encoder, attn, rows)

    outs, stores = [((rows, width), LOW)], []
    if save:
        outs, stores = [((1, width), F32)] + outs, [((rows, width), F32)]
    near = tables + pieces + layer_in
    return kernel_call(body, outs, [counts], near, 20 * rows * width, "norm_middle", [], stores)


def norm_last(counts, pieces, hidden, tables, layer, encoder, save):
    rows, width = hidden.shape
    count = len(pieces)
    pool = layer == 1

    def body(s, *refs):
        at = here()
        tb, added, h_r, refs = refs[:2], refs[2 : 2 + count], refs[2 + count], list(refs[3 + count :])
        out_r = refs.pop(0)
        square_r = refs.pop(0) if save else None
        feed = scattered(*added) + table_row(at, tb, layer, encoder, ROW_SHIFT + 2)
        summed = h_r[...].astype(F32) + feed
        if save:
            refs[0][...] = summed
            refs[0].send()
        xhat, _ = norm_parts(summed)
        gain = table_row(at, tb, layer, encoder, ROW_GAIN + 1)
        out = xhat * gain + table_row(at, tb, layer, encoder, ROW_SHIFT + 3)
        if pool:
            out_r[...] = column_sum(jnp.where(row_keep(at, s, encoder, rows), out, 0.0))
        else:
            out_r[...] = bf(out)
        if save:
            square_r[0:1, :] = masked_squares(at, s, encoder, feed, rows)
            square_r[1:2, :] = masked_squares(at, s, encoder, out, rows)

    outs, stores = [((1, width), F32) if pool else ((rows, width), LOW)], []
    if save:
        outs, stores = outs + [((2, width), F32)], [((rows, width), F32)]
    near = tables + pieces + [hidden]
    return kernel_call(body, outs, [counts], near, 20 * rows * width, "norm_last", [], stores)


def gather(own, wide):
    hops = (hop_one, hop_two, hop_both) if wide else (hop_one,)
    return [own] + [move(own) for move in hops]


def scatter(part, *others):
    hops = (hop_one, hop_two, hop_both)
    return [part] + [move(value) for move, value in zip(hops, others)]


def scattered(part, *others):
    total = part[...].astype(F32)
    for value in others:
        total = total + value[: part.shape[0], :].astype(F32)
    return total


def norm_backward(values, grad, gain_row):
    xhat, rstd = norm_parts(values)
    scaled = grad * gain_row
    d_values = rstd * (
        scaled
        - jnp.mean(scaled, axis=-1, keepdims=True)
        - xhat * jnp.mean(scaled * xhat, axis=-1, keepdims=True)
    )
    return d_values, jnp.sum(grad * xhat, axis=0, keepdims=True)


def column_sum(values):
    return jnp.sum(values, axis=0, keepdims=True)


def norm_gradient(y_r, grad, gain, low_r):
    d_values, d_gain = norm_backward(y_r[...], grad, gain)
    low_r[...] = bf(d_values)
    return d_gain, column_sum(grad), column_sum(d_values)


def last_backward(counts, summed, tables, layer, pooled=None, residual=None, pieces=None):
    rows, width = summed.shape
    near = [pooled] if pooled is not None else [residual] + pieces[1:]
    loads = [summed] if pooled is not None else [summed, pieces[0]]
    inputs = len(near)

    def body(s, held_r, came_r, *rest):
        at = here()
        near_r, (y_r, *part_r), (rows_r, low_r) = rest[:inputs], rest[inputs:-2], rest[-2:]
        if pooled is not None:
            grad = jnp.where(row_keep(at, s, 0, rows), near_r[0][...], 0.0)
        else:
            grad = bf(scattered(part_r[0], *near_r)).astype(F32)
        gain = table_row(at, (held_r, came_r), layer, 0, ROW_GAIN + 1)
        for i, row in enumerate(norm_gradient(y_r, grad, gain, low_r)):
            rows_r[i : i + 1, :] = row

    outs = [((3, width), F32), ((rows, width), LOW)]
    got = kernel_call(
        body, outs, [counts], tables + near, 30 * summed.size, "last_backward", loads
    )
    return got[1], got[0]


def middle_backward(counts, mixed, tables, layer, residual, pieces, last_rows, above, ride):
    rows, width = mixed.shape
    known = [last_rows] + above
    total = 6 + 6 * len(above)

    def body(s, held_r, came_r, *rest):
        at = here()
        last_r, above_r, rest = rest[0], rest[1 : len(known)], rest[len(known) :]
        near_r, (y_r, part_r, rows_r, low_r) = rest[:-4], rest[-4:]
        grad = scattered(part_r, *near_r)
        gain = table_row(at, (held_r, came_r), layer, 0, ROW_GAIN)
        d_gain, in_sum, out_sum = norm_gradient(y_r, grad, gain, low_r.at[pl.ds(0, rows)])
        last = [last_r[i : i + 1, :] for i in range(3)]
        for i, row in enumerate((d_gain, last[0], out_sum, in_sum, last[2], last[1])):
            rows_r[i : i + 1, :] = row
        if above_r:
            rows_r[6:, :] = above_r[0][...]
        if ride:
            spare = jnp.zeros((EXTRA - total, width), F32)
            low_r[rows:, :] = bf(jnp.concatenate([rows_r[...], spare], axis=0))

    outs = [((total, width), F32), ((rows + EXTRA * ride, width), LOW)]
    near = tables + known + [residual] + pieces[1:]
    loads = [mixed, pieces[0]]
    got = kernel_call(body, outs, [counts], near, 30 * mixed.size, "middle_backward", loads)
    return got[1], got[0]


def feed_backward(counts, grads, slope, weights, layer):
    full, units = slope.shape[1:]
    rows, width = grads[0].shape
    count = len(grads)

    def body(s, *refs):
        source, sl_r, refs = refs[:count], refs[count], refs[count + 1 :]
        w_refs, refs = refs[: len(weights)], refs[len(weights) :]
        others, (bias_r, part, dinner_r, w_r, sems) = refs[: count - 1], refs[count - 1 :]
        targets = [part, *others]
        waits = fetch_feed(here(), layer, w_refs, w_r, sems)
        groups = row_groups(source)
        outs = []
        total = jnp.zeros((1, units), F32)
        for unit in range(2):
            if unit == 0:
                waits[1].wait()
            d_inner = dot_nt(stack_rows(groups[unit]), w_r[1]) * sl_r[unit].astype(F32)
            total = total + column_sum(d_inner)
            low = bf(d_inner)
            dinner_r[unit] = low
            dinner_r.send(unit, 1)
            if unit == 0:
                waits[0].wait()
            outs.append(dot_nt(low, w_r[0]))
        bias_r[...] = total
        put_rows(targets, outs)

    part, *outs = [((rows, width), LOW)] * count
    outs, stores = outs + [((1, units), F32)], [part, ((2, full, units), LOW)]
    flops = 8 * full * width * units
    got = kernel_call(
        body, outs, [counts], grads, flops, "feed_backward", [slope], stores, weights, 2
    )
    return [got[count], *got[: count - 1], got[count + 1], got[count - 1]]


def attn_backward(counts, grads, qkv, shares, context, weights, layer):
    wide = len(grads) == 4
    full, triple = qkv.shape[1:]
    local = triple // 3
    heads = local // 64
    rows, width = full // 2, grads[0].shape[1]
    count = len(grads)

    def body(s, *refs):
        source, refs = [g.at[pl.ds(0, rows)] for g in refs[:count]], refs[count:]
        (qkv_r, sh_r, cx_r), refs = refs[:3], refs[3:]
        w_refs, refs = refs[: len(weights)], refs[len(weights) :]
        others, (bias_r, part, dproj_r, w_r, sems) = refs[: count - 1], refs[count - 1 :]
        targets = [part, *others]
        waits = fetch_attn(here(), layer, 0, w_refs, w_r, sems)
        groups = row_groups(source)
        bias_r[...] = jnp.zeros((2, width), F32)
        outs = []
        for unit in range(2):
            side = 0 if wide else unit
            if unit == 0:
                waits[1].wait()
            elif not wide:
                waits[2].wait()
            d_context = bf(dot_nt(stack_rows(groups[unit]), w_r[side, triple:, :]))
            q = qkv_r[unit, :, :local]
            k = qkv_r[unit, :, local : 2 * local]
            v = qkv_r[unit, :, 2 * local :]
            weighted = d_context.astype(F32) * cx_r[unit].astype(F32)
            dqs, dks, dvs = [], [], []
            for h in range(heads):
                cut = slice(64 * h, 64 * h + 64)
                share = sh_r[unit * heads + h]
                dc = d_context[:, cut]
                dvs.append(dot_tn(share, dc))
                drop = jnp.sum(weighted[:, cut], axis=-1, keepdims=True)
                d_scores = bf(share.astype(F32) * (dot_nt(dc, v[:, cut]) - drop))
                dqs.append(dot_nn(d_scores, k[:, cut]) * 0.125)
                dks.append(dot_tn(d_scores, q[:, cut]) * 0.125)
            dq = jnp.concatenate(dqs, axis=1)
            dk = jnp.concatenate(dks, axis=1)
            dv = jnp.concatenate(dvs, axis=1)
            bias_r[unit : unit + 1, :local] = column_sum(dq)
            bias_r[unit : unit + 1, local : 2 * local] = column_sum(dv)
            d_project = bf(jnp.concatenate([dq, dk, dv], axis=1))
            dproj_r[unit] = d_project
            dproj_r.send(unit, 1)
            if unit == 0:
                waits[0].wait()
            outs.append(dot_nn(d_project, w_r[side, :triple, :]))
        put_rows(targets, outs)

    part = ((rows, width), LOW)
    outs = [((rows, width), LOW)] * (count - 1)
    outs, stores = outs + [((2, width), F32)], [part, ((2, full, triple), LOW)]
    flops = 4 * full * (4 * local * width + 4 * local * full)
    loads = [qkv, shares, context]
    side = 1 if wide else 2
    got = kernel_call(
        body, outs, [counts], grads, flops, "attn_backward", loads, stores, weights, side
    )
    return [got[count], *got[: count - 1], got[count + 1], got[count - 1]]


def put_blocks(at, out_ref, parts, extra, blocks, other):
    if extra.shape[0] < EXTRA:
        extra = jnp.concatenate([extra, jnp.zeros((EXTRA - extra.shape[0], extra.shape[1]), F32)], axis=0)
    extra = bf(extra)
    span = parts[0].shape[0] // blocks
    half = span // 2
    wanted = jnp.bitwise_xor(at.core, other)
    for block in range(blocks):
        for i, value in enumerate(parts):
            halves = [bf(value[block * span + j * half : block * span + (j + 1) * half]) for j in range(2)]
            out_ref[block, i * half : (i + 1) * half, :] = jnp.where(wanted == 0, *halves)
        out_ref[block, len(parts) * half :, :] = extra


def weight_grads(counts, grads, inputs, pairs, bias, blocks, name):
    count = len(grads)
    width = grads[0].shape[-1]
    attention = name == "attn_weights"
    columns = sum(p.shape[2] for p in pairs) if attention else pairs[0].shape[2]
    parts_count = 1 if attention else 2

    def body(s, *refs):
        at = here()
        bias_r, g_refs, refs = refs[0], refs[1 : 1 + count], refs[1 + count :]
        x_refs, (o_r, d_r), targets = refs[:count], refs[count : count + 2], refs[count + 2 :]
        half = pairs[0].shape[1] // 2
        g_rows = [stack_rows(g) for g in row_groups([g.at[pl.ds(0, half)] for g in g_refs])]
        back = dot_tn(g_rows[0], o_r[0]) + dot_tn(g_rows[1], o_r[1])
        x_rows = [stack_rows(x) for x in row_groups(x_refs)]
        ahead = dot_tn(x_rows[0], d_r[0]) + dot_tn(x_rows[1], d_r[1])
        row = bias_r[0:1, :] + bias_r[1:2, :] if bias_r.shape[0] == 2 else bias_r[...]
        parts = [jnp.concatenate([ahead, back], axis=1)] if attention else [back, ahead]
        if blocks > 1:
            put_blocks(at, targets[0], parts, row, blocks, 1)
            put_blocks(at, targets[1], parts, row, blocks, 0)
        else:
            for i, part in enumerate(parts):
                targets[0][i] = bf(part)

    if blocks > 1:
        shape = (blocks, parts_count * (width // blocks // 2) + EXTRA, columns)
        outs, stores = [(shape, LOW)], [(shape, LOW)]
    else:
        outs, stores = [((parts_count, width, columns), LOW)], []
    flops = sum(4 * p.shape[1] * width * p.shape[2] for p in pairs)
    loads = grads + inputs + pairs
    got = kernel_call(body, outs, [counts], [bias], flops, name, loads, stores)
    return [got[1], got[0]] if blocks > 1 else got


def add_cores(counts, mine, came, norms=(), arrived=()):
    blocks, rows = mine.shape[:2]
    start = rows - EXTRA

    def body(s, *refs):
        norm_r, (c_r, m_r, *arrived_r, out_r) = refs[: len(norms)], refs[len(norms) :]
        for block in range(blocks):
            total = m_r[block].astype(F32) + c_r[block].astype(F32)
            if norms:
                summed = norm_r[0][...]
                for piece in arrived_r:
                    rows_there = piece[piece.shape[0] - EXTRA :, :].astype(F32)
                    summed = summed + rows_there[: summed.shape[0]]
                spare = jnp.zeros((EXTRA - 1 - summed.shape[0], summed.shape[1]), F32)
                total = jnp.concatenate([total[: start + 1], summed, spare], axis=0)
            out_r[block] = bf(total)
            if block % 2:
                out_r.send(block - 1, 2)

    stores = [(mine.shape, LOW)]
    near, loads = [*norms, came], [mine, *arrived]
    return kernel_call(body, [], [counts], near, mine.size, "add_cores", loads, stores)[0]


def in_core_order(at, refs, start, size):
    run = slice(start, start + size)
    mine = jnp.where(at.core == 0, refs[0][run, :], refs[2][run, :]).astype(F32)
    other = jnp.where(at.core == 0, refs[1][run, :], refs[3][run, :]).astype(F32)
    own = at.core == 0
    return jnp.concatenate([jnp.where(own, mine, other), jnp.where(own, other, mine)], axis=0)


def own_row(at, refs, row):
    return jnp.where(at.core == 0, refs[0][row : row + 1, :], refs[2][row : row + 1, :]).astype(F32)


def place_feed(counts, shares):
    rows, width = shares[0].shape
    part = (rows - EXTRA) // 2

    def body(s, *refs):
        at = here()
        refs, (row_r, con_r, exp_r) = refs[:4], refs[4:]
        con_r[...] = in_core_order(at, refs, 0, part)
        con_r.send()
        exp_r[...] = in_core_order(at, refs, part, part)
        row_r[...] = own_row(at, refs, 2 * part)

    outs, stores = [((1, width), F32)], [((2 * part, width), F32)] * 2
    return kernel_call(
        body, outs, [counts], [], 4 * rows * width, "place_feed", shares, stores
    )


def place_attn(counts, shares):
    rows, width = shares[0].shape
    part = rows - EXTRA
    local = width // 4

    def body(s, *refs):
        at = here()
        refs, (row_r, norm_r, in_r, out_r) = refs[:4], refs[4:]
        both = in_core_order(at, refs, 0, part)
        for i in range(3):
            in_r[i] = both[:, i * local : (i + 1) * local]
        in_r.send()
        out_r[...] = both[:, 3 * local :].T
        row_r[...] = own_row(at, refs, part)
        norms = refs[0][part + 1 : part + 13, :].astype(F32) + refs[1][part + 1 : part + 13, :].astype(F32)
        norm_r[...] = jnp.where(at.core == 0, norms[:6], norms[6:])

    outs = [((1, width), F32), ((6, width), F32)]
    stores = [((3, 2 * part, local), F32), ((local, 2 * part), F32)]
    return kernel_call(
        body, outs, [counts], [], 4 * rows * width, "place_attn", shares, stores
    )


def reduce_plain(layers, section, axis):
    mine = jnp.where(section == 0, layers[0], layers[1]).astype(F32)
    other = over_core(jnp.where(section == 0, layers[1], layers[0]))
    low = bf(mine + other.astype(F32))
    return lax.psum_scatter(low, DP, scatter_dimension=axis, tiled=True).astype(F32)


def summed_over(value, axis):
    count = lax.axis_size(axis)
    distance = 1
    while distance < count:
        value = value + swap(value, axis, distance)
        distance *= 2
    return value


def by_distance(entries, axis):
    count = entries.shape[0]
    order = jnp.bitwise_xor(jnp.arange(count), lax.axis_index(axis))
    chosen = (order[:, None] == jnp.arange(count)[None, :]).astype(entries.dtype)
    flat = jnp.dot(chosen, entries.reshape(count, -1), precision=lax.Precision.HIGHEST)
    return flat.astype(entries.dtype).reshape(entries.shape)


def loss_section(pooled, counts, live, queue_unit):
    count = lax.axis_size(DP)
    width = pooled.shape[-1]
    with jax.named_scope("pool"):
        pooled = pooled + hop_one(pooled)
    vectors = pooled / counts[:, None]
    inverse = lax.rsqrt(jnp.sum(vectors * vectors, axis=-1, keepdims=True) + NORM_EPS)
    units = vectors * inverse
    low = bf(units)
    flags = jnp.broadcast_to(bf(live), (1, width))
    packet = jnp.concatenate([low, flags], axis=0)
    with jax.named_scope("keys"):
        if count <= 8:
            lanes = jnp.stack([packet] + [swap(packet, DP, r) for r in range(1, count)])
        else:
            lanes = by_distance(lax.all_gather(packet, DP, axis=0), DP)
    queries = lanes[:, 0]
    with jax.named_scope("keys"):
        every = jnp.stack([lanes[:, 1:], hop_two(lanes[:, 1:])])
        every = jnp.stack([every, over_core(every)]).reshape(4 * count, 2, width)
    keys, alive = every[:, 0], every[:, 1, 0].astype(F32)
    raised = jnp.exp(dot_nt(queries, queue_unit) / TEMPER)
    mass = jnp.sum(raised, axis=1, keepdims=True)
    pull = dot_nn(bf(raised), queue_unit)
    spread = jnp.concatenate([pull, jnp.broadcast_to(mass, (count, 128))], axis=1)
    with jax.named_scope("pull"):
        if count <= 8:
            total = spread[0:1]
            for r in range(1, count):
                total = total + swap(spread[r : r + 1], DP, r)
        else:
            placed = by_distance(spread, DP)
            total = lax.psum_scatter(placed, DP, scatter_dimension=0, tiled=True)
    positive = dot_nt(low[0:1], keys) / TEMPER
    positive = jnp.where(alive[None, :] > 0, positive, NEG_FILL)
    pos_raised = jnp.exp(positive)
    mass = total[0, width] + jnp.sum(pos_raised)
    own_pair = (jnp.arange(keys.shape[0])[None, :] == 0).astype(F32)
    weight = live / jnp.sum(alive)
    loss_part = weight * (jnp.log(mass) - positive[0, 0])
    d_positive = bf(weight * (pos_raised / mass - own_pair) / TEMPER)
    d_unit = dot_nn(d_positive, keys) + (weight / mass / TEMPER) * total[:, :width]
    unit = units[0:1]
    d_vector = inverse[0:1] * (d_unit - unit * jnp.sum(unit * d_unit, axis=-1, keepdims=True))
    return loss_part, d_vector / counts[0]


def unit_row(total, count):
    vector = total / count.astype(F32)
    inverse = lax.rsqrt(jnp.sum(vector * vector, axis=-1, keepdims=True) + NORM_EPS)
    return vector * inverse, inverse


def queue_units(counts, queue):
    def body(s, x_r, out_r):
        values = x_r[...].astype(F32)
        out_r[...] = bf(values * lax.rsqrt(jnp.sum(values * values, axis=-1, keepdims=True) + NORM_EPS))

    stores = [(queue.shape, LOW)]
    return kernel_call(body, [], [counts], [], 4 * queue.size, "queue_units", [queue], stores)[0]


def live_flag(at, live):
    return live[2 * at.core + at.chosen].astype(F32)


def unit_packet(counts, live, sums):
    width = sums[0].shape[1]

    def body(s, lv, q_r, qc_r, k_r, kc_r, out_r):
        at = here()
        query, _ = unit_row(q_r[...] + qc_r[...], count_of(at, s, 0))
        key, _ = unit_row(k_r[...] + kc_r[...], count_of(at, s, 1))
        flag = jnp.zeros((1, width), F32) + live_flag(at, lv)
        out_r[...] = bf(jnp.concatenate([query, key, flag], axis=0))

    return kernel_call(body, [((3, width), LOW)], [counts, live], sums, 8 * width, "unit_packet")[0]


def queue_scores(counts, lanes, queue):
    count = len(lanes)
    width = queue.shape[1]

    def body(s, *refs):
        lane_r, q_r, outs, key_r = refs[:count], refs[count], refs[count + 1 : -1], refs[-1]
        packets = [lane[...] for lane in lane_r]
        queries = jnp.concatenate([p[0:1] for p in packets], axis=0)
        raised = jnp.exp(dot_nt(queries, q_r[...]) / TEMPER)
        mass = jnp.sum(raised, axis=1, keepdims=True)
        pull = dot_nn(bf(raised), q_r[...])
        for i in range(count):
            outs[i][:, :width] = pull[i : i + 1]
            outs[i][:, width:] = jnp.zeros((1, 128), F32) + mass[i : i + 1]
        key_r[...] = jnp.concatenate([p[1:2] for p in packets] + [p[2:3] for p in packets], axis=0)

    outs = [((1, width + 128), F32)] * count + [((2 * count, width), LOW)]
    near = lanes + [queue]
    return kernel_call(body, outs, [counts], near, 4 * count * queue.size, "queue_scores")


def loss_end(counts, live, sums, keys, pulls, squares):
    width = sums[0].shape[1]
    rows = keys[0].shape[0] // 2
    n_keys, n_pulls = len(keys), len(pulls)

    def body(s, lv, q_r, qc_r, *refs):
        at = here()
        key_r, refs = refs[:n_keys], refs[n_keys:]
        pull_r, square_r, (grad_r, row_r) = refs[:n_pulls], refs[n_pulls:-2], refs[-2:]
        unit, inverse = unit_row(q_r[...] + qc_r[...], count_of(at, s, 0))
        low = bf(unit)
        total = pull_r[0][...]
        for piece in pull_r[1:]:
            total = total + piece[...]
        every = jnp.concatenate([k[0:rows] for k in key_r], axis=0)
        alive = jnp.concatenate([k[rows:] for k in key_r], axis=0).astype(F32)
        flags = dot_nt(jnp.ones((1, 128), F32), alive[:, :128]) * (1.0 / 128)
        positive = dot_nt(low, every) / TEMPER
        positive = jnp.where(flags > 0.5, positive, NEG_FILL)
        raised = jnp.exp(positive)
        mass = total[:, width : width + 1] + jnp.sum(raised, axis=-1, keepdims=True)
        weight = live_flag(at, lv) / jnp.sum(flags, axis=-1, keepdims=True)
        own = lax.broadcasted_iota(jnp.int32, positive.shape, 1) == 0
        self_logit = jnp.sum(jnp.where(own, positive, 0.0), axis=-1, keepdims=True)
        loss = weight * (jnp.log(mass) - self_logit)
        d_positive = bf(weight * (raised / mass - own.astype(F32)) / TEMPER)
        d_unit = dot_nn(d_positive, every) + (weight / mass / TEMPER) * total[:, :width]
        d_vector = inverse * (d_unit - unit * jnp.sum(unit * d_unit, axis=-1, keepdims=True))
        grad_r[...] = d_vector / count_of(at, s, 0).astype(F32)
        lane = lax.broadcasted_iota(jnp.int32, (1, 128), 1)
        tokens = 0.5 * count_of(at, s, 0).astype(F32)
        row = jnp.where(lane == 0, 0.5 * loss, jnp.where(lane == 1, tokens, 0.0))
        at_lane = 2
        for piece in square_r:
            values = jnp.sum(piece[...], axis=-1, keepdims=True)
            for i in range(piece.shape[0]):
                row = jnp.where(lane == at_lane, values[i : i + 1], row)
                at_lane += 1
        row_r[...] = row

    outs = [((1, width), F32), ((1, 128), F32)]
    arrays = sums + keys + pulls + squares
    return kernel_call(
        body, outs, [counts, live], arrays, 4 * n_keys * rows * width, "loss_end"
    )


def small_table(counts, encoders):
    width = encoders[0][0].shape[1]
    arrays = [a for e in encoders for a in e]

    def body(s, *refs):
        out_r = refs[-1]
        for e in range(2):
            gain_r, shift_r, exp_r, in_r = refs[4 * e : 4 * e + 4]
            out_r[e, ROW_GAIN : ROW_GAIN + 2, :] = gain_r[...].astype(F32)
            out_r[e, ROW_SHIFT : ROW_SHIFT + 4, :] = shift_r[...].astype(F32)
            groups, heads = exp_r.shape[0], in_r.shape[0]
            pieces = [exp_r[i : i + 1, :].astype(F32) for i in range(groups)]
            out_r[e, ROW_EXP : ROW_EXP + 1, :] = jnp.concatenate(pieces, axis=1)
            pieces = [in_r[h, i : i + 1, :].astype(F32) for i in range(2) for h in range(heads)]
            used = sum(p.shape[1] for p in pieces)
            pieces.append(jnp.zeros((1, width - used), F32))
            out_r[e, ROW_IN : ROW_IN + 1, :] = jnp.concatenate(pieces, axis=1)

    return kernel_call(body, [((2, 8, width), F32)], [counts], arrays, 64 * width, "small_table")[0]


def per_device(
    query_embed,
    key_embed,
    crop_counts,
    pair_mask,
    negative_queue,
    online_inproj,
    online_inbias,
    online_outproj,
    online_gains,
    online_shifts,
    online_expand,
    online_expbias,
    online_contract,
    momentum_inproj,
    momentum_inbias,
    momentum_outproj,
    momentum_gains,
    momentum_shifts,
    momentum_expand,
    momentum_expbias,
    momentum_contract,
):
    section = lax.axis_index(SECTION)
    head = lax.axis_index(HEADS)
    data = lax.axis_index(DP)
    dp_count = lax.axis_size(DP)
    rows, pairs_dev, width = query_embed.shape
    pairs = pairs_dev // lax.axis_size(SECTION)
    local = online_outproj.shape[1]
    blocks = dp_count if width % (dp_count * 32) == 0 and dp_count <= 8 else 1
    few = blocks > 1
    first = section == 0
    counts = crop_counts
    chosen = jnp.where(first, head // 2, head % 2)

    def pair_of(table, axis, pair):
        return lax.dynamic_index_in_dim(table, section * pairs + pair, axis, keepdims=False)

    order = Order()
    with jax.named_scope("in"):
        raw = []
        for table in (query_embed, key_embed):
            raw.append(jnp.stack([pair_of(table, 1, chosen), pair_of(table, 1, 1 - chosen)]))
    with jax.named_scope("ag0"):
        rows_first = [gather(r, True) for r in raw]
    order.mark(raw[1])

    held = [
        [
            jnp.transpose(inproj[0], (1, 2, 0)).reshape(3 * local, width),
            outproj[0],
            expand[0],
            contract[0],
        ]
        for inproj, outproj, expand, contract in (
            (online_inproj, online_outproj, online_expand, online_contract),
            (momentum_inproj, momentum_outproj, momentum_expand, momentum_contract),
        )
    ]
    with jax.named_scope("tab"):
        small = [
            [gains[0], shifts[0], expbias[0], jnp.transpose(inbias[0], (1, 0, 2))]
            for gains, shifts, expbias, inbias in (
                (online_gains, online_shifts, online_expbias, online_inbias),
                (momentum_gains, momentum_shifts, momentum_expbias, momentum_inbias),
            )
        ]
        table = small_table(order.tie(counts), small)
        order.mark(table)
        tables = [table, over_core(table)]
        neighbour_bias = jnp.where(first, tables[1], tables[0])[1, ROW_IN : ROW_IN + 1]
    with jax.named_scope("w"):
        came_weights = [[over_core(w) for w in held[e]] for e in range(2)]
        attn_sets = [held[e][:2] + came_weights[e][:2] for e in range(2)]
        feed_sets = [held[e][2:] + came_weights[e][2:] for e in range(2)]
    span = width // dp_count
    at_row = data * span
    cut = 3 * local

    def share_of(cols, outp):
        low_part = lax.dynamic_slice_in_dim(cols, jnp.minimum(at_row, cut - span), span, 0)
        high = lax.dynamic_slice_in_dim(outp, jnp.clip(at_row - cut, 0, local - span), span, 0)
        return jnp.where(at_row < cut, low_part, high)

    def layer_share(e):
        mine = share_of(held[e][0], held[e][1])
        other = share_of(came_weights[e][0], came_weights[e][1])
        return jnp.where(first, other, mine)

    with jax.named_scope("nb"):
        shares = layer_share(1)
    order.mark((order.last, shares))
    neighbour = types.SimpleNamespace()
    pooled_bias = jnp.zeros((1, width), F32)
    saved = [types.SimpleNamespace(), types.SimpleNamespace()]
    squares = []
    pooled = [None, None]

    def forward(e):
        save = e == 0
        layer_in = None
        for layer in range(2):
            if layer == 0:
                rows_in = rows_first[e]
                residual = [rows_in[0], rows_in[2]]
                attn_w, theirs = attn_sets[e], pooled_bias
            else:
                with jax.named_scope("ag1"):
                    rows_in = gather(layer_in, save)
                residual = [layer_in]
                attn_w, theirs = attn_sets[e], pooled_bias
                if not save:
                    attn_w, theirs = attn_w + [neighbour.attn], neighbour.bias
            yield
            parts, kept = attn_forward(
                order.tie(counts), rows_in, tables, theirs, attn_w, layer, e, save
            )
            order.mark(parts[0])
            with jax.named_scope("rs1"):
                pieces = scatter(*parts)
            if layer == 0 and e == 1:
                with jax.named_scope("nb"):
                    neighbour.bias = hop_two(behind(neighbour_bias, order.last))
                    neighbour.share = hop_two(behind(shares, order.last))
            yield
            *square, low = norm_middle(order.tie(counts), pieces, residual, tables, layer, e, save)
            if save:
                square, low, mixed = square[0], square[1], low
            order.mark(low)
            if layer == 0 and e == 1:
                with jax.named_scope("nb"):
                    share = behind(neighbour.share, order.last)
                    neighbour.attn = lax.all_gather(share, DP, axis=0, tiled=True)
            if save:
                vars(saved[layer]).update(
                    x=rows_in, qkv=kept[0], shares=kept[1], context=kept[2], mixed=mixed
                )
                squares.append(square)
            with jax.named_scope("ag2"):
                rows_in = gather(low, True)
            yield
            parts, kept = feed_forward(
                order.tie(counts), rows_in, tables, feed_sets[e], layer, e, save
            )
            order.mark(parts[0])
            with jax.named_scope("rs2"):
                pieces = scatter(*parts)
            yield
            outs = list(norm_last(order.tie(counts), pieces, low, tables, layer, e, save))
            out = outs.pop(0)
            order.mark(out)
            if save:
                vars(saved[layer]).update(hidden=rows_in, active=kept[0], slope=kept[1], summed=outs[1])
                squares.append(outs[0])
            layer_in = out
        pooled[e] = out

    threads = [forward(0), forward(1)]
    step = 0
    queue_unit = None
    while threads:
        for thread in list(threads):
            if next(thread, 0) == 0:
                threads.remove(thread)
        step += 1
        if step == 5 and few:
            queue_unit = queue_units(order.tie(counts), negative_queue)
            order.mark(queue_unit)

    with jax.named_scope("loss"):
        if few:
            sums = [pooled[0], hop_one(pooled[0]), pooled[1], hop_one(pooled[1])]
            packet = unit_packet(order.tie(counts), pair_mask, sums)
            lanes = [packet] + [swap(packet, DP, r) for r in range(1, dp_count)]
            *spread, keys = queue_scores(counts, lanes, queue_unit)
            pulls = [spread[0]] + [swap(spread[r], DP, r) for r in range(1, dp_count)]
            keys_two = [keys, hop_two(behind(keys, pulls[1]))]
            keys_all = keys_two + [over_core(k) for k in keys_two]
            d_pool, scalar_row = loss_end(counts, pair_mask, sums[:2], keys_all, pulls, squares)
        else:
            queue = negative_queue.astype(F32)
            norm = lax.rsqrt(jnp.sum(queue * queue, axis=-1, keepdims=True) + NORM_EPS)
            live = pair_of(pair_mask, 0, chosen).astype(F32)
            own_counts = pair_of(crop_counts, 0, chosen).astype(F32)
            both = jnp.concatenate(pooled)
            loss_part, d_pool = loss_section(both, own_counts, live, bf(queue * norm))
            branch = jnp.sum(jnp.concatenate(squares), axis=1)
            scalars = jnp.concatenate([jnp.stack([0.5 * loss_part, 0.5 * own_counts[0]]), branch])
            scalar_row = jnp.zeros((1, 128), F32).at[0, : scalars.shape[0]].set(scalars)

    scalar_hops = [(HEADS, 1), (HEADS, 2), (SECTION, 1)]
    distance = 1
    while distance < dp_count:
        scalar_hops.append((DP, distance))
        distance *= 2

    def scalar_steps(mark, count):
        nonlocal scalar_row
        with jax.named_scope("sc"):
            for _ in range(min(count, len(scalar_hops))):
                axis, far = scalar_hops.pop(0)
                tied = behind(scalar_row, mark)
                scalar_row = tied + swap(tied, axis, far)
        order.mark((order.last, scalar_row))

    order = Order()
    order.mark(d_pool)
    got = {}
    waiting, summed = [], {}

    def share_grads(name, mine, other):
        waiting.append((name, mine, other))

    def add_waiting():
        for name, mine, other in waiting:
            came = over_core(order.tie(other))
            both = add_cores(order.tie(counts), mine, came)
            order.mark(both)
            summed[name] = both
        waiting.clear()

    def reduce_summed(mark):
        for name, both in summed.items():
            with jax.named_scope("rg"):
                both = behind(both, (mark, list(got.values())[-1:]))
                got[name] = lax.psum_scatter(both, DP, scatter_dimension=0, tiled=False)
        summed.clear()

    residual, pieces, rows_above = None, None, []
    plain = types.SimpleNamespace(feed=[None, None], attn=[None, None], bias=[None, None])
    attn_w, feed_w = attn_sets[0], feed_sets[0]
    for layer in (1, 0):
        kept = saved[layer]
        source = dict(pooled=d_pool) if layer == 1 else dict(residual=residual, pieces=pieces)
        low, rows_last = last_backward(
            order.tie(counts), kept.summed, tables, layer, **source
        )
        order.mark(low)
        with jax.named_scope("ag3"):
            grads = gather(low, True)
        add_waiting()
        reduce_summed(grads[1])
        *parts, d_inner, exp_row = feed_backward(
            order.tie(counts), grads, kept.slope, feed_w, layer
        )
        order.mark(exp_row)
        with jax.named_scope("rs3"):
            pieces = scatter(*parts)
        feed_got = weight_grads(
            order.tie(counts),
            grads,
            kept.hidden,
            [kept.active, d_inner],
            exp_row,
            blocks,
            "feed_weights",
        )
        order.mark(feed_got[0])
        if few:
            share_grads(("feed", layer), *feed_got)
            scalar_steps(exp_row, 1)
            if layer == 0:
                add_waiting()
                reduce_summed(pieces[1:])
        low, norm_rows = middle_backward(
            order.tie(counts),
            kept.mixed,
            tables,
            layer,
            low,
            pieces,
            rows_last,
            rows_above,
            int(few and layer == 0),
        )
        residual = low
        order.mark(low)
        rows_above = [norm_rows]
        with jax.named_scope("ag4"):
            grads = gather(low, True)
        add_waiting()
        reduce_summed(grads[1:])
        *parts, d_project, in_rows = attn_backward(
            order.tie(counts),
            grads,
            kept.qkv,
            kept.shares,
            kept.context,
            attn_w,
            layer,
        )
        order.mark(in_rows)
        with jax.named_scope("rs4"):
            pieces = scatter(*parts)
        attn_got = weight_grads(
            order.tie(counts),
            grads,
            kept.x,
            [kept.context, d_project],
            in_rows,
            blocks,
            "attn_weights",
        )
        order.mark(attn_got[0])
        if few:
            scalar_steps(in_rows, 1)
            if layer == 1:
                share_grads(("attn", layer), *attn_got)
        else:
            plain.feed[layer] = feed_got[0]
            plain.attn[layer] = attn_got[0]
            plain.bias[layer] = jnp.concatenate([exp_row, in_rows[0:1] + in_rows[1:2]])

    if not few:
        scalar_steps(in_rows, len(scalar_hops))

    if few:
        with jax.named_scope("lg"):
            both = add_cores(
                order.tie(counts), attn_got[0], over_core(attn_got[1]), [norm_rows], grads[1:]
            )
            order.mark(both)
            scalar_steps(both, len(scalar_hops))
            got["attn", 0] = lax.psum_scatter(both, DP, scatter_dimension=0, tiled=False)
        first_block = both
        d_in = bf(behind(residual[: 2 * rows], first_block).astype(F32) + scattered(*pieces))
        with jax.named_scope("dx"):
            came = hop_two(d_in[rows:])
            in_order = chosen == 0
            both = jnp.stack([jnp.where(in_order, d_in[:rows], came), jnp.where(in_order, came, d_in[:rows])])
            half_width = width // 2
            mine = lax.dynamic_slice_in_dim(both, section * half_width, half_width, 2)
            other = lax.dynamic_slice_in_dim(both, (1 - section) * half_width, half_width, 2)
            other = over_core(other)
            ordered = jnp.where(first, jnp.concatenate([mine, other]), jnp.concatenate([other, mine]))
            input_grad = jnp.transpose(ordered, (1, 0, 2))
        def shares_of(name):
            mine = [got[name, layer] for layer in range(2)]
            return [mine[0], over_core(mine[0]), mine[1], over_core(mine[1])]

        with jax.named_scope("fg"):
            exp_row, contract, expand = place_feed(order.tie(counts), shares_of("feed"))
            order.mark(contract)
        with jax.named_scope("tg"):
            got["attn", 0] = behind(got["attn", 0], contract)
            in_row, norms, inproj, outproj = place_attn(order.tie(counts), shares_of("attn"))
        exp_row, in_row = exp_row[0], in_row[0]
    else:
        first_block = in_rows
        d_in = bf(behind(residual[: 2 * rows], first_block).astype(F32) + scattered(*pieces))
        with jax.named_scope("dx"):
            came = hop_two(d_in[rows:])
            in_order = chosen == 0
            both = jnp.stack([jnp.where(in_order, d_in[:rows], came), jnp.where(in_order, came, d_in[:rows])])
            half_width = width // 2
            mine = lax.dynamic_slice_in_dim(both, section * half_width, half_width, 2)
            other = lax.dynamic_slice_in_dim(both, (1 - section) * half_width, half_width, 2)
            other = over_core(other)
            ordered = jnp.where(first, jnp.concatenate([mine, other]), jnp.concatenate([other, mine]))
            input_grad = jnp.transpose(ordered, (1, 0, 2))
        contract, expand = reduce_plain(plain.feed, section, 1)
        attn_sum = reduce_plain(plain.attn, section, 1)[0]
        inproj = jnp.transpose(attn_sum[:, :cut].reshape(-1, 3, local), (1, 0, 2))
        outproj = jnp.transpose(attn_sum[:, cut:])
        biases = lax.psum(jnp.stack(plain.bias), (SECTION, DP))
        exp_row, in_row = jnp.where(first, biases[0], biases[1])
        norms = lax.psum(norm_rows, (HEADS, SECTION, DP))
        norms = jnp.where(first, norms[:6], norms[6:])
    loss_total = scalar_row[0, 0]
    rms_values = jnp.sqrt(scalar_row[0, 2:8].reshape(2, 3) / (scalar_row[0, 1] * width))
    piece = width // (dp_count * lax.axis_size(HEADS))
    norms = lax.dynamic_slice_in_dim(norms, (data * lax.axis_size(HEADS) + head) * piece, piece, 1)
    exp_shape, in_shape = online_expbias.shape, online_inbias.shape
    grad_expbias = lax.dynamic_slice_in_dim(
        exp_row.reshape(exp_shape), data * (exp_shape[2] // dp_count), exp_shape[2] // dp_count, 2
    )
    grad_inbias = lax.dynamic_slice_in_dim(
        in_row[: 2 * local].reshape(in_shape),
        data * (in_shape[3] // dp_count),
        in_shape[3] // dp_count,
        3,
    )
    return (
        loss_total,
        input_grad,
        jnp.transpose(inproj, (1, 0, 2))[None],
        grad_inbias,
        outproj[None],
        norms[None, 0:2],
        norms[None, 2:6],
        expand[None],
        grad_expbias,
        jnp.transpose(contract)[None],
        rms_values,
    )


def solution(mesh):
    placed = (
        P(HEADS, DP, None),
        P(HEADS, DP, None),
        P(DP, None),
        P(DP),
        P(DP, None),
        P(SECTION, None, None, HEADS),
        P(SECTION, None, HEADS, None),
        P(SECTION, HEADS, None),
        P(SECTION, None, None),
        P(SECTION, None, None),
        P(SECTION, None, HEADS),
        P(SECTION, HEADS, None),
        P(SECTION, HEADS, None),
        P(SECTION, None, None, HEADS),
        P(SECTION, None, HEADS, None),
        P(SECTION, HEADS, None),
        P(SECTION, None, None),
        P(SECTION, None, None),
        P(SECTION, None, HEADS),
        P(SECTION, HEADS, None),
        P(SECTION, HEADS, None),
    )
    return jax.shard_map(
        per_device,
        mesh=mesh,
        in_specs=placed,
        out_specs=(
            P(),
            P(HEADS, DP, SECTION),
            P(SECTION, DP, None, HEADS),
            P(SECTION, None, HEADS, DP),
            P(SECTION, HEADS, DP),
            P(SECTION, None, (DP, HEADS)),
            P(SECTION, None, (DP, HEADS)),
            P(SECTION, DP, HEADS),
            P(SECTION, HEADS, DP),
            P(SECTION, HEADS, DP),
            P(),
        ),
        check_vma=False,
    )
```
